128 devices in a mesh: pb: 8 (over z, core), pa: 16 (over x, y).
Axes of the slice: x: 4, y: 4, z: 4, core: 2. Of those that a mesh axis runs over, the one named last changes fastest.
Arguments:
- queries: float32 [16384, 768], P(('pb', 'pa')), may hold values from -5 to 5
- passages: float32 [16384, 768], P(('pb', 'pa')), may hold values from -5 to 5
- hard_ids: int32 [16384, 32], P(('pb', 'pa')), may hold values from 0 to 16383, as said below
- list_lengths: int32 [16384], P(('pb', 'pa')), may hold values from 1 to 32, 393216 in all
Outputs:
- loss: float32 [], replicated
- grad_queries: float32 [16384, 768], P(('pb', 'pa'))
- grad_passages: float32 [16384, 768], P(('pb', 'pa'))
The draws below stay inside these ranges and needn't reach their ends.
Inputs may be any that keep to these rules, and one draw needn't show every extreme that they name: `hard_ids`: cut the rows into aligned blocks of 128 (the rows of one device) and the passage ids into blocks of 128 consecutive ids: the 32 listed ids of one row block, live or not, fall at most 40 times into any one id block; in every draw some id block receives exactly 40 ids from every row block.
All inputs are finite; a program needn't handle non-finite values. No bound on the sum of `list_lengths` on one device may be relied on, other than what follows from the above.
Results may differ from the reference program's by a relative error of at most 0.0014.
The reference program's roundings to bfloat16 on the way count: a program that leaves them out, or rounds other values in their place, can miss the bound.
Values may be sent and summed in bfloat16 or wider, within the bound.
A program may use at most 128 MiB of HBM per device.

```python
import math
import jax
import jax.numpy as jnp
import numpy as np
from jax import lax

D = 768
ROW_DEV = 128
H = 32
N = 16384
CAP = 40


def hard_layout(key):
    owner_total = N // ROW_DEV
    pair_count = ROW_DEV * H
    slot_total = owner_total * CAP
    base_key = jax.random.fold_in(key, 101)
    special = jax.random.randint(jax.random.fold_in(base_key, 1), (), 0, owner_total)
    block_keys = jax.random.split(jax.random.fold_in(base_key, 2), owner_total)
    slot_owner = jnp.arange(slot_total, dtype=jnp.int32) // CAP

    def one_block(block_key):
        first_key, second_key, third_key, fourth_key = jax.random.split(block_key, 4)
        extra = jax.random.randint(first_key, (), 0, owner_total)
        ranking = jax.random.permutation(second_key, slot_total).astype(jnp.int32)
        forced = (slot_owner == special) | (slot_owner == extra)
        ordering = jnp.where(forced, ranking - slot_total, ranking)
        chosen = slot_owner[jnp.argsort(ordering, stable=True)[:pair_count]]
        shuffled = jax.random.permutation(third_key, chosen)
        within = jax.random.randint(fourth_key, (pair_count,), 0, ROW_DEV)
        return (shuffled * ROW_DEV + within).reshape(ROW_DEV, H)
    return jax.vmap(one_block)(block_keys).reshape(N, H).astype(jnp.int32)


def embeddings(key):
    spread = D ** (-0.25) * 1.2
    low_log = math.log(0.55)
    high_log = math.log(1.8)
    noise_query = jax.random.normal(jax.random.fold_in(key, 201), (N, D), jnp.float32)
    noise_passage = jax.random.normal(jax.random.fold_in(key, 202), (N, D), jnp.float32)
    scale_query = jnp.exp(jax.random.uniform(jax.random.fold_in(key, 204), (N, 1), jnp.float32, low_log, high_log))
    scale_passage = jnp.exp(jax.random.uniform(jax.random.fold_in(key, 205), (N, 1), jnp.float32, low_log, high_log))
    passages = spread * scale_passage * noise_passage
    id_table = hard_layout(key)
    group_rows = math.gcd(N, 256)

    def neighbour_sum(id_part):
        return passages[id_part].sum(1)
    summed = lax.map(neighbour_sum, id_table.reshape(N // group_rows, group_rows, H)).reshape(N, D)
    queries = spread * scale_query * noise_query + 4.0 / H * summed
    return (jnp.clip(queries, -5.0, 5.0), jnp.clip(passages, -5.0, 5.0))


def draw_queries(key, part):
    return embeddings(key)[0].astype(jnp.float32)


def draw_passages(key, part):
    return embeddings(key)[1].astype(jnp.float32)


def draw_hard_ids(key, part):
    return hard_layout(key)


def profile(count, total, most, skew):
    portions = [(1 << 20) // math.isqrt(rank ** skew) + 1 for rank in range(2, count + 1)]
    surplus, counts = total - most - (count - 1), [1] * (count - 1)
    while surplus > 0:
        free = [i for i in range(count - 1) if counts[i] < most]
        mass, left = sum([portions[i] for i in free]), surplus
        for i in free:
            more = min(most - counts[i], max(1, left * portions[i] // mass), surplus)
            counts[i] = counts[i] + more
            surplus = surplus - more
    return np.array([most] + counts)


def ragged(key, number_of, total, reach, slope):
    if number_of == 2:
        one = jax.random.randint(key, (), max(1, total - reach), min(reach, total - 1) + 1)
        return jnp.stack([one, total - one])
    sizes = jnp.asarray(profile(number_of, total, reach, slope), jnp.int32)
    couples = (number_of - 1) // 2
    giver, receiver = sizes[1:1 + 2 * couples:2], sizes[2:2 + 2 * couples:2]
    slack = jnp.minimum(giver - 1, reach - receiver)
    shifted = jax.random.randint(jax.random.fold_in(key, 1), (couples,), 0, 1 << 20) % (slack + 1)
    sizes = sizes.at[1:1 + 2 * couples:2].set(giver - shifted).at[2:2 + 2 * couples:2].set(receiver + shifted)
    return sizes[jax.random.permutation(jax.random.fold_in(key, 2), number_of)]


def setup_inputs(seed: int = 0) -> dict:
    keys = jax.random.split(jax.random.key(seed), 5)
    queries = draw_queries(jax.random.fold_in(keys[4], 71), 0)
    passages = draw_passages(jax.random.fold_in(keys[4], 71), 0)
    hard_ids = draw_hard_ids(jax.random.fold_in(keys[4], 71), 0)
    list_lengths = ragged(keys[3], N, 3 * N * H // 4, H, 1).astype(jnp.int32)
    return dict(queries=queries, passages=passages, hard_ids=hard_ids, list_lengths=list_lengths)


def tile_scores(left_rows, right_rows):
    return lax.dot_general(left_rows, right_rows, (((1,), (1,)), ((), ())), preferred_element_type=jnp.float32)


def reference(queries, passages, hard_ids, list_lengths):
    query_bf = queries.astype(jnp.bfloat16)
    passage_bf = passages.astype(jnp.bfloat16)
    block_rows = math.gcd(N, 1024)
    block_count = N // block_rows
    live_mask = jnp.arange(H, dtype=jnp.int32)[None, :] < list_lengths[:, None]
    query_blocks = query_bf.reshape(block_count, block_rows, D)
    passage_blocks = passage_bf.reshape(block_count, block_rows, D)
    id_blocks = hard_ids.reshape(block_count, block_rows, H)
    live_blocks = live_mask.reshape(block_count, block_rows, H)

    def first_sweep(carried, inputs):
        col_top, col_total = carried
        query_part, id_part, live_part = inputs
        scores = tile_scores(query_part, passage_bf)
        neg_rows = passage_bf[id_part]
        hard_score = jnp.einsum("rd,rhd->rh", query_part.astype(jnp.float32), neg_rows.astype(jnp.float32))
        masked = jnp.where(live_part, hard_score, -jnp.inf)
        row_top = jnp.maximum(scores.max(1), masked.max(1))
        row_total = jnp.exp(scores - row_top[:, None]).sum(1) + jnp.exp(masked - row_top[:, None]).sum(1)
        row_level = row_top + jnp.log(row_total)
        new_top = jnp.maximum(col_top, scores.max(0))
        col_total = col_total * jnp.exp(col_top - new_top) + jnp.exp(scores - new_top[None, :]).sum(0)
        return (new_top, col_total), (row_level, masked)

    start_state = (jnp.full((N,), -jnp.inf, jnp.float32), jnp.zeros((N,), jnp.float32))
    (col_top, col_total), (row_levels, masked_all) = lax.scan(first_sweep, start_state, (query_blocks, id_blocks, live_blocks))
    column_lse = col_top + jnp.log(col_total)
    row_lse = row_levels.reshape(N)
    diagonal = jnp.einsum("rd,rd->r", query_bf.astype(jnp.float32), passage_bf.astype(jnp.float32))
    loss = (jnp.sum(row_lse - diagonal) + jnp.sum(column_lse - diagonal)) / (2.0 * N)

    def second_sweep(passage_acc, inputs):
        query_part, passage_part, id_part, masked, row_level = inputs
        scores = tile_scores(query_part, passage_bf)
        weights = (jnp.exp(scores - row_level[:, None]) + jnp.exp(scores - column_lse[None, :])).astype(jnp.bfloat16)
        query_term = jnp.dot(weights, passage_bf, preferred_element_type=jnp.float32)
        passage_acc = passage_acc + lax.dot_general(weights, query_part, (((0,), (0,)), ((), ())), preferred_element_type=jnp.float32)
        hard_weight = jnp.exp(masked - row_level[:, None]).astype(jnp.bfloat16)
        neg_rows = passage_bf[id_part]
        hard_query = jnp.einsum("rh,rhd->rd", hard_weight.astype(jnp.float32), neg_rows.astype(jnp.float32))
        contribution = hard_weight.astype(jnp.float32)[:, :, None] * query_part.astype(jnp.float32)[:, None, :]
        passage_acc = passage_acc.at[id_part.reshape(-1)].add(contribution.reshape(-1, D))
        grad_rows = 0.5 * (query_term + hard_query - 2.0 * passage_part.astype(jnp.float32))
        return passage_acc, grad_rows

    passage_acc, grad_blocks = lax.scan(
        second_sweep,
        jnp.zeros((N, D), jnp.float32),
        (query_blocks, passage_blocks, id_blocks, masked_all, row_levels),
    )
    grad_queries = grad_blocks.reshape(N, D)
    grad_passages = 0.5 * (passage_acc - 2.0 * query_bf.astype(jnp.float32))
    return (loss, grad_queries, grad_passages)
```

```python
import functools

import jax
import jax.numpy as jnp
from jax import lax
from jax.experimental import pallas as pl
from jax.experimental.pallas import tpu as pltpu
from jax.sharding import PartitionSpec as P

BF = jnp.bfloat16
F32 = jnp.float32
MESH = pl.DeviceIdType.MESH
D = 768
OWN = 128
NQ = 8
NP = 8
QB = 256
COLS = 1024
ROWS = 2048
CH = 32
NEG = float("-inf")


def dot_nt(a, b):
    return lax.dot_general(a, b, (((1,), (1,)), ((), ())), preferred_element_type=F32)


def dot_nn(a, b):
    return lax.dot_general(a, b, (((1,), (0,)), ((), ())), preferred_element_type=F32)


def dot_tn(a, b):
    return lax.dot_general(a, b, (((0,), (0,)), ((), ())), preferred_element_type=F32)


def eighths(value):
    return value.reshape(value.shape[0] // 8, 8, value.shape[1])


def kernel(
    q_ref,
    p_ref,
    dest_ref,
    code_ref,
    loss_ref,
    gq_ref,
    gp_ref,
    qbuf,
    pbuf,
    sbuf,
    mbuf,
    wbuf,
    table,
    tabs,
    cmax,
    csum,
    stat,
    rstat,
    cstat,
    lrow,
    lcol,
    loss_r,
    loss_c,
    dq,
    sib,
    outq,
    inq,
    dp,
    outp,
    inp,
    q_send,
    q_recv,
    p_send,
    p_recv,
    sib_send,
    sib_recv,
    tab_send,
    tab_recv,
    rs_send,
    rs_recv,
    cs_send,
    cs_recv,
    lr_send,
    lr_recv,
    lc_send,
    lc_recv,
    dsib_send,
    dsib_recv,
    gq_send,
    gq_recv,
    gp_send,
    gp_recv,
):
    pb = lax.axis_index("pb")
    pa = lax.axis_index("pa")
    z, h = pb // 2, pb % 2
    x, y = pa // 4, pa % 4
    pair = z // 2
    zs = z % 2
    zc = (z + 3) % 4
    half, sel = zc // 2, zc % 2
    me_q = x * 2 + zs
    me_p = sel * 4 + y
    me_row = me_q * 2 + h

    def device(xx, yy, zz, hh):
        return (zz * 2 + hh, xx * 4 + yy)

    def row_peer(idx):
        q, hh = idx // 2, idx % 2
        return device(q // 2, y, pair * 2 + q % 2, hh)

    def col_peer(p):
        return device(x, p % 4, (half * 2 + p // 4 + 1) % 4, h)

    def chip_peer(q):
        return device(q // 2, y, pair * 2 + q % 2, h)

    sibling = device(x, y, z, 1 - h)

    def remote(src, dst, send, recv, to):
        return pltpu.make_async_remote_copy(
            src_ref=src,
            dst_ref=dst,
            send_sem=send,
            recv_sem=recv,
            device_id=to,
            device_id_type=MESH,
        )

    barrier = pltpu.get_barrier_semaphore()

    def greet_row(j, carry):
        pl.semaphore_signal(
            barrier, inc=1, device_id=row_peer((me_row + j) % 16), device_id_type=MESH
        )
        return carry

    def greet_col(j, carry):
        pl.semaphore_signal(
            barrier, inc=1, device_id=col_peer((me_p + j) % 8), device_id_type=MESH
        )
        return carry

    lax.fori_loop(1, 16, greet_row, 0)
    lax.fori_loop(1, 8, greet_col, 0)
    pl.semaphore_wait(barrier, 22)

    def q_at(xx, zz, first=0, size=OWN):
        return qbuf.at[xx * 2 + zz, pl.ds(pl.multiple_of(h * OWN + first, 64), size), :]

    def p_at(yy, ss, first=0, size=OWN):
        return pbuf.at[ss * 4 + yy, pl.ds(first, size), :]

    def ring(at, pos, side, to_left, to_right, to_pair, send, recv):
        left, right, far = (pos + 3) % 4, (pos + 1) % 4, (pos + 2) % 4
        other = 1 - side

        def own(src):
            here = at(pos, side)
            return [
                remote(src, here, send.at[0], recv.at[0], to_right),
                remote(src, here, send.at[1], recv.at[1], to_left),
                remote(src, here, send.at[2], recv.at[2], to_pair),
            ]

        def passing(ref, k, to):
            return remote(ref, ref, send.at[k], recv.at[k], to)

        forwards = [
            passing(at(left, side, 0, 64), 3, to_right),
            passing(at(right, side, 64, 64), 4, to_left),
            passing(at(pos, other), 5, to_right),
            passing(at(pos, other), 6, to_left),
            passing(at(far, side), 7, to_pair),
        ]
        arriving = [
            at(left, side),
            at(right, side),
            at(pos, other),
            at(far, side, 0, 64),
            at(far, side, 64, 64),
            at(left, other),
            at(right, other),
            at(far, other),
        ]
        waits = [
            remote(ref, ref, send.at[k], recv.at[k], to_pair) for k, ref in enumerate(arriving)
        ]
        return own, forwards, waits

    q_own, q_fwd, q_wait = ring(
        q_at,
        x,
        zs,
        device((x + 3) % 4, y, z, h),
        device((x + 1) % 4, y, z, h),
        device(x, y, pair * 2 + 1 - zs, h),
        q_send,
        q_recv,
    )
    p_own, p_fwd, p_wait = ring(
        p_at,
        y,
        sel,
        device(x, (y + 3) % 4, z, h),
        device(x, (y + 1) % 4, z, h),
        device(x, y, (half * 2 + (1 - sel) + 1) % 4, h),
        p_send,
        p_recv,
    )
    q_sends = q_own(q_ref)
    p_sends = p_own(p_ref)
    for one, two in zip(q_sends, p_sends):
        one.start()
        two.start()

    kinds = [
        (x, zs),
        ((x + 3) % 4, zs),
        ((x + 1) % 4, zs),
        (x, 1 - zs),
        ((x + 2) % 4, zs),
        ((x + 3) % 4, 1 - zs),
        ((x + 1) % 4, 1 - zs),
        ((x + 2) % 4, 1 - zs),
    ]

    def to_sibling(k, src=None):
        ref = q_at(*kinds[k])
        return remote(ref if src is None else src, ref, sib_send.at[k], sib_recv.at[k], sibling)

    def from_sibling(k):
        xx, zz = kinds[k]
        ref = qbuf.at[xx * 2 + zz, pl.ds(pl.multiple_of((1 - h) * OWN, OWN), OWN), :]
        return remote(ref, ref, sib_send.at[k], sib_recv.at[k], sibling)

    sib_copies = [to_sibling(k, q_ref if k == 0 else None) for k in range(8)]
    sib_copies[0].start()
    qbuf[me_q, pl.ds(pl.multiple_of(h * OWN, OWN), OWN), :] = q_ref[...]
    pbuf[me_p] = p_ref[...]

    sub = lax.broadcasted_iota(jnp.int32, (128, 128), 0)
    lane = lax.broadcasted_iota(jnp.int32, (128, 128), 1)
    earlier = jnp.where(sub < lane, 1.0, 0.0).astype(BF)
    prefix = jnp.concatenate([earlier, jnp.ones((128, 128), BF)], axis=1)
    row_code = (lane + 1 + 128 * h).astype(F32)
    offset = (64 * h).astype(F32)
    sub_f = sub.astype(F32)
    table[...] = jnp.zeros_like(table)

    def slot_step(k, count):
        dest = dest_ref[pl.ds(k, 1), :]
        code = code_ref[pl.ds(k, 1), :]
        live = jnp.where(sub == dest, 1.0, 0.0)
        both = dot_nn(live.astype(BF), prefix)
        rank = jnp.sum(live * (both[:, :128] + count), axis=0, keepdims=True) + offset
        slot = sub_f == rank
        chosen = jnp.concatenate(
            [jnp.where(slot, row_code, 0.0), jnp.where(slot, code, 0.0)], axis=0
        ).astype(BF)
        table[...] += dot_nt(live.astype(BF), chosen)
        return count + both[:, 128:]

    lax.fori_loop(0, 32, slot_step, jnp.zeros((128, 128), F32), unroll=2)

    for k in range(3):
        q_wait[k].wait_recv()
        if k < 2:
            q_fwd[k].start()
        else:
            q_fwd[2].start()
            q_fwd[3].start()
        p_wait[k].wait_recv()
        if k < 2:
            p_fwd[k].start()
        else:
            p_fwd[2].start()
            p_fwd[3].start()
        sib_copies[k + 1].start()

    def tab_copy(idx, to):
        q, hh = to // 2, to % 2
        zz = (pair * 2 + q % 2 + 3) % 4
        group = (q // 2) * 4 + (zz // 2) * 2 + hh
        return remote(
            table.at[pl.ds(pl.multiple_of(group * 8, 8), 8), :],
            tabs.at[idx],
            tab_send.at[to],
            tab_recv.at[idx],
            row_peer(to),
        )

    def tab_start(j, carry):
        tab_copy(me_row, (me_row + j) % 16).start()
        return carry

    lax.fori_loop(1, 16, tab_start, 0)
    tabs[me_row] = table[pl.ds(pl.multiple_of((x * 4 + half * 2 + h) * 8, 8), 8), :]

    for k in (3, 4):
        q_wait[k].wait_recv()
        p_wait[k].wait_recv()
    q_fwd[4].start()
    p_fwd[4].start()
    sib_copies[4].start()

    def tab_arrive(j, carry):
        other = (me_row + j) % 16
        ref = tabs.at[other]
        remote(ref, ref, tab_send.at[other], tab_recv.at[other], row_peer(other)).wait_recv()
        return carry

    lax.fori_loop(1, 16, tab_arrive, 0)

    tall = (lax.broadcasted_iota(jnp.int32, (QB, 128), 0) + 1).astype(F32)

    def count_step(q, carry):
        both = tabs[2 * q] + tabs[2 * q + 1]
        for p in range(NP):
            rows = jnp.where(tall == both[p : p + 1, :128], 1.0, 0.0).astype(BF)
            cols = jnp.where(tall[:128] == both[p : p + 1, 128:], 1.0, 0.0).astype(BF)
            mbuf[q, :, p * 128 : (p + 1) * 128] = dot_nt(rows, cols).astype(BF)
        return carry

    lax.fori_loop(0, NQ, count_step, 0)

    for k in (5, 6, 7):
        q_wait[k].wait_recv()
        sib_copies[k].start()
        p_wait[k].wait_recv()
    for k in range(8):
        from_sibling(k).wait_recv()

    cmax[...] = jnp.full(cmax.shape, NEG, F32)
    csum[...] = jnp.zeros_like(csum)
    first_half = lax.broadcasted_iota(jnp.int32, (CH, 128), 1) < 64

    def sweep(q, carry):
        for c in range(4):
            cols = slice(c * 256, (c + 1) * 256)
            part = dot_nt(qbuf[q], pbuf[2 * c : 2 * c + 2].reshape(256, D))
            sbuf[q, :, cols] = part
            old = cmax[:, cols]
            new = jnp.maximum(old, eighths(part).max(0))
            csum[:, cols] = csum[:, cols] * jnp.exp(old - new)
            cmax[:, cols] = new

        def chunk(r, inner):
            rows = pl.ds(pl.multiple_of(r * CH, CH), CH)
            top = sbuf[q, rows, 0:128]
            for g in range(1, 8):
                top = jnp.maximum(top, sbuf[q, rows, g * 128 : (g + 1) * 128])
            top = jnp.max(top, axis=1, keepdims=True)
            wide = jnp.broadcast_to(top, (CH, 128))
            total = jnp.zeros((CH, 128), F32)
            for g in range(8):
                cols = slice(g * 128, (g + 1) * 128)
                s = sbuf[q, rows, cols]
                e = jnp.exp(s - wide)
                total += e + e * mbuf[q, rows, cols].astype(F32)
                csum[:, cols] += jnp.exp(eighths(s) - cmax[:, cols][None]).sum(0)
            total = jnp.sum(total, axis=1, keepdims=True)
            stat[rows, :] = jnp.where(first_half, wide, total)
            return inner

        lax.fori_loop(0, QB // CH, chunk, 0)
        turned = stat[...].T
        rstat[me_row, pl.ds(q, 1), :] = turned[0:1, :]
        rstat[me_row, pl.ds(8 + q, 1), :] = turned[64:65, :]
        return carry

    lax.fori_loop(0, NQ, sweep, 0)

    top = jnp.max(cmax[...], axis=0, keepdims=True)
    cstat[me_p, 0:1, :] = top
    cstat[me_p, 1:2, :] = jnp.sum(csum[...] * jnp.exp(cmax[...] - top), axis=0, keepdims=True)
    diag = eighths(q_ref[...].astype(F32) * p_ref[...].astype(F32)).sum(0)
    diag = diag[:, :256] + diag[:, 256:512] + diag[:, 512:]
    rstat[me_row, 16:24, :] = diag

    def all_row(buf, send, recv):
        def start(j, carry):
            to = (me_row + j) % 16
            here = buf.at[me_row]
            remote(here, here, send.at[to], recv.at[me_row], row_peer(to)).start()
            return carry

        def arrive(j, carry):
            other = (me_row + j) % 16
            ref = buf.at[other]
            remote(ref, ref, send.at[other], recv.at[other], row_peer(other)).wait_recv()
            return carry

        return start, arrive

    def all_col(buf, send, recv):
        def start(j, carry):
            to = (me_p + j) % 8
            here = buf.at[me_p]
            remote(here, here, send.at[to], recv.at[me_p], col_peer(to)).start()
            return carry

        def arrive(j, carry):
            other = (me_p + j) % 8
            ref = buf.at[other]
            remote(ref, ref, send.at[other], recv.at[other], col_peer(other)).wait_recv()
            return carry

        return start, arrive

    rs_start, rs_arrive = all_row(rstat, rs_send, rs_recv)
    cs_start, cs_arrive = all_col(cstat, cs_send, cs_recv)
    lax.fori_loop(1, 8, cs_start, 0)
    lax.fori_loop(1, 16, rs_start, 0)
    lax.fori_loop(1, 8, cs_arrive, 0)

    tops = [cstat[k, 0:1, :] for k in range(8)]
    peak = functools.reduce(jnp.maximum, tops)
    total = functools.reduce(
        jnp.add, [cstat[k, 1:2, :] * jnp.exp(tops[k] - peak) for k in range(8)]
    )
    column_lse = peak + jnp.log(total)
    lcol[...] = jnp.broadcast_to(column_lse, (8, COLS))

    lax.fori_loop(1, 16, rs_arrive, 0)
    peak = rstat[0, 0:8, :]
    for k in range(1, 16):
        peak = jnp.maximum(peak, rstat[k, 0:8, :])
    total = jnp.zeros((8, QB), F32)
    diag = jnp.zeros((8, QB), F32)
    for k in range(16):
        total += rstat[k, 8:16, :] * jnp.exp(rstat[k, 0:8, :] - peak)
        diag += rstat[k, 16:24, :]
    row_lse = peak + jnp.log(total)
    for q in range(NQ):
        lrow[q] = jnp.broadcast_to(row_lse[q : q + 1, :], (128, QB)).T
    part = row_lse - 2.0 * diag
    loss_r[me_p] = part[:, :128] + part[:, 128:]
    part = functools.reduce(jnp.add, [column_lse[:, g * 128 : (g + 1) * 128] for g in range(8)])
    loss_c[me_row] = jnp.where(sub[:8] == 0, jnp.broadcast_to(part, (8, 128)), 0.0)

    def to_own(q):
        low = pl.multiple_of(h * OWN, OWN)
        high = pl.multiple_of((1 - h) * OWN, OWN)
        return dq.at[q, pl.ds(low, OWN), :], dq.at[q, pl.ds(high, OWN), :]

    def dsib_copy(q):
        return remote(to_own(q)[1], sib.at[q], dsib_send.at[q], dsib_recv.at[q], sibling)

    def gq_copy(q):
        return remote(outq.at[q], inq.at[me_q], gq_send.at[q], gq_recv.at[me_q], chip_peer(q))

    def gp_copy(p):
        return remote(outp.at[p], inp.at[me_p], gp_send.at[p], gp_recv.at[me_p], col_peer(p))

    def turn_q(i):
        return (me_q + 1 + i) % NQ

    def weights(q):
        def chunk(r, inner):
            rows = pl.ds(pl.multiple_of(r * CH, CH), CH)
            level = lrow[q, rows, :]
            for g in range(8):
                cols = slice(g * 128, (g + 1) * 128)
                s = sbuf[q, rows, cols]
                er = jnp.exp(s - level)
                ec = jnp.exp(eighths(s) - lcol[:, cols][None]).reshape(CH, 128)
                pair_weight = (er + ec).astype(BF).astype(F32)
                hard_weight = er.astype(BF).astype(F32)
                count = mbuf[q, rows, cols].astype(F32)
                wbuf[q, rows, cols] = (pair_weight + count * hard_weight).astype(BF)
            return inner

        lax.fori_loop(0, QB // CH, chunk, 0)

    def query_sum(q):
        everything = pbuf[...].reshape(COLS, D)
        for n in range(3):
            cols = slice(n * 256, (n + 1) * 256)
            dq[q, :, cols] = dot_nn(wbuf[q], everything[:, cols])

    def take_sibling(q):
        dsib_copy(q).wait_recv()
        low = pl.multiple_of(h * OWN, OWN)
        outq[q] = (dq[q, pl.ds(low, OWN), :] + sib[q]).astype(BF)

    def second(i, carry):
        q = turn_q(i)
        weights(q)

        @pl.when(i > 0)
        def _():
            dsib_copy(turn_q(i - 1)).start()

        @pl.when(i > 1)
        def _():
            gq_copy(turn_q(i - 2)).start()

        query_sum(q)

        @pl.when(i > 0)
        def _():
            take_sibling(turn_q(i - 1))

        return carry

    lax.fori_loop(0, NQ, second, 0)

    def turn_p(i):
        return (me_p // 2 + 1 + i) % 4

    def send_pair(i):
        for k in range(2):
            p = turn_p(i) * 2 + k

            @pl.when(p != me_p)
            def _():
                gp_copy(p).start()

    lr_start, lr_arrive = all_col(loss_r, lr_send, lr_recv)
    lc_start, lc_arrive = all_row(loss_c, lc_send, lc_recv)

    def third(i, carry):
        block = turn_p(i)
        cols = pl.ds(pl.multiple_of(block * 256, 256), 256)
        left = wbuf[:, :, cols].reshape(ROWS, 256)
        part = dot_tn(left, qbuf[...].reshape(ROWS, D))
        dp[...] = part.reshape(2, OWN, D)
        for k in range(2):
            outp[block * 2 + k] = part[k * OWN : (k + 1) * OWN].astype(BF)

        @pl.when(i == 0)
        def _():
            dsib_copy(turn_q(NQ - 1)).start()
            gq_copy(turn_q(NQ - 2)).start()
            lax.fori_loop(1, 8, lr_start, 0)
            lax.fori_loop(1, 16, lc_start, 0)

        @pl.when(i > 0)
        def _():
            send_pair(i - 1)

        return carry

    lax.fori_loop(0, 4, third, 0)
    dsib_copy(me_q).wait_recv()
    low = pl.multiple_of(h * OWN, OWN)
    gq_ref[...] = dq[me_q, pl.ds(low, OWN), :] + sib[me_q]
    send_pair(3)

    lax.fori_loop(1, 8, lr_arrive, 0)
    lax.fori_loop(1, 16, lc_arrive, 0)
    halves = []
    for s in range(2):
        halves.append(functools.reduce(jnp.add, [loss_r[s * 4 + k] for k in range(4)]))
    both = halves[0] + halves[1]
    halves = []
    for s in range(2):
        terms = [loss_c[xx * 4 + s * 2 + hh] for xx in range(4) for hh in range(2)]
        halves.append(functools.reduce(jnp.add, terms))
    both = both + (halves[0] + halves[1])
    both = jnp.sum(jnp.sum(both, axis=0, keepdims=True), axis=1, keepdims=True)
    loss_ref[...] = jnp.broadcast_to(both / (2.0 * 16384), (8, 128))

    def take_q(j, carry):
        other = (me_q + j) % NQ
        ref = inq.at[other]
        remote(ref, ref, gq_send.at[other], gq_recv.at[other], chip_peer(other)).wait_recv()
        gq_ref[...] += inq[other].astype(F32)
        return carry

    lax.fori_loop(1, NQ, take_q, 0)
    gq_ref[...] = 0.5 * (gq_ref[...] - 2.0 * p_ref[...].astype(F32))

    gp_ref[...] = dp[me_p % 2]

    def take_p(j, carry):
        other = (me_p + j) % NP
        ref = inp.at[other]
        remote(ref, ref, gp_send.at[other], gp_recv.at[other], col_peer(other)).wait_recv()
        gp_ref[...] += inp[other].astype(F32)
        return carry

    lax.fori_loop(1, NP, take_p, 0)
    gp_ref[...] = 0.5 * (gp_ref[...] - 2.0 * q_ref[...].astype(F32))

    for copy in q_sends + p_sends + q_fwd + p_fwd + sib_copies:
        copy.wait_send()

    def left_row(j, carry):
        to = (me_row + j) % 16
        tab_copy(me_row, to).wait_send()
        here = rstat.at[me_row]
        remote(here, here, rs_send.at[to], rs_recv.at[me_row], row_peer(to)).wait_send()
        here = loss_c.at[me_row]
        remote(here, here, lc_send.at[to], lc_recv.at[me_row], row_peer(to)).wait_send()
        return carry

    def left_col(j, carry):
        to = (me_p + j) % 8
        here = cstat.at[me_p]
        remote(here, here, cs_send.at[to], cs_recv.at[me_p], col_peer(to)).wait_send()
        here = loss_r.at[me_p]
        remote(here, here, lr_send.at[to], lr_recv.at[me_p], col_peer(to)).wait_send()
        gp_copy(to).wait_send()
        gq_copy((me_q + j) % 8).wait_send()
        return carry

    def left_sib(q, carry):
        dsib_copy(q).wait_send()
        return carry

    lax.fori_loop(1, 16, left_row, 0)
    lax.fori_loop(1, 8, left_col, 0)
    lax.fori_loop(0, 8, left_sib, 0)


def per_device(queries, passages, hard_ids, list_lengths):
    listed = hard_ids.shape[1]
    live = jnp.arange(listed, dtype=jnp.int32)[:, None] < list_lengths[None, :]
    ids = hard_ids.T
    owner, column = ids // OWN, ids % OWN
    core, zz = (owner // 16) % 2, (owner // 32 + 3) % 4
    xx, yy = (owner // 4) % 4, owner % 4
    dest = xx * 32 + (zz // 2) * 16 + core * 8 + (zz % 2) * 4 + yy
    dest = jnp.where(live, dest, -1)
    code = (column + 1).astype(F32)

    vm = pl.BlockSpec(memory_space=pltpu.VMEM)
    dma = pltpu.SemaphoreType.DMA
    loss, grad_queries, grad_passages = pl.pallas_call(
        kernel,
        out_shape=(
            jax.ShapeDtypeStruct((8, 128), F32),
            jax.ShapeDtypeStruct((OWN, D), F32),
            jax.ShapeDtypeStruct((OWN, D), F32),
        ),
        in_specs=[vm] * 4,
        out_specs=(vm, vm, vm),
        scratch_shapes=[
            pltpu.VMEM((NQ, QB, D), BF),
            pltpu.VMEM((NP, OWN, D), BF),
            pltpu.VMEM((NQ, QB, COLS), F32),
            pltpu.VMEM((NQ, QB, COLS), BF),
            pltpu.VMEM((NQ, QB, COLS), BF),
            pltpu.VMEM((128, 256), F32),
            pltpu.VMEM((16, 8, 256), F32),
            pltpu.VMEM((8, COLS), F32),
            pltpu.VMEM((8, COLS), F32),
            pltpu.VMEM((QB, 128), F32),
            pltpu.VMEM((16, 24, QB), F32),
            pltpu.VMEM((8, 2, COLS), F32),
            pltpu.VMEM((NQ, QB, 128), F32),
            pltpu.VMEM((8, COLS), F32),
            pltpu.VMEM((8, 8, 128), F32),
            pltpu.VMEM((16, 8, 128), F32),
            pltpu.VMEM((NQ, QB, D), F32),
            pltpu.VMEM((NQ, OWN, D), F32),
            pltpu.VMEM((NQ, OWN, D), BF),
            pltpu.VMEM((NQ, OWN, D), BF),
            pltpu.VMEM((2, OWN, D), F32),
            pltpu.VMEM((NP, OWN, D), BF),
            pltpu.VMEM((NP, OWN, D), BF),
            dma((8,)),
            dma((8,)),
            dma((8,)),
            dma((8,)),
            dma((8,)),
            dma((8,)),
            dma((16,)),
            dma((16,)),
            dma((16,)),
            dma((16,)),
            dma((8,)),
            dma((8,)),
            dma((8,)),
            dma((8,)),
            dma((16,)),
            dma((16,)),
            dma((8,)),
            dma((8,)),
            dma((8,)),
            dma((8,)),
            dma((8,)),
            dma((8,)),
        ],
        compiler_params=pltpu.CompilerParams(
            collective_id=0, has_side_effects=True, vmem_limit_bytes=60 * 1024 * 1024
        ),
        name="infonce",
    )(queries.astype(BF), passages.astype(BF), dest, code)
    return loss[0, 0], grad_queries, grad_passages


def solution(mesh):
    placed = (P(("pb", "pa"), None), P(("pb", "pa"), None), P(("pb", "pa"), None), P(("pb", "pa")))
    return jax.shard_map(
        per_device,
        mesh=mesh,
        in_specs=placed,
        out_specs=(P(), P(("pb", "pa"), None), P(("pb", "pa"), None)),
        check_vma=False,
    )
```

```python
import functools

import jax
import jax.numpy as jnp
from jax import lax
from jax.experimental import pallas as pl
from jax.experimental.pallas import tpu as pltpu
from jax.sharding import PartitionSpec as P

BF = jnp.bfloat16
F32 = jnp.float32
MESH = pl.DeviceIdType.MESH
D = 768
OWN = 128
NQ = 8
NP = 8
QB = 256
COLS = 1024
ROWS = 2048
CH = 64
NEG = float("-inf")


def dot_nt(a, b):
    return lax.dot_general(a, b, (((1,), (1,)), ((), ())), preferred_element_type=F32)


def dot_nn(a, b):
    return lax.dot_general(a, b, (((1,), (0,)), ((), ())), preferred_element_type=F32)


def dot_tn(a, b):
    return lax.dot_general(a, b, (((0,), (0,)), ((), ())), preferred_element_type=F32)


def eighths(value):
    return value.reshape(value.shape[0] // 8, 8, value.shape[1])


def kernel(
    queries_ref,
    passages_ref,
    ids_ref,
    lengths_ref,
    loss_ref,
    gq_ref,
    gp_ref,
    q_ref,
    p_ref,
    dest_ref,
    code_ref,
    qbuf,
    pbuf,
    sbuf,
    mbuf,
    wbuf,
    table,
    tabs,
    cmax,
    cnext,
    csum,
    rnext,
    wide_ref,
    rsum,
    rstat,
    cstat,
    lrow,
    lcol,
    loss_r,
    loss_c,
    dq,
    sib,
    outq,
    inq,
    dp,
    outp,
    inp,
    q_send,
    q_recv,
    p_send,
    p_recv,
    sib_send,
    sib_recv,
    tab_send,
    tab_recv,
    rs_send,
    rs_recv,
    cs_send,
    cs_recv,
    lr_send,
    lr_recv,
    lc_send,
    lc_recv,
    dsib_send,
    dsib_recv,
    gq_send,
    gq_recv,
    gp_send,
    gp_recv,
):
    pb = lax.axis_index("pb")
    pa = lax.axis_index("pa")
    z, h = pb // 2, pb % 2
    x, y = pa // 4, pa % 4
    pair = z // 2
    zs = z % 2
    zc = (z + 3) % 4
    half, sel = zc // 2, zc % 2
    me_q = x * 2 + zs
    me_p = sel * 4 + y
    me_row = me_q * 2 + h

    def device(xx, yy, zz, hh):
        return (zz * 2 + hh, xx * 4 + yy)

    def row_peer(idx):
        q, hh = idx // 2, idx % 2
        return device(q // 2, y, pair * 2 + q % 2, hh)

    def col_peer(p):
        return device(x, p % 4, (half * 2 + p // 4 + 1) % 4, h)

    def chip_peer(q):
        return device(q // 2, y, pair * 2 + q % 2, h)

    sibling = device(x, y, z, 1 - h)

    def remote(src, dst, send, recv, to):
        return pltpu.make_async_remote_copy(
            src_ref=src,
            dst_ref=dst,
            send_sem=send,
            recv_sem=recv,
            device_id=to,
            device_id_type=MESH,
        )

    barrier = pltpu.get_barrier_semaphore()

    def greet_row(j, carry):
        pl.semaphore_signal(
            barrier, inc=1, device_id=row_peer((me_row + j) % 16), device_id_type=MESH
        )
        return carry

    def greet_col(j, carry):
        pl.semaphore_signal(
            barrier, inc=1, device_id=col_peer((me_p + j) % 8), device_id_type=MESH
        )
        return carry

    lax.fori_loop(1, 16, greet_row, 0)
    lax.fori_loop(1, 8, greet_col, 0)

    q_ref[...] = queries_ref[...].astype(BF)
    p_ref[...] = passages_ref[...].astype(BF)
    ids = ids_ref[...]
    owner = ids // OWN
    third_z = (owner // 32 + 3) % 4
    dest = (owner // 4) % 4 * 32 + (third_z // 2) * 16 + (owner // 16) % 2 * 8
    dest = dest + (third_z % 2) * 4 + owner % 4
    place = lax.broadcasted_iota(jnp.int32, ids.shape, 0)
    dest_ref[...] = jnp.where(place < lengths_ref[...], dest, -1)
    code_ref[...] = (ids % OWN + 1).astype(F32)
    qbuf[me_q, pl.ds(pl.multiple_of(h * OWN, OWN), OWN), :] = q_ref[...]
    pbuf[me_p] = p_ref[...]
    pl.semaphore_wait(barrier, 22)

    def q_at(xx, zz, first=0, size=OWN):
        return qbuf.at[xx * 2 + zz, pl.ds(pl.multiple_of(h * OWN + first, 64), size), :]

    def p_at(yy, ss, first=0, size=OWN):
        return pbuf.at[ss * 4 + yy, pl.ds(first, size), :]

    def ring(at, pos, side, to_left, to_right, to_pair, send, recv):
        left, right, far = (pos + 3) % 4, (pos + 1) % 4, (pos + 2) % 4
        other = 1 - side

        def own(src):
            here = at(pos, side)
            return [
                remote(src, here, send.at[0], recv.at[0], to_right),
                remote(src, here, send.at[1], recv.at[1], to_left),
                remote(src, here, send.at[2], recv.at[2], to_pair),
            ]

        def passing(ref, k, to):
            return remote(ref, ref, send.at[k], recv.at[k], to)

        forwards = [
            passing(at(left, side, 0, 64), 3, to_right),
            passing(at(right, side, 64, 64), 4, to_left),
            passing(at(pos, other), 5, to_right),
            passing(at(pos, other), 6, to_left),
            passing(at(far, side), 7, to_pair),
        ]
        arriving = [
            at(left, side),
            at(right, side),
            at(pos, other),
            at(far, side, 0, 64),
            at(far, side, 64, 64),
            at(left, other),
            at(right, other),
            at(far, other),
        ]
        waits = [
            remote(ref, ref, send.at[k], recv.at[k], to_pair) for k, ref in enumerate(arriving)
        ]
        return own, forwards, waits

    q_own, q_fwd, q_wait = ring(
        q_at,
        x,
        zs,
        device((x + 3) % 4, y, z, h),
        device((x + 1) % 4, y, z, h),
        device(x, y, pair * 2 + 1 - zs, h),
        q_send,
        q_recv,
    )
    p_own, p_fwd, p_wait = ring(
        p_at,
        y,
        sel,
        device(x, (y + 3) % 4, z, h),
        device(x, (y + 1) % 4, z, h),
        device(x, y, (half * 2 + (1 - sel) + 1) % 4, h),
        p_send,
        p_recv,
    )
    q_sends = q_own(q_ref)
    p_sends = p_own(p_ref)
    for one, two in zip(q_sends, p_sends):
        one.start()
        two.start()

    kinds = [
        (x, zs),
        ((x + 3) % 4, zs),
        ((x + 1) % 4, zs),
        (x, 1 - zs),
        ((x + 2) % 4, zs),
        ((x + 3) % 4, 1 - zs),
        ((x + 1) % 4, 1 - zs),
        ((x + 2) % 4, 1 - zs),
    ]

    def to_sibling(k, src=None):
        ref = q_at(*kinds[k])
        return remote(ref if src is None else src, ref, sib_send.at[k], sib_recv.at[k], sibling)

    def from_sibling(k):
        xx, zz = kinds[k]
        ref = qbuf.at[xx * 2 + zz, pl.ds(pl.multiple_of((1 - h) * OWN, OWN), OWN), :]
        return remote(ref, ref, sib_send.at[k], sib_recv.at[k], sibling)

    sib_copies = [to_sibling(k, q_ref if k == 0 else None) for k in range(8)]
    sib_copies[0].start()

    sub = lax.broadcasted_iota(jnp.int32, (128, 128), 0)
    lane = lax.broadcasted_iota(jnp.int32, (128, 128), 1)
    earlier = jnp.where(sub < lane, 1.0, 0.0).astype(BF)
    prefix = jnp.concatenate([earlier, jnp.ones((128, 128), BF)], axis=1)
    row_code = (lane + 1 + 128 * h).astype(F32)
    offset = (64 * h).astype(F32)
    sub_f = sub.astype(F32)
    table[...] = jnp.zeros_like(table)

    def slot_step(k, count):
        dest = dest_ref[pl.ds(k, 1), :]
        code = code_ref[pl.ds(k, 1), :]
        live = jnp.where(sub == dest, 1.0, 0.0)
        both = dot_nn(live.astype(BF), prefix)
        rank = jnp.sum(live * (both[:, :128] + count), axis=0, keepdims=True) + offset
        slot = sub_f == rank
        chosen = jnp.concatenate(
            [jnp.where(slot, row_code, 0.0), jnp.where(slot, code, 0.0)], axis=0
        ).astype(BF)
        table[...] += dot_nt(live.astype(BF), chosen)
        return count + both[:, 128:]

    lax.fori_loop(0, 32, slot_step, jnp.zeros((128, 128), F32), unroll=2)

    def tab_copy(idx, to):
        q, hh = to // 2, to % 2
        zz = (pair * 2 + q % 2 + 3) % 4
        group = (q // 2) * 4 + (zz // 2) * 2 + hh
        return remote(
            table.at[pl.ds(pl.multiple_of(group * 8, 8), 8), :],
            tabs.at[idx],
            tab_send.at[to],
            tab_recv.at[idx],
            row_peer(to),
        )

    def tab_start(j, carry):
        tab_copy(me_row, (me_row + j) % 16).start()
        return carry

    lax.fori_loop(1, 16, tab_start, 0)
    tabs[me_row] = table[pl.ds(pl.multiple_of((x * 4 + half * 2 + h) * 8, 8), 8), :]

    for k in range(3):
        q_wait[k].wait_recv()
        if k < 2:
            q_fwd[k].start()
        else:
            q_fwd[2].start()
            q_fwd[3].start()
        p_wait[k].wait_recv()
        if k < 2:
            p_fwd[k].start()
        else:
            p_fwd[2].start()
            p_fwd[3].start()
        sib_copies[k + 1].start()

    for k in (3, 4):
        q_wait[k].wait_recv()
        p_wait[k].wait_recv()
    q_fwd[4].start()
    p_fwd[4].start()
    sib_copies[4].start()

    def tab_arrive(j, carry):
        other = (me_row + j) % 16
        ref = tabs.at[other]
        remote(ref, ref, tab_send.at[other], tab_recv.at[other], row_peer(other)).wait_recv()
        return carry

    lax.fori_loop(1, 16, tab_arrive, 0)

    tall = (lax.broadcasted_iota(jnp.int32, (QB, 128), 0) + 1).astype(F32)

    def count_step(q, carry):
        both = tabs[2 * q] + tabs[2 * q + 1]
        for p in range(NP):
            rows = jnp.where(tall == both[p : p + 1, :128], 1.0, 0.0).astype(BF)
            cols = jnp.where(tall[:128] == both[p : p + 1, 128:], 1.0, 0.0).astype(BF)
            mbuf[q, :, p * 128 : (p + 1) * 128] = dot_nt(rows, cols).astype(BF)
        return carry

    lax.fori_loop(0, NQ, count_step, 0)

    for k in (5, 6, 7):
        q_wait[k].wait_recv()
        sib_copies[k].start()
        p_wait[k].wait_recv()
    for k in range(8):
        from_sibling(k).wait_recv()

    cmax[...] = jnp.full(cmax.shape, NEG, F32)
    cnext[...] = jnp.full(cnext.shape, NEG, F32)
    csum[...] = jnp.zeros_like(csum)
    rnext[...] = jnp.full(rnext.shape, NEG, F32)

    def scores(q, c):
        cols = pl.ds(pl.multiple_of(c * 256, 256), 256)
        part = dot_nt(qbuf[q], pbuf[pl.ds(2 * c, 2)].reshape(256, D))
        sbuf[q, :, cols] = part
        cnext[:, cols] = jnp.maximum(cnext[:, cols], eighths(part).max(0))
        rnext[...] = jnp.maximum(rnext[...], jnp.maximum(part[:, :128], part[:, 128:]))

    def levels():
        csum[...] = csum[...] * jnp.exp(cmax[...] - cnext[...])
        cmax[...] = cnext[...]
        top = jnp.max(rnext[...], axis=1, keepdims=True)
        wide_ref[...] = jnp.broadcast_to(top, (QB, 128))
        rnext[...] = jnp.full(rnext.shape, NEG, F32)

    def sums(q, r):
        rows = pl.ds(pl.multiple_of(r * CH, CH), CH)
        wide = wide_ref[rows, :]
        total = jnp.zeros((CH, 128), F32)
        for g in range(8):
            cols = slice(g * 128, (g + 1) * 128)
            s = sbuf[q, rows, cols]
            e = jnp.exp(s - wide)
            total += e + e * mbuf[q, rows, cols].astype(F32)
            csum[:, cols] += jnp.exp(eighths(s) - cmax[:, cols][None]).sum(0)
        rsum[rows, :] = total

    def row_level(q):
        top = wide_ref[...].T[0:1, :]
        total = jnp.sum(rsum[...].T, axis=0, keepdims=True)
        rstat[me_row, pl.ds(q, 1), :] = top + jnp.log(total)

    def first_scores(c, carry):
        scores(0, c)
        return carry

    lax.fori_loop(0, 4, first_scores, 0)

    def sweep(q, carry):
        levels()

        def step(c, inner):
            sums(q, c)
            scores(q + 1, c)
            return inner

        lax.fori_loop(0, 4, step, 0)
        row_level(q)
        return carry

    lax.fori_loop(0, NQ - 1, sweep, 0)
    levels()

    def last_sums(c, carry):
        sums(NQ - 1, c)
        return carry

    lax.fori_loop(0, 4, last_sums, 0)
    row_level(NQ - 1)

    top = jnp.max(cmax[...], axis=0, keepdims=True)
    total = jnp.sum(csum[...] * jnp.exp(cmax[...] - top), axis=0, keepdims=True)
    cstat[me_p, 0:1, :] = top + jnp.log(total)
    diag = q_ref[...].astype(F32) * p_ref[...].astype(F32)
    diag = jnp.sum(diag, axis=0, keepdims=True)
    cstat[me_p, 1:2, 0:D] = diag
    cstat[me_p, 1:2, D:COLS] = jnp.zeros((1, COLS - D), F32)

    def all_row(buf, send, recv):
        def start(j, carry):
            to = (me_row + j) % 16
            here = buf.at[me_row]
            remote(here, here, send.at[to], recv.at[me_row], row_peer(to)).start()
            return carry

        def arrive(j, carry):
            other = (me_row + j) % 16
            ref = buf.at[other]
            remote(ref, ref, send.at[other], recv.at[other], row_peer(other)).wait_recv()
            return carry

        return start, arrive

    def all_col(buf, send, recv):
        def start(j, carry):
            to = (me_p + j) % 8
            here = buf.at[me_p]
            remote(here, here, send.at[to], recv.at[me_p], col_peer(to)).start()
            return carry

        def arrive(j, carry):
            other = (me_p + j) % 8
            ref = buf.at[other]
            remote(ref, ref, send.at[other], recv.at[other], col_peer(other)).wait_recv()
            return carry

        return start, arrive

    rs_start, rs_arrive = all_row(rstat, rs_send, rs_recv)
    cs_start, cs_arrive = all_col(cstat, cs_send, cs_recv)
    lax.fori_loop(1, 16, rs_start, 0)
    lax.fori_loop(1, 8, cs_start, 0)
    lax.fori_loop(1, 8, cs_arrive, 0)

    parts = [cstat[k, 0:1, :] for k in range(8)]
    peak = functools.reduce(jnp.maximum, parts)
    total = functools.reduce(jnp.add, [jnp.exp(part - peak) for part in parts])
    column_lse = peak + jnp.log(total)
    lcol[...] = jnp.broadcast_to(column_lse, (8, COLS))
    diag = functools.reduce(jnp.add, [cstat[k, 1:2, :] for k in range(8)])
    part = column_lse - 2.0 * diag
    part = functools.reduce(jnp.add, [part[:, g * 128 : (g + 1) * 128] for g in range(8)])
    loss_c[me_row] = jnp.where(sub[:8] == 0, jnp.broadcast_to(part, (8, 128)), 0.0)

    lax.fori_loop(1, 16, rs_arrive, 0)
    peak = rstat[0]
    for k in range(1, 16):
        peak = jnp.maximum(peak, rstat[k])
    total = jnp.zeros((8, QB), F32)
    for k in range(16):
        total += jnp.exp(rstat[k] - peak)
    row_lse = peak + jnp.log(total)
    for q in range(NQ):
        lrow[q] = jnp.broadcast_to(row_lse[q : q + 1, :], (128, QB)).T
    loss_r[me_p] = row_lse[:, :128] + row_lse[:, 128:]

    def to_own(q):
        low = pl.multiple_of(h * OWN, OWN)
        high = pl.multiple_of((1 - h) * OWN, OWN)
        return dq.at[q, pl.ds(low, OWN), :], dq.at[q, pl.ds(high, OWN), :]

    def dsib_copy(q):
        return remote(to_own(q)[1], sib.at[q], dsib_send.at[q], dsib_recv.at[q], sibling)

    def gq_copy(q):
        return remote(outq.at[q], inq.at[me_q], gq_send.at[q], gq_recv.at[me_q], chip_peer(q))

    def gp_copy(p):
        return remote(outp.at[p], inp.at[me_p], gp_send.at[p], gp_recv.at[me_p], col_peer(p))

    def turn_q(i):
        return (me_q + 1 + i) % NQ

    def weights(q):
        for r in range(QB // CH):
            rows = slice(r * CH, (r + 1) * CH)
            level = lrow[q, rows, :]
            for g in range(8):
                cols = slice(g * 128, (g + 1) * 128)
                s = sbuf[q, rows, cols]
                er = jnp.exp(s - level)
                ec = jnp.exp(eighths(s) - lcol[:, cols][None]).reshape(CH, 128)
                pair_weight = (er + ec).astype(BF).astype(F32)
                hard_weight = er.astype(BF).astype(F32)
                count = mbuf[q, rows, cols].astype(F32)
                wbuf[q, rows, cols] = (pair_weight + count * hard_weight).astype(BF)

    def query_sum(q):
        everything = pbuf[...].reshape(COLS, D)
        for n in range(3):
            cols = slice(n * 256, (n + 1) * 256)
            dq[q, :, cols] = dot_nn(wbuf[q], everything[:, cols])

    def take_sibling(q):
        dsib_copy(q).wait_recv()
        low = pl.multiple_of(h * OWN, OWN)
        outq[q] = (dq[q, pl.ds(low, OWN), :] + sib[q]).astype(BF)

    lr_start, lr_arrive = all_col(loss_r, lr_send, lr_recv)
    lc_start, lc_arrive = all_row(loss_c, lc_send, lc_recv)
    weights(turn_q(0))
    lax.fori_loop(1, 8, lr_start, 0)
    lax.fori_loop(1, 16, lc_start, 0)

    def second(i, carry):
        @pl.when(i > 1)
        def _():
            dsib_copy(turn_q(i - 2)).start()

        @pl.when(i > 4)
        def _():
            gq_copy(turn_q(i - 5)).start()

        query_sum(turn_q(i - 1))
        weights(turn_q(i))

        @pl.when(i > 3)
        def _():
            take_sibling(turn_q(i - 4))

        return carry

    lax.fori_loop(1, NQ, second, 0)
    query_sum(turn_q(NQ - 1))
    dsib_copy(turn_q(NQ - 2)).start()
    gq_copy(turn_q(NQ - 5)).start()

    def turn_p(i):
        return (me_p // 2 + 1 + i) % 4

    def send_pair(i):
        for k in range(2):
            p = turn_p(i) * 2 + k

            @pl.when(p != me_p)
            def _():
                gp_copy(p).start()

    def third(i, carry):
        block = turn_p(i)
        cols = pl.ds(pl.multiple_of(block * 256, 256), 256)
        left = wbuf[:, :, cols].reshape(ROWS, 256)
        part = dot_tn(left, qbuf[...].reshape(ROWS, D))
        dp[...] = part.reshape(2, OWN, D)
        for k in range(2):
            outp[block * 2 + k] = part[k * OWN : (k + 1) * OWN].astype(BF)

        @pl.when(i == 0)
        def _():
            dsib_copy(turn_q(NQ - 1)).start()

        @pl.when(i < 3)
        def _():
            take_sibling(turn_q(NQ - 4 + i))

        @pl.when((i > 0) & (i < 4))
        def _():
            gq_copy(turn_q(NQ - 5 + i)).start()

        @pl.when(i > 0)
        def _():
            send_pair(i - 1)

        return carry

    lax.fori_loop(0, 4, third, 0)
    dsib_copy(me_q).wait_recv()
    low = pl.multiple_of(h * OWN, OWN)
    gq_ref[...] = dq[me_q, pl.ds(low, OWN), :] + sib[me_q]
    send_pair(3)

    def take_q(j, carry):
        other = (me_q + j) % NQ
        ref = inq.at[other]
        remote(ref, ref, gq_send.at[other], gq_recv.at[other], chip_peer(other)).wait_recv()
        gq_ref[...] += inq[other].astype(F32)
        return carry

    lax.fori_loop(1, NQ, take_q, 0)
    gq_ref[...] = 0.5 * (gq_ref[...] - 2.0 * p_ref[...].astype(F32))

    gp_ref[...] = dp[me_p % 2]

    def take_p(j, carry):
        other = (me_p + j) % NP
        ref = inp.at[other]
        remote(ref, ref, gp_send.at[other], gp_recv.at[other], col_peer(other)).wait_recv()
        gp_ref[...] += inp[other].astype(F32)
        return carry

    lax.fori_loop(1, NP, take_p, 0)
    gp_ref[...] = 0.5 * (gp_ref[...] - 2.0 * q_ref[...].astype(F32))

    lax.fori_loop(1, 8, lr_arrive, 0)
    lax.fori_loop(1, 16, lc_arrive, 0)
    halves = []
    for s in range(2):
        halves.append(functools.reduce(jnp.add, [loss_r[s * 4 + k] for k in range(4)]))
    both = halves[0] + halves[1]
    halves = []
    for s in range(2):
        terms = [loss_c[xx * 4 + s * 2 + hh] for xx in range(4) for hh in range(2)]
        halves.append(functools.reduce(jnp.add, terms))
    both = both + (halves[0] + halves[1])
    both = jnp.sum(jnp.sum(both, axis=0, keepdims=True), axis=1, keepdims=True)
    loss_ref[...] = jnp.broadcast_to(both / (2.0 * 16384), (8, 128))

    for copy in q_sends + p_sends + q_fwd + p_fwd + sib_copies:
        copy.wait_send()

    def left_row(j, carry):
        to = (me_row + j) % 16
        tab_copy(me_row, to).wait_send()
        here = rstat.at[me_row]
        remote(here, here, rs_send.at[to], rs_recv.at[me_row], row_peer(to)).wait_send()
        here = loss_c.at[me_row]
        remote(here, here, lc_send.at[to], lc_recv.at[me_row], row_peer(to)).wait_send()
        return carry

    def left_col(j, carry):
        to = (me_p + j) % 8
        here = cstat.at[me_p]
        remote(here, here, cs_send.at[to], cs_recv.at[me_p], col_peer(to)).wait_send()
        here = loss_r.at[me_p]
        remote(here, here, lr_send.at[to], lr_recv.at[me_p], col_peer(to)).wait_send()
        gp_copy(to).wait_send()
        gq_copy((me_q + j) % 8).wait_send()
        return carry

    def left_sib(q, carry):
        dsib_copy(q).wait_send()
        return carry

    lax.fori_loop(1, 16, left_row, 0)
    lax.fori_loop(1, 8, left_col, 0)
    lax.fori_loop(0, 8, left_sib, 0)


def per_device(queries, passages, hard_ids, list_lengths):
    vm = pl.BlockSpec(memory_space=pltpu.VMEM)
    dma = pltpu.SemaphoreType.DMA
    loss, grad_queries, grad_passages = pl.pallas_call(
        kernel,
        out_shape=(
            jax.ShapeDtypeStruct((8, 128), F32),
            jax.ShapeDtypeStruct((OWN, D), F32),
            jax.ShapeDtypeStruct((OWN, D), F32),
        ),
        in_specs=[vm] * 4,
        out_specs=(vm, vm, vm),
        scratch_shapes=[
            pltpu.VMEM((OWN, D), BF),
            pltpu.VMEM((OWN, D), BF),
            pltpu.VMEM((32, OWN), jnp.int32),
            pltpu.VMEM((32, OWN), F32),
            pltpu.VMEM((NQ, QB, D), BF),
            pltpu.VMEM((NP, OWN, D), BF),
            pltpu.VMEM((NQ, QB, COLS), F32),
            pltpu.VMEM((NQ, QB, COLS), BF),
            pltpu.VMEM((NQ, QB, COLS), BF),
            pltpu.VMEM((128, 256), F32),
            pltpu.VMEM((16, 8, 256), F32),
            pltpu.VMEM((8, COLS), F32),
            pltpu.VMEM((8, COLS), F32),
            pltpu.VMEM((8, COLS), F32),
            pltpu.VMEM((QB, 128), F32),
            pltpu.VMEM((QB, 128), F32),
            pltpu.VMEM((QB, 128), F32),
            pltpu.VMEM((16, 8, QB), F32),
            pltpu.VMEM((8, 2, COLS), F32),
            pltpu.VMEM((NQ, QB, 128), F32),
            pltpu.VMEM((8, COLS), F32),
            pltpu.VMEM((8, 8, 128), F32),
            pltpu.VMEM((16, 8, 128), F32),
            pltpu.VMEM((NQ, QB, D), F32),
            pltpu.VMEM((NQ, OWN, D), F32),
            pltpu.VMEM((NQ, OWN, D), BF),
            pltpu.VMEM((NQ, OWN, D), BF),
            pltpu.VMEM((2, OWN, D), F32),
            pltpu.VMEM((NP, OWN, D), BF),
            pltpu.VMEM((NP, OWN, D), BF),
            dma((8,)),
            dma((8,)),
            dma((8,)),
            dma((8,)),
            dma((8,)),
            dma((8,)),
            dma((16,)),
            dma((16,)),
            dma((16,)),
            dma((16,)),
            dma((8,)),
            dma((8,)),
            dma((8,)),
            dma((8,)),
            dma((16,)),
            dma((16,)),
            dma((8,)),
            dma((8,)),
            dma((8,)),
            dma((8,)),
            dma((8,)),
            dma((8,)),
        ],
        compiler_params=pltpu.CompilerParams(
            collective_id=0, has_side_effects=True, vmem_limit_bytes=60 * 1024 * 1024
        ),
        name="infonce",
    )(queries, passages, hard_ids.T, list_lengths.reshape(1, OWN))
    return loss[0, 0], grad_queries, grad_passages


def solution(mesh):
    placed = (P(("pb", "pa"), None), P(("pb", "pa"), None), P(("pb", "pa"), None), P(("pb", "pa")))
    return jax.shard_map(
        per_device,
        mesh=mesh,
        in_specs=placed,
        out_specs=(P(), P(("pb", "pa"), None), P(("pb", "pa"), None)),
        check_vma=False,
    )
```

```python
import functools

import jax
import jax.numpy as jnp
from jax import lax
from jax.experimental import pallas as pl
from jax.experimental.pallas import tpu as pltpu
from jax.sharding import PartitionSpec as P

BF = jnp.bfloat16
F32 = jnp.float32
MESH = pl.DeviceIdType.MESH
D = 768
OWN = 128
NQ = 8
NP = 8
QB = 256
COLS = 1024
ROWS = 2048
CH = 64
PO, PL, PR, FAR, PAIR, LEFT, RIGHT, ME = range(8)
RING = (2, 3, 1, 2, 0, 3, 1, 0)
FLIP = (1, 1, 1, 0, 1, 0, 0, 0)
NEG = float("-inf")


def dot_nt(a, b):
    return lax.dot_general(a, b, (((1,), (1,)), ((), ())), preferred_element_type=F32)


def dot_nn(a, b):
    return lax.dot_general(a, b, (((1,), (0,)), ((), ())), preferred_element_type=F32)


def dot_tn(a, b):
    return lax.dot_general(a, b, (((0,), (0,)), ((), ())), preferred_element_type=F32)


def eighths(value):
    return value.reshape(value.shape[0] // 8, 8, value.shape[1])


def kernel(
    queries_hbm,
    passages_hbm,
    ids_hbm,
    lengths_hbm,
    loss_ref,
    gq_ref,
    gp_ref,
    queries_ref,
    passages_ref,
    ids_ref,
    lengths_ref,
    q_ref,
    p_ref,
    dest_ref,
    code_ref,
    qbuf,
    pbuf,
    sbuf,
    mbuf,
    wbuf,
    table,
    tabs,
    codes,
    cmax,
    cnext,
    csum,
    rnext,
    wide_ref,
    rsum,
    rstat,
    cstat,
    rlse,
    clse,
    lrow,
    lcol,
    loss_r,
    loss_c,
    dq,
    sib,
    dp,
    most,
    outq,
    inq,
    outq_scale,
    inq_scale,
    outp,
    inp,
    outp_scale,
    inp_scale,
    in_sem,
    q_send,
    q_recv,
    p_send,
    p_recv,
    sib_send,
    sib_recv,
    tab_send,
    tab_recv,
    rs_send,
    rs_recv,
    cs_send,
    cs_recv,
    lr_send,
    lr_recv,
    lc_send,
    lc_recv,
    dsib_send,
    dsib_recv,
    gq_send,
    gq_recv,
    gq_scale_send,
    gq_scale_recv,
    gp_send,
    gp_recv,
    gp_scale_send,
    gp_scale_recv,
):
    pb = lax.axis_index("pb")
    pa = lax.axis_index("pa")
    z, h = pb // 2, pb % 2
    x, y = pa // 4, pa % 4
    pair = z // 2
    zs = z % 2
    zc = (z + 3) % 4
    half, sel = zc // 2, zc % 2
    me_q = x * 2 + zs
    me_p = sel * 4 + y
    me_row = me_q * 2 + h

    def device(xx, yy, zz, hh):
        return (zz * 2 + hh, xx * 4 + yy)

    def row_peer(idx):
        q, hh = idx // 2, idx % 2
        return device(q // 2, y, pair * 2 + q % 2, hh)

    def col_peer(p):
        return device(x, p % 4, (half * 2 + p // 4 + 1) % 4, h)

    def q_index(k):
        return (x + RING[k]) % 4 * 2 + (1 - zs if FLIP[k] else zs)

    def p_index(k):
        return (1 - sel if FLIP[k] else sel) * 4 + (y + RING[k]) % 4

    sibling = device(x, y, z, 1 - h)
    mine = pl.ds(pl.multiple_of(h * OWN, OWN), OWN)
    others = pl.ds(pl.multiple_of((1 - h) * OWN, OWN), OWN)
    loads = [
        pltpu.make_async_copy(src, dst, in_sem.at[k])
        for k, (src, dst) in enumerate(
            [
                (queries_hbm, queries_ref),
                (passages_hbm, passages_ref),
                (ids_hbm, ids_ref),
                (lengths_hbm, lengths_ref),
            ]
        )
    ]
    for load in loads:
        load.start()

    def remote(src, dst, send, recv, to):
        return pltpu.make_async_remote_copy(
            src_ref=src,
            dst_ref=dst,
            send_sem=send,
            recv_sem=recv,
            device_id=to,
            device_id_type=MESH,
        )

    barrier = pltpu.get_barrier_semaphore()

    def greet_row(j, carry):
        pl.semaphore_signal(
            barrier, inc=1, device_id=row_peer((me_row + j) % 16), device_id_type=MESH
        )
        return carry

    def greet_col(j, carry):
        pl.semaphore_signal(
            barrier, inc=1, device_id=col_peer((me_p + j) % 8), device_id_type=MESH
        )
        return carry

    lax.fori_loop(1, 16, greet_row, 0)
    lax.fori_loop(1, 8, greet_col, 0)

    for load in loads:
        load.wait()
    q_ref[...] = queries_ref[...].astype(BF)
    p_ref[...] = passages_ref[...].astype(BF)
    ids = ids_ref[...]
    owner = ids // OWN
    third_z = (owner // 32 + 3) % 4
    dest = (owner // 4) % 4 * 32 + (third_z // 2) * 16 + (owner // 16) % 2 * 8
    dest = dest + (third_z % 2) * 4 + owner % 4
    place = lax.broadcasted_iota(jnp.int32, ids.shape, 0)
    dest_ref[...] = jnp.where(place < lengths_ref[...], dest, -1)
    code_ref[...] = (ids % OWN + 1).astype(F32)
    qbuf[ME, mine, :] = q_ref[...]
    pbuf[ME] = p_ref[...]
    pl.semaphore_wait(barrier, 22)

    def q_at(k, first=0, size=OWN):
        return qbuf.at[k, pl.ds(pl.multiple_of(h * OWN + first, 64), size), :]

    def p_at(k, first=0, size=OWN):
        return pbuf.at[k, pl.ds(first, size), :]

    def ring(at, own, to_left, to_right, to_pair, send, recv):
        plan = [
            (own, at(LEFT), to_right),
            (own, at(RIGHT), to_left),
            (own, at(PAIR), to_pair),
            (at(LEFT, 0, 64), at(FAR, 0, 64), to_right),
            (at(RIGHT, 64, 64), at(FAR, 64, 64), to_left),
            (at(PAIR), at(PL), to_right),
            (at(PAIR), at(PR), to_left),
            (at(FAR), at(PO), to_pair),
        ]
        return [
            remote(src, dst, send.at[k], recv.at[k], to) for k, (src, dst, to) in enumerate(plan)
        ]

    q_to = (
        device((x + 3) % 4, y, z, h),
        device((x + 1) % 4, y, z, h),
        device(x, y, pair * 2 + 1 - zs, h),
    )
    p_to = (
        device(x, (y + 3) % 4, z, h),
        device(x, (y + 1) % 4, z, h),
        device(x, y, (half * 2 + (1 - sel) + 1) % 4, h),
    )
    q_copies = ring(q_at, q_ref, *q_to, q_send, q_recv)
    p_copies = ring(p_at, p_ref, *p_to, p_send, p_recv)
    for k in range(3):
        q_copies[k].start()
        p_copies[k].start()

    sib_copies = [
        remote(q_ref if k == ME else q_at(k), q_at(k), sib_send.at[k], sib_recv.at[k], sibling)
        for k in range(8)
    ]
    sib_copies[ME].start()

    sub = lax.broadcasted_iota(jnp.int32, (128, 128), 0)
    lane = lax.broadcasted_iota(jnp.int32, (128, 128), 1)
    earlier = jnp.where(sub < lane, 1.0, 0.0).astype(BF)
    prefix = jnp.concatenate([earlier, jnp.ones((128, 128), BF)], axis=1)
    row_code = (lane + 1 + 128 * h).astype(F32)
    second_core = h.astype(F32)
    slot_of = (sub % 64).astype(F32)
    rows_here = jnp.where(sub < 64, 1.0 - second_core, second_core)
    table[...] = jnp.zeros_like(table)

    def slot_step(k, count):
        dest = dest_ref[pl.ds(k, 1), :]
        code = code_ref[pl.ds(k, 1), :]
        live = jnp.where(sub == dest, 1.0, 0.0)
        both = dot_nn(live.astype(BF), prefix)
        rank = jnp.sum(live * (both[:, :128] + count), axis=0, keepdims=True)
        value = rows_here * row_code + (1.0 - rows_here) * code
        chosen = jnp.where(slot_of == rank, value, 0.0).astype(BF)
        table[...] += dot_nt(live.astype(BF), chosen)
        return count + both[:, 128:]

    lax.fori_loop(0, 32, slot_step, jnp.zeros((128, 128), F32), unroll=4)

    def tab_copy(idx, to):
        q, hh = to // 2, to % 2
        zz = (pair * 2 + q % 2 + 3) % 4
        group = (q // 2) * 4 + (zz // 2) * 2 + hh
        return remote(
            table.at[pl.ds(pl.multiple_of(group * 8, 8), 8), :],
            tabs.at[idx],
            tab_send.at[to],
            tab_recv.at[idx],
            row_peer(to),
        )

    def tab_start(j, carry):
        tab_copy(me_row, (me_row + j) % 16).start()
        return carry

    lax.fori_loop(1, 16, tab_start, 0)
    tabs[me_row] = table[pl.ds(pl.multiple_of((x * 4 + half * 2 + h) * 8, 8), 8), :]

    for k, slot in ((0, LEFT), (1, RIGHT)):
        q_copies[k].wait_recv()
        q_copies[k + 3].start()
        p_copies[k].wait_recv()
        p_copies[k + 3].start()
        sib_copies[slot].start()
    q_copies[2].wait_recv()
    q_copies[5].start()
    q_copies[6].start()
    p_copies[2].wait_recv()
    p_copies[5].start()
    p_copies[6].start()
    sib_copies[PAIR].start()

    cmax[...] = jnp.full(cmax.shape, NEG, F32)
    cnext[...] = jnp.full(cnext.shape, NEG, F32)
    csum[...] = jnp.zeros_like(csum)
    rnext[...] = jnp.full(rnext.shape, NEG, F32)

    def scores(k, c):
        cols = slice(c * 256, (c + 1) * 256)
        part = dot_nt(qbuf[k], pbuf[2 * c : 2 * c + 2].reshape(256, D))
        sbuf[k, :, cols] = part
        cnext[:, cols] = jnp.maximum(cnext[:, cols], eighths(part).max(0))
        rnext[k] = jnp.maximum(rnext[k], jnp.maximum(part[:, :128], part[:, 128:]))

    for k in (ME, RIGHT, LEFT, PAIR):
        sib_copies[k].wait_recv()
        scores(k, 3)
        scores(k, 2)

    for k in (3, 4):
        q_copies[k].wait_recv()
        p_copies[k].wait_recv()
    q_copies[7].start()
    p_copies[7].start()
    sib_copies[FAR].start()

    def tab_arrive(j, carry):
        other = (me_row + j) % 16
        ref = tabs.at[other]
        remote(ref, ref, tab_send.at[other], tab_recv.at[other], row_peer(other)).wait_recv()
        return carry

    lax.fori_loop(1, 16, tab_arrive, 0)

    tall = (lax.broadcasted_iota(jnp.int32, (QB, 128), 0) + 1).astype(F32)
    near = lane[:8] < 64
    for k in range(8):
        first, last = tabs[2 * q_index(k)], tabs[2 * q_index(k) + 1]
        codes[k, 0:8, :] = jnp.where(near, first, last)
        codes[k, 8:16, :] = pltpu.roll(jnp.where(near, last, first), 64, 1)

    def count_step(k, carry):
        for p in range(NP):
            rows = codes[k, pl.ds(p_index(p), 1), :]
            cols = codes[k, pl.ds(p_index(p) + 8, 1), :]
            rows = jnp.where(tall == rows, 1.0, 0.0).astype(BF)
            cols = jnp.where(tall[:128] == cols, 1.0, 0.0).astype(BF)
            mbuf[k, :, p * 128 : (p + 1) * 128] = dot_nt(rows, cols).astype(BF)
        return carry

    lax.fori_loop(0, NQ, count_step, 0)
    sib_copies[FAR].wait_recv()
    scores(FAR, 3)
    scores(FAR, 2)

    for k, slot in ((5, PL), (6, PR), (7, PO)):
        q_copies[k].wait_recv()
        sib_copies[slot].start()
        p_copies[k].wait_recv()

    def levels(k):
        csum[...] = csum[...] * jnp.exp(cmax[...] - cnext[...])
        cmax[...] = cnext[...]
        top = jnp.max(rnext[k], axis=1, keepdims=True)
        wide_ref[k] = jnp.broadcast_to(top, (QB, 128))

    def sums(k, r):
        rows = slice(r * CH, (r + 1) * CH)
        wide = wide_ref[k, rows, :]
        total = jnp.zeros((CH, 128), F32)
        for g in range(8):
            cols = slice(g * 128, (g + 1) * 128)
            s = sbuf[k, rows, cols]
            e = jnp.exp(s - wide)
            total += e + e * mbuf[k, rows, cols].astype(F32)
            csum[:, cols] += jnp.exp(eighths(s) - cmax[:, cols][None]).sum(0)
        rsum[k, rows, :] = total

    def row_level(k):
        top = wide_ref[k].T[0:1, :]
        total = jnp.sum(rsum[k].T, axis=0, keepdims=True)
        rstat[me_row, pl.ds(q_index(k), 1), :] = top + jnp.log(total)

    turn = (ME, RIGHT, LEFT, PAIR, FAR, PR, PL, PO)
    scores(ME, 1)
    scores(ME, 0)
    for i, k in enumerate(turn):
        later = turn[i + 1] if i < 7 else None
        if later in (PR, PL, PO):
            sib_copies[later].wait_recv()
        levels(k)
        for r in range(4):
            sums(k, r)
            if later in (PR, PL, PO):
                scores(later, r)
            elif later is not None and r < 2:
                scores(later, r)
        row_level(k)

    top = jnp.max(cmax[...], axis=0, keepdims=True)
    total = jnp.sum(csum[...] * jnp.exp(cmax[...] - top), axis=0, keepdims=True)
    total = top + jnp.log(total)
    for p in range(NP):
        cstat[me_p, pl.ds(p_index(p), 1), :] = total[:, p * 128 : (p + 1) * 128]
    diag = eighths(q_ref[...].astype(F32) * p_ref[...].astype(F32)).sum(0)
    diag = functools.reduce(jnp.add, [diag[:, g * 128 : (g + 1) * 128] for g in range(6)])
    cstat[me_p, 8:16, :] = diag

    def all_row(buf, send, recv):
        def start(j, carry):
            to = (me_row + j) % 16
            here = buf.at[me_row]
            remote(here, here, send.at[to], recv.at[me_row], row_peer(to)).start()
            return carry

        def arrive(j, carry):
            other = (me_row + j) % 16
            ref = buf.at[other]
            remote(ref, ref, send.at[other], recv.at[other], row_peer(other)).wait_recv()
            return carry

        return start, arrive

    def all_col(buf, send, recv):
        def start(j, carry):
            to = (me_p + j) % 8
            here = buf.at[me_p]
            remote(here, here, send.at[to], recv.at[me_p], col_peer(to)).start()
            return carry

        def arrive(j, carry):
            other = (me_p + j) % 8
            ref = buf.at[other]
            remote(ref, ref, send.at[other], recv.at[other], col_peer(other)).wait_recv()
            return carry

        return start, arrive

    rs_start, rs_arrive = all_row(rstat, rs_send, rs_recv)
    cs_start, cs_arrive = all_col(cstat, cs_send, cs_recv)
    lax.fori_loop(1, 16, rs_start, 0)
    lax.fori_loop(1, 8, cs_start, 0)
    lax.fori_loop(1, 8, cs_arrive, 0)

    peak = functools.reduce(jnp.maximum, [cstat[k, 0:8, :] for k in range(8)])
    total = functools.reduce(jnp.add, [jnp.exp(cstat[k, 0:8, :] - peak) for k in range(8)])
    column_lse = peak + jnp.log(total)
    clse[...] = column_lse
    for p in range(NP):
        level = clse[pl.ds(p_index(p), 1), :]
        lcol[:, p * 128 : (p + 1) * 128] = jnp.broadcast_to(level, (8, 128))
    diag = functools.reduce(jnp.add, [cstat[k, 8:16, :] for k in range(8)])
    loss_c[me_row] = column_lse - 2.0 * diag

    lax.fori_loop(1, 16, rs_arrive, 0)
    peak = rstat[0]
    for k in range(1, 16):
        peak = jnp.maximum(peak, rstat[k])
    total = jnp.zeros((8, QB), F32)
    for k in range(16):
        total += jnp.exp(rstat[k] - peak)
    row_lse = peak + jnp.log(total)
    rlse[...] = row_lse
    for k in range(NQ):
        level = rlse[pl.ds(q_index(k), 1), :]
        lrow[k] = jnp.broadcast_to(level, (128, QB)).T
    loss_r[me_p] = row_lse[:, :128] + row_lse[:, 128:]

    def weights(k, c):
        for r in range(QB // CH):
            rows = slice(r * CH, (r + 1) * CH)
            level = lrow[k, rows, :]
            for g in (2 * c, 2 * c + 1):
                cols = slice(g * 128, (g + 1) * 128)
                s = sbuf[k, rows, cols]
                er = jnp.exp(s - level)
                ec = jnp.exp(eighths(s) - lcol[:, cols][None]).reshape(CH, 128)
                pair_weight = (er + ec).astype(BF).astype(F32)
                hard_weight = er.astype(BF).astype(F32)
                count = mbuf[k, rows, cols].astype(F32)
                wbuf[k, rows, cols] = (pair_weight + count * hard_weight).astype(BF)

    def query_sum(k, n):
        cols = slice(n * 256, (n + 1) * 256)
        dq[k, :, cols] = dot_nn(wbuf[k], pbuf[...].reshape(COLS, D)[:, cols])

    def passage_sums(c):
        left = wbuf[:, :, c * 256 : (c + 1) * 256].reshape(ROWS, 256)
        part = dot_tn(left, qbuf[...].reshape(ROWS, D))
        dp[2 * c : 2 * c + 2] = part.reshape(2, OWN, D)

    def dsib_copy(k):
        return remote(
            dq.at[k, others, :], sib.at[k], dsib_send.at[k], dsib_recv.at[k], sibling
        )

    def query_part(k):
        def rows(first, size):
            start = pl.multiple_of(h * OWN + first, 32)
            return dq[k, pl.ds(start, size), :] + sib[k, first : first + size, :]

        return rows

    def passage_part(p):
        return lambda first, size: dp[p, first : first + size, :]

    class Sums:
        def __init__(self, part, to, bufs, sems):
            to_left, to_right, to_pair = to
            self.part = part
            self.out, self.inn, self.out_scale, self.in_scale = bufs
            self.sems = sems
            self.block = {0: PO, 1: PL, 2: PR, 3: FAR, 5: PAIR, 6: LEFT, 7: RIGHT}
            self.to = (
                to_pair,
                to_left,
                to_right,
                to_left,
                to_right,
                to_pair,
                to_left,
                to_right,
            )

        def copies(self, k):
            send, recv, scale_send, scale_recv = self.sems
            src, dst = self.out.at[k], self.inn.at[k]
            scale = self.out_scale.at[k]
            if k in (3, 4):
                rows = pl.ds((k - 3) * 64, 64)
                src, dst, scale = self.out.at[3, rows, :], dst.at[rows, :], self.out_scale.at[3]
            return [
                remote(src, dst, send.at[k], recv.at[k], self.to[k]),
                remote(scale, self.in_scale.at[k], scale_send.at[k], scale_recv.at[k], self.to[k]),
            ]

        def start(self, *slots):
            for k in slots:
                for copy in self.copies(k):
                    copy.start()

        def arrive(self, *slots):
            for k in slots:
                for copy in self.copies(k):
                    copy.wait_recv()

        def levels(self, k):
            return jnp.broadcast_to(self.in_scale[k], (OWN, OWN)).T

        def decoded(self, k, level, first, size):
            value = self.inn[k, first : first + size, :].astype(jnp.int32).astype(F32)
            return value * jnp.concatenate([level[first : first + size]] * (D // OWN), axis=1)

        def encode(self, k, added=()):
            part = self.part(self.block[k])
            levels = {a: self.levels(a) for a, _, _ in added}
            for first in range(0, OWN, 32):
                value = part(first, 32)
                for a, low, high in added:
                    if low <= first < high:
                        value = value + self.decoded(a, levels[a], first, 32)
                top = jnp.max(jnp.abs(value), axis=1, keepdims=True)
                top = jnp.maximum(top, 1e-30)
                whole = jnp.round(value * (32766.0 / top)).astype(jnp.int32)
                self.out[k, first : first + 32, :] = whole.astype(jnp.int16)
                most[first : first + 32, :] = jnp.broadcast_to(top, (32, OWN))
            self.out_scale[k] = most[...].T[0:1, :] * (1.0 / 32766.0)

        def finish(self, grad, positive):
            part = self.part(ME)
            levels = {a: self.levels(a) for a in (5, 6, 7)}
            for first in range(0, OWN, 32):
                value = part(first, 32)
                for a in (5, 6, 7):
                    value = value + self.decoded(a, levels[a], first, 32)
                rows = slice(first, first + 32)
                grad[rows, :] = 0.5 * (value - 2.0 * positive[rows, :].astype(F32))

    qs = Sums(
        query_part,
        q_to,
        (outq, inq, outq_scale, inq_scale),
        (gq_send, gq_recv, gq_scale_send, gq_scale_recv),
    )
    ps = Sums(
        passage_part,
        p_to,
        (outp, inp, outp_scale, inp_scale),
        (gp_send, gp_recv, gp_scale_send, gp_scale_recv),
    )
    lr_start, lr_arrive = all_col(loss_r, lr_send, lr_recv)
    lc_start, lc_arrive = all_row(loss_c, lc_send, lc_recv)

    def both(k, *todo):
        for n in range(3):
            query_sum(k, n)
            for work in todo[n::3]:
                weights(*work)

    for c in range(4):
        weights(PO, c)
    both(PO, *[(PL, c) for c in range(4)])
    lax.fori_loop(1, 8, lr_start, 0)
    lax.fori_loop(1, 16, lc_start, 0)
    dsib_copy(PO).start()
    both(PL, *[(PR, c) for c in range(4)])
    dsib_copy(PL).start()
    rest = (FAR, PAIR, LEFT, RIGHT, ME)
    both(PR, *[(k, 0) for k in rest])
    dsib_copy(PO).wait_recv()
    qs.encode(0)
    dsib_copy(PR).start()
    passage_sums(0)
    for k in rest:
        weights(k, 1)
    qs.start(0)
    dsib_copy(PL).wait_recv()
    qs.encode(1)
    ps.encode(0)
    ps.encode(1)
    passage_sums(1)
    for k in rest:
        weights(k, 2)
    qs.start(1)
    ps.start(0, 1)
    dsib_copy(PR).wait_recv()
    qs.encode(2)
    ps.encode(2)
    for k in rest[:1]:
        weights(k, 3)
    both(FAR, *[(k, 3) for k in rest[1:]])
    qs.start(2)
    ps.start(2)
    query_sum(PAIR, 0)
    dsib_copy(FAR).start()
    query_sum(PAIR, 1)
    query_sum(PAIR, 2)
    passage_sums(2)
    dsib_copy(PAIR).start()
    both(LEFT)
    dsib_copy(FAR).wait_recv()
    qs.arrive(0)
    qs.encode(3, [(0, 0, OWN)])
    both(RIGHT)
    qs.start(3, 4)
    dsib_copy(LEFT).start()
    dsib_copy(PAIR).wait_recv()
    qs.arrive(1, 2)
    qs.encode(5, [(1, 0, OWN), (2, 0, OWN)])
    ps.arrive(0)
    ps.encode(3, [(0, 0, OWN)])
    both(ME)
    qs.start(5)
    ps.start(3, 4)
    dsib_copy(RIGHT).start()
    ps.arrive(1, 2)
    ps.encode(5, [(1, 0, OWN), (2, 0, OWN)])
    passage_sums(3)
    ps.start(5)
    dsib_copy(ME).start()
    dsib_copy(LEFT).wait_recv()
    qs.arrive(3)
    qs.encode(6, [(3, 0, 64)])
    dsib_copy(RIGHT).wait_recv()
    qs.arrive(4)
    qs.encode(7, [(4, 64, OWN)])
    qs.start(6, 7)
    ps.arrive(3)
    ps.encode(6, [(3, 0, 64)])
    ps.arrive(4)
    ps.encode(7, [(4, 64, OWN)])
    ps.start(6, 7)
    dsib_copy(ME).wait_recv()
    qs.arrive(5, 6, 7)
    qs.finish(gq_ref, p_ref)
    ps.arrive(5, 6, 7)
    ps.finish(gp_ref, q_ref)

    lax.fori_loop(1, 8, lr_arrive, 0)
    lax.fori_loop(1, 16, lc_arrive, 0)
    halves = []
    for s in range(2):
        halves.append(functools.reduce(jnp.add, [loss_r[s * 4 + k] for k in range(4)]))
    both = halves[0] + halves[1]
    halves = []
    for s in range(2):
        terms = [loss_c[xx * 4 + s * 2 + hh] for xx in range(4) for hh in range(2)]
        halves.append(functools.reduce(jnp.add, terms))
    both = both + (halves[0] + halves[1])
    both = jnp.sum(jnp.sum(both, axis=0, keepdims=True), axis=1, keepdims=True)
    loss_ref[...] = both / (2.0 * 16384)

    for side in (qs, ps):
        for k in range(8):
            for copy in side.copies(k):
                copy.wait_send()
    for copy in q_copies + p_copies + sib_copies:
        copy.wait_send()

    def left_row(j, carry):
        to = (me_row + j) % 16
        tab_copy(me_row, to).wait_send()
        here = rstat.at[me_row]
        remote(here, here, rs_send.at[to], rs_recv.at[me_row], row_peer(to)).wait_send()
        here = loss_c.at[me_row]
        remote(here, here, lc_send.at[to], lc_recv.at[me_row], row_peer(to)).wait_send()
        return carry

    def left_col(j, carry):
        to = (me_p + j) % 8
        here = cstat.at[me_p]
        remote(here, here, cs_send.at[to], cs_recv.at[me_p], col_peer(to)).wait_send()
        here = loss_r.at[me_p]
        remote(here, here, lr_send.at[to], lr_recv.at[me_p], col_peer(to)).wait_send()
        return carry

    def left_sib(q, carry):
        dsib_copy(q).wait_send()
        return carry

    lax.fori_loop(1, 16, left_row, 0)
    lax.fori_loop(1, 8, left_col, 0)
    lax.fori_loop(0, 8, left_sib, 0)


def per_device(queries, passages, hard_ids, list_lengths):
    vm = pl.BlockSpec(memory_space=pltpu.VMEM)
    dma = pltpu.SemaphoreType.DMA
    loss, grad_queries, grad_passages = pl.pallas_call(
        kernel,
        out_shape=(
            jax.ShapeDtypeStruct((1, 1), F32),
            jax.ShapeDtypeStruct((OWN, D), F32),
            jax.ShapeDtypeStruct((OWN, D), F32),
        ),
        in_specs=[pl.BlockSpec(memory_space=pltpu.HBM)] * 4,
        out_specs=(vm, vm, vm),
        scratch_shapes=[
            pltpu.VMEM((OWN, D), F32),
            pltpu.VMEM((OWN, D), F32),
            pltpu.VMEM((32, OWN), jnp.int32),
            pltpu.VMEM((1, OWN), jnp.int32),
            pltpu.VMEM((OWN, D), BF),
            pltpu.VMEM((OWN, D), BF),
            pltpu.VMEM((32, OWN), jnp.int32),
            pltpu.VMEM((32, OWN), F32),
            pltpu.VMEM((NQ, QB, D), BF),
            pltpu.VMEM((NP, OWN, D), BF),
            pltpu.VMEM((NQ, QB, COLS), F32),
            pltpu.VMEM((NQ, QB, COLS), BF),
            pltpu.VMEM((NQ, QB, COLS), BF),
            pltpu.VMEM((128, 128), F32),
            pltpu.VMEM((16, 8, 128), F32),
            pltpu.VMEM((NQ, 16, 128), F32),
            pltpu.VMEM((8, COLS), F32),
            pltpu.VMEM((8, COLS), F32),
            pltpu.VMEM((8, COLS), F32),
            pltpu.VMEM((NQ, QB, 128), F32),
            pltpu.VMEM((NQ, QB, 128), F32),
            pltpu.VMEM((NQ, QB, 128), F32),
            pltpu.VMEM((16, 8, QB), F32),
            pltpu.VMEM((8, 16, 128), F32),
            pltpu.VMEM((8, QB), F32),
            pltpu.VMEM((8, 128), F32),
            pltpu.VMEM((NQ, QB, 128), F32),
            pltpu.VMEM((8, COLS), F32),
            pltpu.VMEM((8, 8, 128), F32),
            pltpu.VMEM((16, 8, 128), F32),
            pltpu.VMEM((NQ, QB, D), F32),
            pltpu.VMEM((NQ, OWN, D), F32),
            pltpu.VMEM((NP, OWN, D), F32),
            pltpu.VMEM((OWN, OWN), F32),
            pltpu.VMEM((8, OWN, D), jnp.int16),
            pltpu.VMEM((8, OWN, D), jnp.int16),
            pltpu.VMEM((8, 1, OWN), F32),
            pltpu.VMEM((8, 1, OWN), F32),
            pltpu.VMEM((8, OWN, D), jnp.int16),
            pltpu.VMEM((8, OWN, D), jnp.int16),
            pltpu.VMEM((8, 1, OWN), F32),
            pltpu.VMEM((8, 1, OWN), F32),
            dma((4,)),
            dma((8,)),
            dma((8,)),
            dma((8,)),
            dma((8,)),
            dma((8,)),
            dma((8,)),
            dma((16,)),
            dma((16,)),
            dma((16,)),
            dma((16,)),
            dma((8,)),
            dma((8,)),
            dma((8,)),
            dma((8,)),
            dma((16,)),
            dma((16,)),
            dma((8,)),
            dma((8,)),
            dma((8,)),
            dma((8,)),
            dma((8,)),
            dma((8,)),
            dma((8,)),
            dma((8,)),
            dma((8,)),
            dma((8,)),
        ],
        compiler_params=pltpu.CompilerParams(
            collective_id=0, has_side_effects=True, vmem_limit_bytes=50 * 1024 * 1024
        ),
        name="infonce",
    )(queries, passages, hard_ids.T, list_lengths.reshape(1, OWN))
    return loss[0, 0], grad_queries, grad_passages


def solution(mesh):
    placed = (P(("pb", "pa"), None), P(("pb", "pa"), None), P(("pb", "pa"), None), P(("pb", "pa")))
    return jax.shard_map(
        per_device,
        mesh=mesh,
        in_specs=placed,
        out_specs=(P(), P(("pb", "pa"), None), P(("pb", "pa"), None)),
        check_vma=False,
    )
```

```python
import functools

import jax
import jax.numpy as jnp
from jax import lax
from jax.experimental import pallas as pl
from jax.experimental.pallas import tpu as pltpu
from jax.sharding import PartitionSpec as P

BF = jnp.bfloat16
F32 = jnp.float32
MESH = pl.DeviceIdType.MESH
D = 768
OWN = 128
NQ = 8
NP = 8
QB = 256
COLS = 1024
ROWS = 2048
CH = 64
PO, PL, PR, FAR, PAIR, LEFT, RIGHT, ME = range(8)
RING = (2, 3, 1, 2, 0, 3, 1, 0)
FLIP = (1, 1, 1, 0, 1, 0, 0, 0)
NEG = float("-inf")
LOG2E = 1.4426950408889634
LN2 = 0.6931471805599453


def dot_nt(a, b):
    return lax.dot_general(a, b, (((1,), (1,)), ((), ())), preferred_element_type=F32)


def dot_nn(a, b):
    return lax.dot_general(a, b, (((1,), (0,)), ((), ())), preferred_element_type=F32)


def dot_tn(a, b):
    return lax.dot_general(a, b, (((0,), (0,)), ((), ())), preferred_element_type=F32)


def eighths(value):
    return value.reshape(value.shape[0] // 8, 8, value.shape[1])


def kernel(
    queries_hbm,
    passages_hbm,
    ids_hbm,
    lengths_hbm,
    loss_ref,
    gq_ref,
    gp_ref,
    queries_ref,
    passages_ref,
    ids_ref,
    lengths_ref,
    q_ref,
    p_ref,
    dest_ref,
    code_ref,
    qbuf,
    pbuf,
    sbuf,
    mbuf,
    wbuf,
    table,
    tabs,
    codes,
    cmax,
    cnext,
    csum,
    rnext,
    wide_ref,
    rsum,
    rstat,
    cstat,
    rlse,
    clse,
    lrow,
    lcol,
    loss_r,
    loss_c,
    dq,
    sib,
    dp,
    most,
    outq,
    inq,
    outq_scale,
    inq_scale,
    outp,
    inp,
    outp_scale,
    inp_scale,
    in_sem,
    q_send,
    q_recv,
    p_send,
    p_recv,
    sib_send,
    sib_recv,
    tab_send,
    tab_recv,
    rs_send,
    rs_recv,
    cs_send,
    cs_recv,
    lr_send,
    lr_recv,
    lc_send,
    lc_recv,
    dsib_send,
    dsib_recv,
    gq_send,
    gq_recv,
    gq_scale_send,
    gq_scale_recv,
    gp_send,
    gp_recv,
    gp_scale_send,
    gp_scale_recv,
):
    pb = lax.axis_index("pb")
    pa = lax.axis_index("pa")
    z, h = pb // 2, pb % 2
    x, y = pa // 4, pa % 4
    pair = z // 2
    zs = z % 2
    zc = (z + 3) % 4
    half, sel = zc // 2, zc % 2
    me_q = x * 2 + zs
    me_p = sel * 4 + y
    me_row = me_q * 2 + h

    def device(xx, yy, zz, hh):
        return (zz * 2 + hh, xx * 4 + yy)

    def row_peer(idx):
        q, hh = idx // 2, idx % 2
        return device(q // 2, y, pair * 2 + q % 2, hh)

    def col_peer(p):
        return device(x, p % 4, (half * 2 + p // 4 + 1) % 4, h)

    def q_index(k):
        return (x + RING[k]) % 4 * 2 + (1 - zs if FLIP[k] else zs)

    def p_index(k):
        return (1 - sel if FLIP[k] else sel) * 4 + (y + RING[k]) % 4

    sibling = device(x, y, z, 1 - h)
    mine = pl.ds(pl.multiple_of(h * OWN, OWN), OWN)
    others = pl.ds(pl.multiple_of((1 - h) * OWN, OWN), OWN)
    loads = [
        pltpu.make_async_copy(src, dst, in_sem.at[k])
        for k, (src, dst) in enumerate(
            [
                (queries_hbm, queries_ref),
                (passages_hbm, passages_ref),
                (ids_hbm, ids_ref),
                (lengths_hbm, lengths_ref),
            ]
        )
    ]
    for load in loads:
        load.start()

    def remote(src, dst, send, recv, to):
        return pltpu.make_async_remote_copy(
            src_ref=src,
            dst_ref=dst,
            send_sem=send,
            recv_sem=recv,
            device_id=to,
            device_id_type=MESH,
        )

    barrier = pltpu.get_barrier_semaphore()

    def greet_row(j, carry):
        pl.semaphore_signal(
            barrier, inc=1, device_id=row_peer((me_row + j) % 16), device_id_type=MESH
        )
        return carry

    def greet_col(j, carry):
        pl.semaphore_signal(
            barrier, inc=1, device_id=col_peer((me_p + j) % 8), device_id_type=MESH
        )
        return carry

    lax.fori_loop(1, 16, greet_row, 0)
    lax.fori_loop(1, 8, greet_col, 0)

    for load in loads:
        load.wait()
    q_ref[...] = queries_ref[...].astype(BF)
    p_ref[...] = passages_ref[...].astype(BF)
    ids = ids_ref[...]
    owner = ids // OWN
    third_z = (owner // 32 + 3) % 4
    dest = (owner // 4) % 4 * 32 + (third_z // 2) * 16 + (owner // 16) % 2 * 8
    dest = dest + (third_z % 2) * 4 + owner % 4
    place = lax.broadcasted_iota(jnp.int32, ids.shape, 0)
    dest_ref[...] = jnp.where(place < lengths_ref[...], dest, -1)
    code_ref[...] = (ids % OWN + 1).astype(F32)
    qbuf[ME, mine, :] = q_ref[...]
    pbuf[ME] = p_ref[...]
    pl.semaphore_wait(barrier, 22)

    def q_at(k, first=0, size=OWN):
        return qbuf.at[k, pl.ds(pl.multiple_of(h * OWN + first, 64), size), :]

    def p_at(k, first=0, size=OWN):
        return pbuf.at[k, pl.ds(first, size), :]

    def ring(at, own, to_left, to_right, to_pair, send, recv):
        plan = [
            (own, at(LEFT), to_right),
            (own, at(RIGHT), to_left),
            (own, at(PAIR), to_pair),
            (at(LEFT, 0, 64), at(FAR, 0, 64), to_right),
            (at(RIGHT, 64, 64), at(FAR, 64, 64), to_left),
            (at(PAIR), at(PL), to_right),
            (at(PAIR), at(PR), to_left),
            (at(FAR), at(PO), to_pair),
        ]
        return [
            remote(src, dst, send, recv.at[k], to) for k, (src, dst, to) in enumerate(plan)
        ]

    q_to = (
        device((x + 3) % 4, y, z, h),
        device((x + 1) % 4, y, z, h),
        device(x, y, pair * 2 + 1 - zs, h),
    )
    p_to = (
        device(x, (y + 3) % 4, z, h),
        device(x, (y + 1) % 4, z, h),
        device(x, y, (half * 2 + (1 - sel) + 1) % 4, h),
    )
    q_copies = ring(q_at, q_ref, *q_to, q_send, q_recv)
    p_copies = ring(p_at, p_ref, *p_to, p_send, p_recv)
    for k in range(3):
        q_copies[k].start()
        p_copies[k].start()

    sib_copies = [
        remote(q_ref if k == ME else q_at(k), q_at(k), sib_send, sib_recv.at[k], sibling)
        for k in range(8)
    ]
    sib_copies[ME].start()

    sub = lax.broadcasted_iota(jnp.int32, (128, 128), 0)
    lane = lax.broadcasted_iota(jnp.int32, (128, 128), 1)
    earlier = jnp.where(sub < lane, 1.0, 0.0).astype(BF)
    prefix = jnp.concatenate([earlier, jnp.ones((128, 128), BF)], axis=1)
    row_code = (lane + 1 + 128 * h).astype(F32)
    second_core = h.astype(F32)
    slot_of = (sub % 64).astype(F32)
    rows_here = jnp.where(sub < 64, 1.0 - second_core, second_core)
    table[...] = jnp.zeros_like(table)

    def slot_step(k, count):
        dest = dest_ref[pl.ds(k, 1), :]
        code = code_ref[pl.ds(k, 1), :]
        live = jnp.where(sub == dest, 1.0, 0.0)
        both = dot_nn(live.astype(BF), prefix)
        rank = jnp.sum(live * (both[:, :128] + count), axis=0, keepdims=True)
        value = rows_here * row_code + (1.0 - rows_here) * code
        chosen = jnp.where(slot_of == rank, value, 0.0).astype(BF)
        table[...] += dot_nt(live.astype(BF), chosen)
        return count + both[:, 128:]

    lax.fori_loop(0, 32, slot_step, jnp.zeros((128, 128), F32), unroll=4)

    def tab_copy(idx, to):
        q, hh = to // 2, to % 2
        zz = (pair * 2 + q % 2 + 3) % 4
        group = (q // 2) * 4 + (zz // 2) * 2 + hh
        return remote(
            table.at[pl.ds(pl.multiple_of(group * 8, 8), 8), :],
            tabs.at[idx],
            tab_send,
            tab_recv,
            row_peer(to),
        )

    def tab_start(j, carry):
        tab_copy(me_row, (me_row + j) % 16).start()
        return carry

    lax.fori_loop(1, 16, tab_start, 0)
    tabs[me_row] = table[pl.ds(pl.multiple_of((x * 4 + half * 2 + h) * 8, 8), 8), :]

    for k, slot in ((0, LEFT), (1, RIGHT)):
        q_copies[k].wait_recv()
        q_copies[k + 3].start()
        p_copies[k].wait_recv()
        p_copies[k + 3].start()
        sib_copies[slot].start()
    q_copies[2].wait_recv()
    q_copies[5].start()
    q_copies[6].start()
    p_copies[2].wait_recv()
    p_copies[5].start()
    p_copies[6].start()
    sib_copies[PAIR].start()

    cmax[...] = jnp.full(cmax.shape, NEG, F32)
    cnext[...] = jnp.full(cnext.shape, NEG, F32)
    csum[...] = jnp.zeros_like(csum)
    rnext[...] = jnp.full(rnext.shape, NEG, F32)

    def scores(k, slots, c):
        cols = slice(c * 256, (c + 1) * 256)
        left = qbuf[k : k + slots].reshape(slots * QB, D)
        part = dot_nt(left, pbuf[2 * c : 2 * c + 2].reshape(256, D)) * LOG2E
        cnext[:, cols] = jnp.maximum(cnext[:, cols], eighths(part).max(0))
        for n in range(slots):
            own = part[n * QB : (n + 1) * QB]
            sbuf[k + n, :, cols] = own
            rnext[k + n] = jnp.maximum(rnext[k + n], jnp.maximum(own[:, :128], own[:, 128:]))

    for k in (RIGHT, PAIR):
        sib_copies[k].wait_recv()
        sib_copies[k + 1].wait_recv()
        scores(k, 2, 3)
        scores(k, 2, 2)

    for k in (3, 4):
        q_copies[k].wait_recv()
        p_copies[k].wait_recv()
    q_copies[7].start()
    p_copies[7].start()
    sib_copies[FAR].start()

    def group(ref, send, recv):
        return remote(ref, ref, send, recv, sibling)

    group(tabs.at[0:15], tab_send, tab_recv).wait_recv()

    tall = (lax.broadcasted_iota(jnp.int32, (QB, 128), 0) + 1).astype(F32)
    near = lane[:8] < 64
    for k in range(8):
        first, last = tabs[2 * q_index(k)], tabs[2 * q_index(k) + 1]
        codes[k, 0:8, :] = jnp.where(near, first, last)
        codes[k, 8:16, :] = pltpu.roll(jnp.where(near, last, first), 64, 1)

    def count_step(k, carry):
        for p in range(NP):
            rows = codes[k, pl.ds(p_index(p), 1), :]
            cols = codes[k, pl.ds(p_index(p) + 8, 1), :]
            rows = jnp.where(tall == rows, 1.0, 0.0).astype(BF)
            cols = jnp.where(tall[:128] == cols, 1.0, 0.0).astype(BF)
            mbuf[k, :, p * 128 : (p + 1) * 128] = dot_nt(rows, cols).astype(BF)
        return carry

    lax.fori_loop(0, NQ, count_step, 0)
    sib_copies[FAR].wait_recv()
    scores(FAR, 1, 3)
    scores(FAR, 1, 2)

    for k, slot in ((5, PL), (6, PR), (7, PO)):
        q_copies[k].wait_recv()
        sib_copies[slot].start()
        p_copies[k].wait_recv()

    def levels(k):
        csum[...] = csum[...] * jnp.exp2(cmax[...] - cnext[...])
        cmax[...] = cnext[...]
        top = jnp.max(rnext[k], axis=1, keepdims=True)
        wide_ref[k] = jnp.broadcast_to(top, (QB, 128))

    def sums(k, r):
        rows = slice(r * CH, (r + 1) * CH)
        wide = wide_ref[k, rows, :]
        total = jnp.zeros((CH, 128), F32)
        for g in range(8):
            cols = slice(g * 128, (g + 1) * 128)
            s = sbuf[k, rows, cols]
            e = jnp.exp2(s - wide)
            total += e + e * mbuf[k, rows, cols].astype(F32)
            csum[:, cols] += jnp.exp2(eighths(s) - cmax[:, cols][None]).sum(0)
        rsum[k, rows, :] = total

    def row_level(k):
        top = wide_ref[k].T[0:1, :]
        total = jnp.sum(rsum[k].T, axis=0, keepdims=True)
        rstat[me_row, pl.ds(q_index(k), 1), :] = top + jnp.log2(total)

    turn = (ME, RIGHT, LEFT, PAIR, FAR, PR, PL, PO)
    plan = {
        ME: [(PAIR, 2, 1), (PAIR, 2, 0)],
        LEFT: [(PR, 2, 1), (PR, 2, 0)],
        FAR: [(PR, 1, 3), (PR, 1, 2)],
        PAIR: [(PO, 2, 3), (PO, 2, 2)],
        PR: [(PO, 2, 1), (PO, 2, 0)],
    }
    scores(RIGHT, 2, 1)
    scores(RIGHT, 2, 0)
    for k in turn:
        if k == LEFT:
            sib_copies[PR].wait_recv()
        if k == PAIR:
            sib_copies[PL].wait_recv()
            sib_copies[PO].wait_recv()
        levels(k)
        for r in range(4):
            sums(k, r)
            if r % 2 and k in plan:
                scores(*plan[k][r // 2])
        row_level(k)

    top = jnp.max(cmax[...], axis=0, keepdims=True)
    total = jnp.sum(csum[...] * jnp.exp2(cmax[...] - top), axis=0, keepdims=True)
    total = top + jnp.log2(total)
    for p in range(NP):
        cstat[me_p, pl.ds(p_index(p), 1), :] = total[:, p * 128 : (p + 1) * 128]
    diag = eighths(q_ref[...].astype(F32) * p_ref[...].astype(F32)).sum(0)
    diag = functools.reduce(jnp.add, [diag[:, g * 128 : (g + 1) * 128] for g in range(6)])
    cstat[me_p, 8:16, :] = diag

    def all_row(buf, send, recv):
        def start(j, carry):
            here = buf.at[me_row]
            remote(here, here, send, recv, row_peer((me_row + j) % 16)).start()
            return carry

        return start

    def all_col(buf, send, recv):
        def start(j, carry):
            here = buf.at[me_p]
            remote(here, here, send, recv, col_peer((me_p + j) % 8)).start()
            return carry

        return start

    rs_start = all_row(rstat, rs_send, rs_recv)
    cs_start = all_col(cstat, cs_send, cs_recv)
    lax.fori_loop(1, 16, rs_start, 0)
    lax.fori_loop(1, 8, cs_start, 0)
    group(cstat.at[0:7], cs_send, cs_recv).wait_recv()

    peak = functools.reduce(jnp.maximum, [cstat[k, 0:8, :] for k in range(8)])
    total = functools.reduce(jnp.add, [jnp.exp2(cstat[k, 0:8, :] - peak) for k in range(8)])
    column_lse = peak + jnp.log2(total)
    clse[...] = column_lse
    for p in range(NP):
        level = clse[pl.ds(p_index(p), 1), :]
        lcol[:, p * 128 : (p + 1) * 128] = jnp.broadcast_to(level, (8, 128))
    diag = functools.reduce(jnp.add, [cstat[k, 8:16, :] for k in range(8)])
    loss_c[me_row] = LN2 * column_lse - 2.0 * diag

    group(rstat.at[0:15], rs_send, rs_recv).wait_recv()
    peak = rstat[0]
    for k in range(1, 16):
        peak = jnp.maximum(peak, rstat[k])
    total = jnp.zeros((8, QB), F32)
    for k in range(16):
        total += jnp.exp2(rstat[k] - peak)
    row_lse = peak + jnp.log2(total)
    rlse[...] = row_lse
    for k in range(NQ):
        level = rlse[pl.ds(q_index(k), 1), :]
        lrow[k] = jnp.broadcast_to(level, (128, QB)).T
    loss_r[me_p] = LN2 * (row_lse[:, :128] + row_lse[:, 128:])

    def weights(k, c):
        for r in range(QB // CH):
            rows = slice(r * CH, (r + 1) * CH)
            level = lrow[k, rows, :]
            for g in (2 * c, 2 * c + 1):
                cols = slice(g * 128, (g + 1) * 128)
                s = sbuf[k, rows, cols]
                er = jnp.exp2(s - level)
                ec = jnp.exp2(eighths(s) - lcol[:, cols][None]).reshape(CH, 128)
                pair_weight = (er + ec).astype(BF)
                hard_weight = er.astype(BF)
                wbuf[k, rows, cols] = pair_weight + mbuf[k, rows, cols] * hard_weight

    def query_sums(k, slots):
        def part(n):
            cols = slice(n * 256, (n + 1) * 256)
            left = wbuf[k : k + slots].reshape(slots * QB, COLS)
            found = dot_nn(left, pbuf[...].reshape(COLS, D)[:, cols])
            dq[k : k + slots, :, cols] = found.reshape(slots, QB, 256)

        return part

    def passage_sums(c):
        def part(n):
            cols = slice(n * 256, (n + 1) * 256)
            left = wbuf[:, :, c * 256 : (c + 1) * 256].reshape(ROWS, 256)
            found = dot_tn(left, qbuf[...].reshape(ROWS, D)[:, cols])
            dp[2 * c : 2 * c + 2, :, cols] = found.reshape(2, OWN, 256)

        return part

    def dsib_copy(k):
        return remote(
            dq.at[k, others, :], sib.at[k], dsib_send, dsib_recv.at[k], sibling
        )

    def query_part(k):
        def rows(first, size):
            start = pl.multiple_of(h * OWN + first, 32)
            return dq[k, pl.ds(start, size), :] + sib[k, first : first + size, :]

        return rows

    def passage_part(p):
        return lambda first, size: dp[p, first : first + size, :]

    class Sums:
        def __init__(self, part, to, bufs, sems):
            to_left, to_right, to_pair = to
            self.part = part
            self.out, self.inn, self.out_scale, self.in_scale = bufs
            self.sems = sems
            self.slots = (
                (PO, 0, OWN, to_pair),
                (PL, 0, OWN, to_left),
                (PR, 0, OWN, to_right),
                (FAR, 0, 64, to_left),
                (FAR, 64, OWN, to_right),
                (PAIR, 0, OWN, to_pair),
                (LEFT, 64, OWN, to_left),
                (RIGHT, 0, 64, to_right),
                (LEFT, 0, 64, to_left),
                (RIGHT, 64, OWN, to_right),
            )

        def copies(self, k):
            send, recv, scale_send, scale_recv = self.sems
            _, low, high, to = self.slots[k]
            src, dst = self.out.at[k], self.inn.at[k]
            if high - low < OWN:
                src, dst = src.at[pl.ds(low, high - low), :], dst.at[pl.ds(low, high - low), :]
            scale, scale_dst = self.out_scale.at[k], self.in_scale.at[k]
            return [
                remote(src, dst, send, recv.at[k], to),
                remote(scale, scale_dst, scale_send, scale_recv.at[k], to),
            ]

        def start(self, *slots):
            for k in slots:
                for copy in self.copies(k):
                    copy.start()

        def arrive(self, *slots):
            for k in slots:
                for copy in self.copies(k):
                    copy.wait_recv()

        def levels(self, k):
            return jnp.broadcast_to(self.in_scale[k], (OWN, OWN)).T

        def decoded(self, k, level, first, size):
            value = self.inn[k, first : first + size, :].astype(jnp.int32).astype(F32)
            return value * jnp.concatenate([level[first : first + size]] * (D // OWN), axis=1)

        def encode(self, k, added=()):
            block, low, high, _ = self.slots[k]
            part = self.part(block)
            levels = {a: self.levels(a) for a in added}
            for first in range(low, high, 32):
                value = part(first, 32)
                for a in added:
                    value = value + self.decoded(a, levels[a], first, 32)
                top = jnp.max(jnp.abs(value), axis=1, keepdims=True)
                top = jnp.maximum(top, 1e-30)
                whole = jnp.round(value * (32766.0 / top)).astype(jnp.int32)
                self.out[k, first : first + 32, :] = whole.astype(jnp.int16)
                most[first : first + 32, :] = jnp.broadcast_to(top, (32, OWN))
            self.out_scale[k] = most[...].T[0:1, :] * (1.0 / 32766.0)

        def finish(self, grad, positive):
            part = self.part(ME)
            levels = {a: self.levels(a) for a in range(5, 10)}
            for first in range(0, OWN, 32):
                value = part(first, 32)
                for a in range(5, 10):
                    if self.slots[a][1] <= first < self.slots[a][2]:
                        value = value + self.decoded(a, levels[a], first, 32)
                rows = slice(first, first + 32)
                grad[rows, :] = 0.5 * (value - 2.0 * positive[rows, :].astype(F32))

    qs = Sums(
        query_part,
        q_to,
        (outq, inq, outq_scale, inq_scale),
        (gq_send, gq_recv, gq_scale_send, gq_scale_recv),
    )
    ps = Sums(
        passage_part,
        p_to,
        (outp, inp, outp_scale, inp_scale),
        (gp_send, gp_recv, gp_scale_send, gp_scale_recv),
    )
    lr_start = all_col(loss_r, lr_send, lr_recv)
    lc_start = all_row(loss_c, lc_send, lc_recv)

    def beside(part, todo=()):
        for n in range(3):
            part(n)
            for work in todo[n::3]:
                weights(*work)

    def every(slots, columns):
        return [(k, c) for k in slots for c in columns]

    most[...] = jnp.ones_like(most)
    rest = (FAR, PAIR, LEFT, RIGHT, ME)
    for work in every((PO, PL, PR), range(4)):
        weights(*work)
    beside(query_sums(PO, 3), every(rest, (0, 1)))
    dsib_copy(PO).start()
    dsib_copy(PL).start()
    dsib_copy(PR).start()
    beside(passage_sums(0), every(rest, (2, 3)))
    dsib_copy(PO).wait_recv()
    qs.encode(0)
    ps.encode(0)
    ps.encode(1)
    qs.start(0)
    ps.start(0, 1)
    dsib_copy(PL).wait_recv()
    qs.encode(1)
    beside(passage_sums(1))
    qs.start(1)
    dsib_copy(PR).wait_recv()
    qs.encode(2)
    ps.encode(2)
    qs.start(2)
    ps.start(2)
    beside(query_sums(FAR, 2))
    beside(query_sums(LEFT, 2))
    for k in (FAR, PAIR, LEFT, RIGHT):
        dsib_copy(k).start()
    beside(passage_sums(2))
    dsib_copy(FAR).wait_recv()
    qs.arrive(0)
    qs.encode(3, [0])
    qs.encode(4, [0])
    qs.start(3, 4)
    ps.arrive(0)
    ps.encode(3, [0])
    ps.encode(4, [0])
    ps.start(3, 4)
    dsib_copy(LEFT).wait_recv()
    qs.encode(6)
    dsib_copy(RIGHT).wait_recv()
    qs.encode(7)
    beside(passage_sums(3))
    qs.start(6, 7)
    dsib_copy(PAIR).wait_recv()
    qs.arrive(1, 2)
    qs.encode(5, [1, 2])
    ps.encode(6)
    ps.encode(7)
    qs.start(5)
    ps.arrive(1, 2)
    ps.encode(5, [1, 2])
    ps.start(6, 7)
    beside(query_sums(ME, 1))
    ps.start(5)
    dsib_copy(ME).start()
    lax.fori_loop(1, 8, lr_start, 0)
    lax.fori_loop(1, 16, lc_start, 0)
    qs.arrive(3)
    qs.encode(8, [3])
    qs.arrive(4)
    qs.encode(9, [4])
    qs.start(8, 9)
    ps.arrive(3)
    ps.encode(8, [3])
    ps.arrive(4)
    ps.encode(9, [4])
    ps.start(8, 9)
    dsib_copy(ME).wait_recv()
    qs.arrive(5, 6, 7, 8, 9)
    qs.finish(gq_ref, p_ref)
    ps.arrive(5, 6, 7, 8, 9)
    ps.finish(gp_ref, q_ref)

    group(loss_r.at[0:7], lr_send, lr_recv).wait_recv()
    group(loss_c.at[0:15], lc_send, lc_recv).wait_recv()
    halves = []
    for s in range(2):
        halves.append(functools.reduce(jnp.add, [loss_r[s * 4 + k] for k in range(4)]))
    both = halves[0] + halves[1]
    halves = []
    for s in range(2):
        terms = [loss_c[xx * 4 + s * 2 + hh] for xx in range(4) for hh in range(2)]
        halves.append(functools.reduce(jnp.add, terms))
    both = both + (halves[0] + halves[1])
    both = jnp.sum(jnp.sum(both, axis=0, keepdims=True), axis=1, keepdims=True)
    loss_ref[...] = both / (2.0 * 16384)

    group(pbuf.at[0:7], q_send, q_recv.at[0]).wait_send()
    group(pbuf.at[0:7], p_send, p_recv.at[0]).wait_send()
    group(pbuf, sib_send, sib_recv.at[0]).wait_send()
    group(tabs.at[0:15], tab_send, tab_recv).wait_send()
    group(rstat.at[0:15], rs_send, rs_recv).wait_send()
    group(cstat.at[0:7], cs_send, cs_recv).wait_send()
    group(loss_r.at[0:7], lr_send, lr_recv).wait_send()
    group(loss_c.at[0:15], lc_send, lc_recv).wait_send()
    group(sib, dsib_send, dsib_recv.at[0]).wait_send()
    group(outq.at[0:7], gq_send, gq_recv.at[0]).wait_send()
    group(outp.at[0:7], gp_send, gp_recv.at[0]).wait_send()
    group(outq_scale, gq_scale_send, gq_scale_recv.at[0]).wait_send()
    group(outp_scale, gp_scale_send, gp_scale_recv.at[0]).wait_send()


def per_device(queries, passages, hard_ids, list_lengths):
    vm = pl.BlockSpec(memory_space=pltpu.VMEM)
    dma = pltpu.SemaphoreType.DMA
    loss, grad_queries, grad_passages = pl.pallas_call(
        kernel,
        out_shape=(
            jax.ShapeDtypeStruct((1, 1), F32),
            jax.ShapeDtypeStruct((OWN, D), F32),
            jax.ShapeDtypeStruct((OWN, D), F32),
        ),
        in_specs=[pl.BlockSpec(memory_space=pltpu.HBM)] * 4,
        out_specs=(vm, vm, vm),
        scratch_shapes=[
            pltpu.VMEM((OWN, D), F32),
            pltpu.VMEM((OWN, D), F32),
            pltpu.VMEM((32, OWN), jnp.int32),
            pltpu.VMEM((1, OWN), jnp.int32),
            pltpu.VMEM((OWN, D), BF),
            pltpu.VMEM((OWN, D), BF),
            pltpu.VMEM((32, OWN), jnp.int32),
            pltpu.VMEM((32, OWN), F32),
            pltpu.VMEM((NQ, QB, D), BF),
            pltpu.VMEM((NP, OWN, D), BF),
            pltpu.VMEM((NQ, QB, COLS), F32),
            pltpu.VMEM((NQ, QB, COLS), BF),
            pltpu.VMEM((NQ, QB, COLS), BF),
            pltpu.VMEM((128, 128), F32),
            pltpu.VMEM((16, 8, 128), F32),
            pltpu.VMEM((NQ, 16, 128), F32),
            pltpu.VMEM((8, COLS), F32),
            pltpu.VMEM((8, COLS), F32),
            pltpu.VMEM((8, COLS), F32),
            pltpu.VMEM((NQ, QB, 128), F32),
            pltpu.VMEM((NQ, QB, 128), F32),
            pltpu.VMEM((NQ, QB, 128), F32),
            pltpu.VMEM((16, 8, QB), F32),
            pltpu.VMEM((8, 16, 128), F32),
            pltpu.VMEM((8, QB), F32),
            pltpu.VMEM((8, 128), F32),
            pltpu.VMEM((NQ, QB, 128), F32),
            pltpu.VMEM((8, COLS), F32),
            pltpu.VMEM((8, 8, 128), F32),
            pltpu.VMEM((16, 8, 128), F32),
            pltpu.VMEM((NQ, QB, D), F32),
            pltpu.VMEM((NQ, OWN, D), F32),
            pltpu.VMEM((NP, OWN, D), F32),
            pltpu.VMEM((OWN, OWN), F32),
            pltpu.VMEM((10, OWN, D), jnp.int16),
            pltpu.VMEM((10, OWN, D), jnp.int16),
            pltpu.VMEM((10, 1, OWN), F32),
            pltpu.VMEM((10, 1, OWN), F32),
            pltpu.VMEM((10, OWN, D), jnp.int16),
            pltpu.VMEM((10, OWN, D), jnp.int16),
            pltpu.VMEM((10, 1, OWN), F32),
            pltpu.VMEM((10, 1, OWN), F32),
            dma((4,)),
            dma,
            dma((8,)),
            dma,
            dma((8,)),
            dma,
            dma((8,)),
            dma,
            dma,
            dma,
            dma,
            dma,
            dma,
            dma,
            dma,
            dma,
            dma,
            dma,
            dma((8,)),
            dma,
            dma((10,)),
            dma,
            dma((10,)),
            dma,
            dma((10,)),
            dma,
            dma((10,)),
        ],
        compiler_params=pltpu.CompilerParams(
            collective_id=0, has_side_effects=True, vmem_limit_bytes=50 * 1024 * 1024
        ),
        name="infonce",
    )(queries, passages, hard_ids.T, list_lengths.reshape(1, OWN))
    return loss[0, 0], grad_queries, grad_passages


def solution(mesh):
    placed = (P(("pb", "pa"), None), P(("pb", "pa"), None), P(("pb", "pa"), None), P(("pb", "pa")))
    return jax.shard_map(
        per_device,
        mesh=mesh,
        in_specs=placed,
        out_specs=(P(), P(("pb", "pa"), None), P(("pb", "pa"), None)),
        check_vma=False,
    )
```

```python
import functools

import jax
import jax.numpy as jnp
from jax import lax
from jax.experimental import pallas as pl
from jax.experimental.pallas import tpu as pltpu
from jax.sharding import PartitionSpec as P

BF = jnp.bfloat16
F32 = jnp.float32
MESH = pl.DeviceIdType.MESH
D = 768
OWN = 128
NQ = 8
NP = 8
QB = 256
COLS = 1024
ROWS = 2048
CH = 64
PO, PL, PR, FAR, PAIR, LEFT, RIGHT, ME = range(8)
RING = (2, 3, 1, 2, 0, 3, 1, 0)
FLIP = (1, 1, 1, 0, 1, 0, 0, 0)
NEG = float("-inf")
LOG2E = 1.4426950408889634
LN2 = 0.6931471805599453


def dot_nt(a, b):
    return lax.dot_general(a, b, (((1,), (1,)), ((), ())), preferred_element_type=F32)


def dot_nn(a, b):
    return lax.dot_general(a, b, (((1,), (0,)), ((), ())), preferred_element_type=F32)


def dot_tn(a, b):
    return lax.dot_general(a, b, (((0,), (0,)), ((), ())), preferred_element_type=F32)


def eighths(value):
    return value.reshape(value.shape[0] // 8, 8, value.shape[1])


def kernel(
    queries_hbm,
    passages_hbm,
    ids_hbm,
    lengths_hbm,
    loss_ref,
    gq_ref,
    gp_ref,
    queries_ref,
    passages_ref,
    ids_ref,
    lengths_ref,
    q_ref,
    p_ref,
    dest_ref,
    code_ref,
    qbuf,
    pbuf,
    sbuf,
    mbuf,
    wbuf,
    table,
    tabs,
    codes,
    cmax,
    cnext,
    csum,
    rnext,
    wide_ref,
    rsum,
    rstat,
    cstat,
    rlse,
    clse,
    lrow,
    lcol,
    loss_r,
    loss_c,
    dq,
    sib,
    dp,
    most,
    outq,
    inq,
    outq_scale,
    inq_scale,
    outp,
    inp,
    outp_scale,
    inp_scale,
    in_sem,
    q_send,
    q_recv,
    p_send,
    p_recv,
    sib_send,
    sib_recv,
    tab_send,
    tab_recv,
    rs_send,
    rs_recv,
    cs_send,
    cs_recv,
    lr_send,
    lr_recv,
    lc_send,
    lc_recv,
    dsib_send,
    dsib_recv,
    gq_send,
    gq_recv,
    gq_scale_send,
    gq_scale_recv,
    gp_send,
    gp_recv,
    gp_scale_send,
    gp_scale_recv,
):
    pb = lax.axis_index("pb")
    pa = lax.axis_index("pa")
    z, h = pb // 2, pb % 2
    x, y = pa // 4, pa % 4
    pair = z // 2
    zs = z % 2
    zc = (z + 3) % 4
    half, sel = zc // 2, zc % 2
    me_q = x * 2 + zs
    me_p = sel * 4 + y
    me_row = me_q * 2 + h

    def device(xx, yy, zz, hh):
        return (zz * 2 + hh, xx * 4 + yy)

    def row_peer(idx):
        q, hh = idx // 2, idx % 2
        return device(q // 2, y, pair * 2 + q % 2, hh)

    def col_peer(p):
        return device(x, p % 4, (half * 2 + p // 4 + 1) % 4, h)

    def q_index(k):
        return (x + RING[k]) % 4 * 2 + (1 - zs if FLIP[k] else zs)

    def p_index(k):
        return (1 - sel if FLIP[k] else sel) * 4 + (y + RING[k]) % 4

    sibling = device(x, y, z, 1 - h)
    mine = pl.ds(pl.multiple_of(h * OWN, OWN), OWN)
    others = pl.ds(pl.multiple_of((1 - h) * OWN, OWN), OWN)
    loads = [
        pltpu.make_async_copy(src, dst, in_sem.at[k])
        for k, (src, dst) in enumerate(
            [
                (queries_hbm, queries_ref),
                (passages_hbm, passages_ref),
                (ids_hbm, ids_ref),
                (lengths_hbm, lengths_ref),
            ]
        )
    ]
    for load in loads:
        load.start()

    def remote(src, dst, send, recv, to):
        return pltpu.make_async_remote_copy(
            src_ref=src,
            dst_ref=dst,
            send_sem=send,
            recv_sem=recv,
            device_id=to,
            device_id_type=MESH,
        )

    barrier = pltpu.get_barrier_semaphore()

    def greet_row(j, carry):
        pl.semaphore_signal(
            barrier, inc=1, device_id=row_peer((me_row + j) % 16), device_id_type=MESH
        )
        return carry

    def greet_col(j, carry):
        pl.semaphore_signal(
            barrier, inc=1, device_id=col_peer((me_p + j) % 8), device_id_type=MESH
        )
        return carry

    lax.fori_loop(1, 16, greet_row, 0)
    lax.fori_loop(1, 8, greet_col, 0)

    for load in loads:
        load.wait()
    q_ref[...] = queries_ref[...].astype(BF)
    p_ref[...] = passages_ref[...].astype(BF)
    ids = ids_ref[...]
    owner = ids // OWN
    third_z = (owner // 32 + 3) % 4
    dest = (owner // 4) % 4 * 32 + (third_z // 2) * 16 + (owner // 16) % 2 * 8
    dest = dest + (third_z % 2) * 4 + owner % 4
    place = lax.broadcasted_iota(jnp.int32, ids.shape, 0)
    dest_ref[...] = jnp.where(place < lengths_ref[...], dest, -1)
    code_ref[...] = (ids % OWN + 1).astype(F32)
    qbuf[ME, mine, :] = q_ref[...]
    pbuf[ME] = p_ref[...]
    pl.semaphore_wait(barrier, 22)

    def q_at(k, first=0, size=OWN):
        return qbuf.at[k, pl.ds(pl.multiple_of(h * OWN + first, 64), size), :]

    def p_at(k, first=0, size=OWN):
        return pbuf.at[k, pl.ds(first, size), :]

    def ring(at, own, to_left, to_right, to_pair, send, recv):
        low, high = own.at[pl.ds(0, 64), :], own.at[pl.ds(64, 64), :]
        plan = [
            (low, at(LEFT, 0, 64), to_right),
            (high, at(RIGHT, 64, 64), to_left),
            (own, at(PAIR), to_pair),
            (high, at(LEFT, 64, 64), to_right),
            (low, at(RIGHT, 0, 64), to_left),
            (at(LEFT, 0, 64), at(FAR, 0, 64), to_right),
            (at(RIGHT, 64, 64), at(FAR, 64, 64), to_left),
            (at(LEFT, 0, 64), at(PL, 0, 64), to_pair),
            (at(RIGHT, 64, 64), at(PR, 64, 64), to_pair),
            (at(PAIR, 64, 64), at(PL, 64, 64), to_right),
            (at(PAIR, 0, 64), at(PR, 0, 64), to_left),
            (at(PL, 0, 64), at(PO, 0, 64), to_right),
            (at(PR, 64, 64), at(PO, 64, 64), to_left),
        ]
        return [
            remote(src, dst, send, recv.at[k], to) for k, (src, dst, to) in enumerate(plan)
        ]

    q_to = (
        device((x + 3) % 4, y, z, h),
        device((x + 1) % 4, y, z, h),
        device(x, y, pair * 2 + 1 - zs, h),
    )
    p_to = (
        device(x, (y + 3) % 4, z, h),
        device(x, (y + 1) % 4, z, h),
        device(x, y, (half * 2 + (1 - sel) + 1) % 4, h),
    )
    q_copies = ring(q_at, q_ref, *q_to, q_send, q_recv)
    p_copies = ring(p_at, p_ref, *p_to, p_send, p_recv)
    for k in range(5):
        q_copies[k].start()
        p_copies[k].start()

    sib_copies = [
        remote(q_ref if k == ME else q_at(k), q_at(k), sib_send, sib_recv.at[k], sibling)
        for k in range(8)
    ]
    sib_copies[ME].start()

    sub = lax.broadcasted_iota(jnp.int32, (128, 128), 0)
    lane = lax.broadcasted_iota(jnp.int32, (128, 128), 1)
    earlier = jnp.where(sub < lane, 1.0, 0.0).astype(BF)
    prefix = jnp.concatenate([earlier, jnp.ones((128, 128), BF)], axis=1)
    row_code = (lane + 1 + 128 * h).astype(F32)
    second_core = h.astype(F32)
    slot_of = (sub % 64).astype(F32)
    rows_here = jnp.where(sub < 64, 1.0 - second_core, second_core)
    table[...] = jnp.zeros_like(table)

    def slot_step(k, count):
        dest = dest_ref[pl.ds(k, 1), :]
        code = code_ref[pl.ds(k, 1), :]
        live = jnp.where(sub == dest, 1.0, 0.0)
        both = dot_nn(live.astype(BF), prefix)
        rank = jnp.sum(live * (both[:, :128] + count), axis=0, keepdims=True)
        value = rows_here * row_code + (1.0 - rows_here) * code
        chosen = jnp.where(slot_of == rank, value, 0.0).astype(BF)
        table[...] += dot_nt(live.astype(BF), chosen)
        return count + both[:, 128:]

    lax.fori_loop(0, 32, slot_step, jnp.zeros((128, 128), F32), unroll=4)

    def tab_copy(idx, to):
        q, hh = to // 2, to % 2
        zz = (pair * 2 + q % 2 + 3) % 4
        group = (q // 2) * 4 + (zz // 2) * 2 + hh
        return remote(
            table.at[pl.ds(pl.multiple_of(group * 8, 8), 8), :],
            tabs.at[idx],
            tab_send,
            tab_recv,
            row_peer(to),
        )

    def tab_start(j, carry):
        tab_copy(me_row, (me_row + j) % 16).start()
        return carry

    lax.fori_loop(1, 16, tab_start, 0)
    tabs[me_row] = table[pl.ds(pl.multiple_of((x * 4 + half * 2 + h) * 8, 8), 8), :]

    def arrive(*ks):
        for k in ks:
            q_copies[k].wait_recv()
            p_copies[k].wait_recv()

    def forward(*ks):
        for k in ks:
            q_copies[k].start()
            p_copies[k].start()

    arrive(0)
    forward(5, 7)
    arrive(1)
    forward(6, 8)
    arrive(3, 4)
    sib_copies[LEFT].start()
    sib_copies[RIGHT].start()
    arrive(2)
    forward(9, 10)
    sib_copies[PAIR].start()

    cmax[...] = jnp.full(cmax.shape, NEG, F32)
    cnext[...] = jnp.full(cnext.shape, NEG, F32)
    csum[...] = jnp.zeros_like(csum)
    rnext[...] = jnp.full(rnext.shape, NEG, F32)

    def scores(k, slots, c):
        cols = slice(c * 256, (c + 1) * 256)
        left = qbuf[k : k + slots].reshape(slots * QB, D)
        part = dot_nt(left, pbuf[2 * c : 2 * c + 2].reshape(256, D)) * LOG2E
        cnext[:, cols] = jnp.maximum(cnext[:, cols], eighths(part).max(0))
        for n in range(slots):
            own = part[n * QB : (n + 1) * QB]
            sbuf[k + n, :, cols] = own
            top = jnp.maximum(own[:, :128], own[:, 128:])
            rnext[c // 2, k + n] = jnp.maximum(rnext[c // 2, k + n], top)

    sib_copies[ME].wait_recv()
    sib_copies[RIGHT].wait_recv()
    scores(RIGHT, 2, 3)
    scores(RIGHT, 2, 2)

    arrive(7)
    forward(11)
    arrive(8)
    forward(12)
    arrive(5, 6)
    sib_copies[FAR].start()
    sib_copies[LEFT].wait_recv()
    sib_copies[PAIR].wait_recv()
    scores(PAIR, 2, 3)
    scores(PAIR, 2, 2)

    def group(ref, send, recv):
        return remote(ref, ref, send, recv, sibling)

    group(tabs.at[0:15], tab_send, tab_recv).wait_recv()

    tall = (lax.broadcasted_iota(jnp.int32, (QB, 128), 0) + 1).astype(F32)
    near = lane[:8] < 64
    for k in range(8):
        first, last = tabs[2 * q_index(k)], tabs[2 * q_index(k) + 1]
        codes[k, 0:8, :] = jnp.where(near, first, last)
        codes[k, 8:16, :] = pltpu.roll(jnp.where(near, last, first), 64, 1)

    def count_step(k, carry):
        for p in range(NP):
            rows = codes[k, pl.ds(p_index(p), 1), :]
            cols = codes[k, pl.ds(p_index(p) + 8, 1), :]
            rows = jnp.where(tall == rows, 1.0, 0.0).astype(BF)
            cols = jnp.where(tall[:128] == cols, 1.0, 0.0).astype(BF)
            mbuf[k, :, p * 128 : (p + 1) * 128] = dot_nt(rows, cols).astype(BF)
        return carry

    lax.fori_loop(FAR, NQ, count_step, 0)
    sib_copies[FAR].wait_recv()

    def levels(half, k):
        cols = slice(half * 512, half * 512 + 512)
        csum[:, cols] = csum[:, cols] * jnp.exp2(cmax[:, cols] - cnext[:, cols])
        cmax[:, cols] = cnext[:, cols]
        top = jnp.max(rnext[half, k], axis=1, keepdims=True)
        wide_ref[half, k] = jnp.broadcast_to(top, (QB, 128))

    def sums(half, k, r):
        rows = slice(r * CH, (r + 1) * CH)
        wide = wide_ref[half, k, rows, :]
        total = jnp.zeros((CH, 128), F32)
        for g in range(half * 4, half * 4 + 4):
            cols = slice(g * 128, (g + 1) * 128)
            s = sbuf[k, rows, cols]
            e = jnp.exp2(s - wide)
            total += e + e * mbuf[k, rows, cols].astype(F32)
            csum[:, cols] += jnp.exp2(eighths(s) - cmax[:, cols][None]).sum(0)
        rsum[half, k, rows, :] = total

    def row_level(k):
        top = jnp.maximum(wide_ref[0, k], wide_ref[1, k])
        total = rsum[0, k] * jnp.exp2(wide_ref[0, k] - top)
        total += rsum[1, k] * jnp.exp2(wide_ref[1, k] - top)
        total = jnp.sum(total.T, axis=0, keepdims=True)
        rstat[me_row, pl.ds(q_index(k), 1), :] = top.T[0:1, :] + jnp.log2(total)

    def sweep(half, k, *todo):
        levels(half, k)
        for r in range(4):
            sums(half, k, r)
            for work in todo[r // 2 :: 2] if r % 2 else ():
                scores(*work)

    sweep(1, ME, (FAR, 1, 3))
    sweep(1, RIGHT, (FAR, 1, 2))
    sweep(1, LEFT)
    sweep(1, PAIR)
    sweep(1, FAR)
    lax.fori_loop(PO, FAR, count_step, 0)

    arrive(9, 10)
    sib_copies[PL].start()
    sib_copies[PR].start()
    arrive(11, 12)
    sib_copies[PO].start()
    scores(RIGHT, 2, 1)
    scores(RIGHT, 2, 0)
    sweep(0, ME, (PAIR, 2, 1))
    sweep(0, RIGHT, (PAIR, 2, 0))
    row_level(ME)
    row_level(RIGHT)
    sib_copies[PR].wait_recv()
    sweep(0, LEFT, (PR, 2, 1))
    sweep(0, PAIR, (PR, 2, 0))
    row_level(LEFT)
    row_level(PAIR)
    sib_copies[PL].wait_recv()
    sib_copies[PO].wait_recv()
    sweep(0, FAR, (PR, 1, 3), (PR, 1, 2))
    row_level(FAR)
    sweep(0, PR, (PO, 2, 3))
    sweep(1, PR, (PO, 2, 2))
    row_level(PR)
    sweep(1, PL, (PO, 2, 1))
    sweep(1, PO, (PO, 2, 0))
    sweep(0, PL)
    sweep(0, PO)
    row_level(PL)
    row_level(PO)

    top = jnp.max(cmax[...], axis=0, keepdims=True)
    total = jnp.sum(csum[...] * jnp.exp2(cmax[...] - top), axis=0, keepdims=True)
    total = top + jnp.log2(total)
    for p in range(NP):
        cstat[me_p, pl.ds(p_index(p), 1), :] = total[:, p * 128 : (p + 1) * 128]
    diag = eighths(q_ref[...].astype(F32) * p_ref[...].astype(F32)).sum(0)
    diag = functools.reduce(jnp.add, [diag[:, g * 128 : (g + 1) * 128] for g in range(6)])
    cstat[me_p, 8:16, :] = diag

    def all_row(buf, send, recv):
        def start(j, carry):
            here = buf.at[me_row]
            remote(here, here, send, recv, row_peer((me_row + j) % 16)).start()
            return carry

        return start

    def all_col(buf, send, recv):
        def start(j, carry):
            here = buf.at[me_p]
            remote(here, here, send, recv, col_peer((me_p + j) % 8)).start()
            return carry

        return start

    rs_start = all_row(rstat, rs_send, rs_recv)
    cs_start = all_col(cstat, cs_send, cs_recv)
    lax.fori_loop(1, 16, rs_start, 0)
    lax.fori_loop(1, 8, cs_start, 0)
    group(cstat.at[0:7], cs_send, cs_recv).wait_recv()

    peak = functools.reduce(jnp.maximum, [cstat[k, 0:8, :] for k in range(8)])
    total = functools.reduce(jnp.add, [jnp.exp2(cstat[k, 0:8, :] - peak) for k in range(8)])
    column_lse = peak + jnp.log2(total)
    clse[...] = column_lse
    for p in range(NP):
        level = clse[pl.ds(p_index(p), 1), :]
        lcol[:, p * 128 : (p + 1) * 128] = jnp.broadcast_to(level, (8, 128))
    diag = functools.reduce(jnp.add, [cstat[k, 8:16, :] for k in range(8)])
    loss_c[me_row] = LN2 * column_lse - 2.0 * diag

    group(rstat.at[0:15], rs_send, rs_recv).wait_recv()
    peak = rstat[0]
    for k in range(1, 16):
        peak = jnp.maximum(peak, rstat[k])
    total = jnp.zeros((8, QB), F32)
    for k in range(16):
        total += jnp.exp2(rstat[k] - peak)
    row_lse = peak + jnp.log2(total)
    rlse[...] = row_lse
    for k in range(NQ):
        level = rlse[pl.ds(q_index(k), 1), :]
        lrow[k] = jnp.broadcast_to(level, (128, QB)).T
    loss_r[me_p] = LN2 * (row_lse[:, :128] + row_lse[:, 128:])

    def weights(k, c):
        for r in range(QB // CH):
            rows = slice(r * CH, (r + 1) * CH)
            level = lrow[k, rows, :]
            for g in (2 * c, 2 * c + 1):
                cols = slice(g * 128, (g + 1) * 128)
                s = sbuf[k, rows, cols]
                er = jnp.exp2(s - level)
                ec = jnp.exp2(eighths(s) - lcol[:, cols][None]).reshape(CH, 128)
                pair_weight = (er + ec).astype(BF)
                hard_weight = er.astype(BF)
                wbuf[k, rows, cols] = pair_weight + mbuf[k, rows, cols] * hard_weight

    def query_sums(k, slots):
        def part(n):
            cols = slice(n * 256, (n + 1) * 256)
            left = wbuf[k : k + slots].reshape(slots * QB, COLS)
            found = dot_nn(left, pbuf[...].reshape(COLS, D)[:, cols])
            dq[k : k + slots, :, cols] = found.reshape(slots, QB, 256)

        return part

    def passage_sums(c):
        def part(n):
            cols = slice(n * 256, (n + 1) * 256)
            left = wbuf[:, :, c * 256 : (c + 1) * 256].reshape(ROWS, 256)
            found = dot_tn(left, qbuf[...].reshape(ROWS, D)[:, cols])
            dp[2 * c : 2 * c + 2, :, cols] = found.reshape(2, OWN, 256)

        return part

    def dsib_copy(k):
        return remote(
            dq.at[k, others, :], sib.at[k], dsib_send, dsib_recv.at[k], sibling
        )

    def query_part(k):
        def rows(first, size):
            start = pl.multiple_of(h * OWN + first, 32)
            return dq[k, pl.ds(start, size), :] + sib[k, first : first + size, :]

        return rows

    def passage_part(p):
        return lambda first, size: dp[p, first : first + size, :]

    class Sums:
        def __init__(self, part, to, bufs, sems):
            to_left, to_right, to_pair = to
            self.part = part
            self.out, self.inn, self.out_scale, self.in_scale = bufs
            self.sems = sems
            self.slots = (
                (PO, 0, OWN, to_pair),
                (PL, 0, OWN, to_left),
                (PR, 0, OWN, to_right),
                (FAR, 0, 64, to_left),
                (FAR, 64, OWN, to_right),
                (PAIR, 0, OWN, to_pair),
                (LEFT, 64, OWN, to_left),
                (RIGHT, 0, 64, to_right),
                (LEFT, 0, 64, to_left),
                (RIGHT, 64, OWN, to_right),
            )

        def copies(self, k):
            send, recv, scale_send, scale_recv = self.sems
            _, low, high, to = self.slots[k]
            src, dst = self.out.at[k], self.inn.at[k]
            if high - low < OWN:
                src, dst = src.at[pl.ds(low, high - low), :], dst.at[pl.ds(low, high - low), :]
            scale, scale_dst = self.out_scale.at[k], self.in_scale.at[k]
            return [
                remote(src, dst, send, recv.at[k], to),
                remote(scale, scale_dst, scale_send, scale_recv.at[k], to),
            ]

        def start(self, *slots):
            for k in slots:
                for copy in self.copies(k):
                    copy.start()

        def arrive(self, *slots):
            for k in slots:
                for copy in self.copies(k):
                    copy.wait_recv()

        def levels(self, k):
            return jnp.broadcast_to(self.in_scale[k], (OWN, OWN)).T

        def decoded(self, k, level, first, size):
            value = self.inn[k, first : first + size, :].astype(jnp.int32).astype(F32)
            return value * jnp.concatenate([level[first : first + size]] * (D // OWN), axis=1)

        def encode(self, k, added=()):
            block, low, high, _ = self.slots[k]
            part = self.part(block)
            levels = {a: self.levels(a) for a in added}
            for first in range(low, high, 32):
                value = part(first, 32)
                for a in added:
                    value = value + self.decoded(a, levels[a], first, 32)
                top = jnp.max(jnp.abs(value), axis=1, keepdims=True)
                top = jnp.maximum(top, 1e-30)
                whole = jnp.round(value * (32766.0 / top)).astype(jnp.int32)
                self.out[k, first : first + 32, :] = whole.astype(jnp.int16)
                most[first : first + 32, :] = jnp.broadcast_to(top, (32, OWN))
            self.out_scale[k] = most[...].T[0:1, :] * (1.0 / 32766.0)

        def finish(self, grad, positive):
            part = self.part(ME)
            levels = {a: self.levels(a) for a in range(5, 10)}
            for first in range(0, OWN, 32):
                value = part(first, 32)
                for a in range(5, 10):
                    if self.slots[a][1] <= first < self.slots[a][2]:
                        value = value + self.decoded(a, levels[a], first, 32)
                rows = slice(first, first + 32)
                grad[rows, :] = 0.5 * (value - 2.0 * positive[rows, :].astype(F32))

    qs = Sums(
        query_part,
        q_to,
        (outq, inq, outq_scale, inq_scale),
        (gq_send, gq_recv, gq_scale_send, gq_scale_recv),
    )
    ps = Sums(
        passage_part,
        p_to,
        (outp, inp, outp_scale, inp_scale),
        (gp_send, gp_recv, gp_scale_send, gp_scale_recv),
    )
    lr_start = all_col(loss_r, lr_send, lr_recv)
    lc_start = all_row(loss_c, lc_send, lc_recv)

    def beside(part, todo=()):
        for n in range(3):
            part(n)
            for work in todo[n::3]:
                weights(*work)

    def every(slots, columns):
        return [(k, c) for k in slots for c in columns]

    most[...] = jnp.ones_like(most)
    rest = (FAR, PAIR, LEFT, RIGHT, ME)
    for work in every((PO, PL, PR), range(4)):
        weights(*work)
    beside(query_sums(PO, 3), every(rest, (0, 1)))
    dsib_copy(PO).start()
    dsib_copy(PL).start()
    dsib_copy(PR).start()
    beside(passage_sums(0), every(rest, (2, 3)))
    dsib_copy(PO).wait_recv()
    qs.encode(0)
    ps.encode(0)
    ps.encode(1)
    qs.start(0)
    ps.start(0, 1)
    dsib_copy(PL).wait_recv()
    qs.encode(1)
    beside(passage_sums(1))
    qs.start(1)
    dsib_copy(PR).wait_recv()
    qs.encode(2)
    ps.encode(2)
    qs.start(2)
    ps.start(2)
    beside(query_sums(FAR, 2))
    beside(query_sums(LEFT, 2))
    for k in (FAR, PAIR, LEFT, RIGHT):
        dsib_copy(k).start()
    beside(passage_sums(2))
    dsib_copy(FAR).wait_recv()
    qs.arrive(0)
    qs.encode(3, [0])
    qs.encode(4, [0])
    qs.start(3, 4)
    ps.arrive(0)
    ps.encode(3, [0])
    ps.encode(4, [0])
    ps.start(3, 4)
    dsib_copy(LEFT).wait_recv()
    qs.encode(6)
    dsib_copy(RIGHT).wait_recv()
    qs.encode(7)
    beside(passage_sums(3))
    qs.start(6, 7)
    dsib_copy(PAIR).wait_recv()
    qs.arrive(1, 2)
    qs.encode(5, [1, 2])
    ps.encode(6)
    ps.encode(7)
    qs.start(5)
    ps.arrive(1, 2)
    ps.encode(5, [1, 2])
    ps.start(6, 7)
    beside(query_sums(ME, 1))
    ps.start(5)
    dsib_copy(ME).start()
    lax.fori_loop(1, 8, lr_start, 0)
    lax.fori_loop(1, 16, lc_start, 0)
    qs.arrive(3)
    qs.encode(8, [3])
    qs.arrive(4)
    qs.encode(9, [4])
    qs.start(8, 9)
    ps.arrive(3)
    ps.encode(8, [3])
    ps.arrive(4)
    ps.encode(9, [4])
    ps.start(8, 9)
    dsib_copy(ME).wait_recv()
    qs.arrive(5, 6, 7, 8, 9)
    qs.finish(gq_ref, p_ref)
    ps.arrive(5, 6, 7, 8, 9)
    ps.finish(gp_ref, q_ref)

    group(loss_r.at[0:7], lr_send, lr_recv).wait_recv()
    group(loss_c.at[0:15], lc_send, lc_recv).wait_recv()
    halves = []
    for s in range(2):
        halves.append(functools.reduce(jnp.add, [loss_r[s * 4 + k] for k in range(4)]))
    both = halves[0] + halves[1]
    halves = []
    for s in range(2):
        terms = [loss_c[xx * 4 + s * 2 + hh] for xx in range(4) for hh in range(2)]
        halves.append(functools.reduce(jnp.add, terms))
    both = both + (halves[0] + halves[1])
    both = jnp.sum(jnp.sum(both, axis=0, keepdims=True), axis=1, keepdims=True)
    loss_ref[...] = both / (2.0 * 16384)

    group(pbuf.at[0:7], q_send, q_recv.at[0]).wait_send()
    group(pbuf.at[0:7], p_send, p_recv.at[0]).wait_send()
    group(pbuf, sib_send, sib_recv.at[0]).wait_send()
    group(tabs.at[0:15], tab_send, tab_recv).wait_send()
    group(rstat.at[0:15], rs_send, rs_recv).wait_send()
    group(cstat.at[0:7], cs_send, cs_recv).wait_send()
    group(loss_r.at[0:7], lr_send, lr_recv).wait_send()
    group(loss_c.at[0:15], lc_send, lc_recv).wait_send()
    group(sib, dsib_send, dsib_recv.at[0]).wait_send()
    group(outq.at[0:7], gq_send, gq_recv.at[0]).wait_send()
    group(outp.at[0:7], gp_send, gp_recv.at[0]).wait_send()
    group(outq_scale, gq_scale_send, gq_scale_recv.at[0]).wait_send()
    group(outp_scale, gp_scale_send, gp_scale_recv.at[0]).wait_send()


def per_device(queries, passages, hard_ids, list_lengths):
    given = (queries, passages, hard_ids.T, list_lengths.reshape(1, OWN))
    given = [pltpu.with_memory_space_constraint(value, pltpu.HBM) for value in given]
    vm = pl.BlockSpec(memory_space=pltpu.VMEM)
    dma = pltpu.SemaphoreType.DMA
    loss, grad_queries, grad_passages = pl.pallas_call(
        kernel,
        out_shape=(
            jax.ShapeDtypeStruct((1, 1), F32),
            jax.ShapeDtypeStruct((OWN, D), F32),
            jax.ShapeDtypeStruct((OWN, D), F32),
        ),
        in_specs=[pl.BlockSpec(memory_space=pltpu.HBM)] * 4,
        out_specs=(vm, vm, vm),
        scratch_shapes=[
            pltpu.VMEM((OWN, D), F32),
            pltpu.VMEM((OWN, D), F32),
            pltpu.VMEM((32, OWN), jnp.int32),
            pltpu.VMEM((1, OWN), jnp.int32),
            pltpu.VMEM((OWN, D), BF),
            pltpu.VMEM((OWN, D), BF),
            pltpu.VMEM((32, OWN), jnp.int32),
            pltpu.VMEM((32, OWN), F32),
            pltpu.VMEM((NQ, QB, D), BF),
            pltpu.VMEM((NP, OWN, D), BF),
            pltpu.VMEM((NQ, QB, COLS), F32),
            pltpu.VMEM((NQ, QB, COLS), BF),
            pltpu.VMEM((NQ, QB, COLS), BF),
            pltpu.VMEM((128, 128), F32),
            pltpu.VMEM((16, 8, 128), F32),
            pltpu.VMEM((NQ, 16, 128), F32),
            pltpu.VMEM((8, COLS), F32),
            pltpu.VMEM((8, COLS), F32),
            pltpu.VMEM((8, COLS), F32),
            pltpu.VMEM((2, NQ, QB, 128), F32),
            pltpu.VMEM((2, NQ, QB, 128), F32),
            pltpu.VMEM((2, NQ, QB, 128), F32),
            pltpu.VMEM((16, 8, QB), F32),
            pltpu.VMEM((8, 16, 128), F32),
            pltpu.VMEM((8, QB), F32),
            pltpu.VMEM((8, 128), F32),
            pltpu.VMEM((NQ, QB, 128), F32),
            pltpu.VMEM((8, COLS), F32),
            pltpu.VMEM((8, 8, 128), F32),
            pltpu.VMEM((16, 8, 128), F32),
            pltpu.VMEM((NQ, QB, D), F32),
            pltpu.VMEM((NQ, OWN, D), F32),
            pltpu.VMEM((NP, OWN, D), F32),
            pltpu.VMEM((OWN, OWN), F32),
            pltpu.VMEM((10, OWN, D), jnp.int16),
            pltpu.VMEM((10, OWN, D), jnp.int16),
            pltpu.VMEM((10, 1, OWN), F32),
            pltpu.VMEM((10, 1, OWN), F32),
            pltpu.VMEM((10, OWN, D), jnp.int16),
            pltpu.VMEM((10, OWN, D), jnp.int16),
            pltpu.VMEM((10, 1, OWN), F32),
            pltpu.VMEM((10, 1, OWN), F32),
            dma((4,)),
            dma,
            dma((13,)),
            dma,
            dma((13,)),
            dma,
            dma((8,)),
            dma,
            dma,
            dma,
            dma,
            dma,
            dma,
            dma,
            dma,
            dma,
            dma,
            dma,
            dma((8,)),
            dma,
            dma((10,)),
            dma,
            dma((10,)),
            dma,
            dma((10,)),
            dma,
            dma((10,)),
        ],
        compiler_params=pltpu.CompilerParams(
            collective_id=0, has_side_effects=True, vmem_limit_bytes=51 * 1024 * 1024
        ),
        name="infonce",
    )(*given)
    return loss[0, 0], grad_queries, grad_passages


def solution(mesh):
    placed = (P(("pb", "pa"), None), P(("pb", "pa"), None), P(("pb", "pa"), None), P(("pb", "pa")))
    return jax.shard_map(
        per_device,
        mesh=mesh,
        in_specs=placed,
        out_specs=(P(), P(("pb", "pa"), None), P(("pb", "pa"), None)),
        check_vma=False,
    )
```

```python
import functools

import jax
import jax.numpy as jnp
from jax import lax
from jax.experimental import pallas as pl
from jax.experimental.pallas import tpu as pltpu
from jax.sharding import PartitionSpec as P

BF = jnp.bfloat16
F32 = jnp.float32
MESH = pl.DeviceIdType.MESH
D = 768
OWN = 128
NQ = 8
NP = 8
QB = 256
COLS = 1024
ROWS = 2048
CH = 64
PO, PL, PR, FAR, PAIR, LEFT, RIGHT, ME = range(8)
RING = (2, 3, 1, 2, 0, 3, 1, 0)
FLIP = (1, 1, 1, 0, 1, 0, 0, 0)
NEG = float("-inf")
LOG2E = 1.4426950408889634
LN2 = 0.6931471805599453


def dot_nt(a, b):
    return lax.dot_general(a, b, (((1,), (1,)), ((), ())), preferred_element_type=F32)


def dot_nn(a, b):
    return lax.dot_general(a, b, (((1,), (0,)), ((), ())), preferred_element_type=F32)


def dot_tn(a, b):
    return lax.dot_general(a, b, (((0,), (0,)), ((), ())), preferred_element_type=F32)


def eighths(value):
    return value.reshape(value.shape[0] // 8, 8, value.shape[1])


def kernel(
    queries_hbm,
    passages_hbm,
    ids_hbm,
    lengths_hbm,
    loss_ref,
    gq_ref,
    gp_ref,
    queries_ref,
    passages_ref,
    ids_ref,
    lengths_ref,
    q_ref,
    p_ref,
    dest_ref,
    code_ref,
    qbuf,
    pbuf,
    sbuf,
    mbuf,
    wbuf,
    table,
    tabs,
    codes,
    cmax,
    cnext,
    csum,
    rnext,
    wide_ref,
    rsum,
    rstat,
    cstat,
    rlse,
    clse,
    lrow,
    lcol,
    loss_r,
    loss_c,
    dq,
    sib,
    dp,
    exact,
    outq,
    inq,
    outq_scale,
    inq_scale,
    outp,
    inp,
    outp_scale,
    inp_scale,
    in_sem,
    q_send,
    q_recv,
    p_send,
    p_recv,
    sib_send,
    sib_recv,
    tab_send,
    tab_recv,
    rs_send,
    rs_recv,
    cs_send,
    cs_recv,
    lr_send,
    lr_recv,
    lc_send,
    lc_recv,
    dsib_send,
    dsib_recv,
    gq_send,
    gq_recv,
    gq_scale_send,
    gq_scale_recv,
    gp_send,
    gp_recv,
    gp_scale_send,
    gp_scale_recv,
):
    pb = lax.axis_index("pb")
    pa = lax.axis_index("pa")
    z, h = pb // 2, pb % 2
    x, y = pa // 4, pa % 4
    pair = z // 2
    zs = z % 2
    zc = (z + 3) % 4
    half, sel = zc // 2, zc % 2
    me_q = x * 2 + zs
    me_p = sel * 4 + y
    me_row = me_q * 2 + h

    def device(xx, yy, zz, hh):
        return (zz * 2 + hh, xx * 4 + yy)

    def row_peer(idx):
        q, hh = idx // 2, idx % 2
        return device(q // 2, y, pair * 2 + q % 2, hh)

    def col_peer(p):
        return device(x, p % 4, (half * 2 + p // 4 + 1) % 4, h)

    def q_index(k):
        return (x + RING[k]) % 4 * 2 + (1 - zs if FLIP[k] else zs)

    def p_index(k):
        return (1 - sel if FLIP[k] else sel) * 4 + (y + RING[k]) % 4

    sibling = device(x, y, z, 1 - h)
    mine = pl.ds(pl.multiple_of(h * OWN, OWN), OWN)
    others = pl.ds(pl.multiple_of((1 - h) * OWN, OWN), OWN)
    loads = [
        pltpu.make_async_copy(src, dst, in_sem.at[k])
        for k, (src, dst) in enumerate(
            [
                (queries_hbm, queries_ref),
                (passages_hbm, passages_ref),
                (ids_hbm, ids_ref),
                (lengths_hbm, lengths_ref),
            ]
        )
    ]
    for load in loads:
        load.start()

    def remote(src, dst, send, recv, to):
        return pltpu.make_async_remote_copy(
            src_ref=src,
            dst_ref=dst,
            send_sem=send,
            recv_sem=recv,
            device_id=to,
            device_id_type=MESH,
        )

    barrier = pltpu.get_barrier_semaphore()

    def greet_row(j, carry):
        pl.semaphore_signal(
            barrier, inc=1, device_id=row_peer((me_row + j) % 16), device_id_type=MESH
        )
        return carry

    def greet_col(j, carry):
        pl.semaphore_signal(
            barrier, inc=1, device_id=col_peer((me_p + j) % 8), device_id_type=MESH
        )
        return carry

    lax.fori_loop(1, 16, greet_row, 0)
    lax.fori_loop(1, 8, greet_col, 0)

    for load in loads:
        load.wait()
    q_ref[...] = queries_ref[...].astype(BF)
    p_ref[...] = passages_ref[...].astype(BF)
    ids = ids_ref[...]
    owner = ids // OWN
    third_z = (owner // 32 + 3) % 4
    dest = (owner // 4) % 4 * 32 + (third_z // 2) * 16 + (owner // 16) % 2 * 8
    dest = dest + (third_z % 2) * 4 + owner % 4
    place = lax.broadcasted_iota(jnp.int32, ids.shape, 0)
    dest_ref[...] = jnp.where(place < lengths_ref[...], dest, -1)
    code_ref[...] = (ids % OWN + 1).astype(F32)
    qbuf[ME, mine, :] = q_ref[...]
    pbuf[ME] = p_ref[...]
    pl.semaphore_wait(barrier, 22)

    def q_at(k, first=0, size=OWN):
        return qbuf.at[k, pl.ds(pl.multiple_of(h * OWN + first, 64), size), :]

    def p_at(k, first=0, size=OWN):
        return pbuf.at[k, pl.ds(first, size), :]

    def ring(at, own, to_left, to_right, to_pair, send, recv):
        low, high = own.at[pl.ds(0, 64), :], own.at[pl.ds(64, 64), :]
        plan = [
            (low, at(LEFT, 0, 64), to_right),
            (high, at(RIGHT, 64, 64), to_left),
            (own, at(PAIR), to_pair),
            (high, at(LEFT, 64, 64), to_right),
            (low, at(RIGHT, 0, 64), to_left),
            (at(LEFT, 0, 64), at(FAR, 0, 64), to_right),
            (at(RIGHT, 64, 64), at(FAR, 64, 64), to_left),
            (at(LEFT, 0, 64), at(PL, 0, 64), to_pair),
            (at(RIGHT, 64, 64), at(PR, 64, 64), to_pair),
            (at(PAIR, 64, 64), at(PL, 64, 64), to_right),
            (at(PAIR, 0, 64), at(PR, 0, 64), to_left),
            (at(PL, 0, 64), at(PO, 0, 64), to_right),
            (at(PR, 64, 64), at(PO, 64, 64), to_left),
        ]
        return [
            remote(src, dst, send, recv.at[k], to) for k, (src, dst, to) in enumerate(plan)
        ]

    q_to = (
        device((x + 3) % 4, y, z, h),
        device((x + 1) % 4, y, z, h),
        device(x, y, pair * 2 + 1 - zs, h),
    )
    p_to = (
        device(x, (y + 3) % 4, z, h),
        device(x, (y + 1) % 4, z, h),
        device(x, y, (half * 2 + (1 - sel) + 1) % 4, h),
    )
    q_copies = ring(q_at, q_ref, *q_to, q_send, q_recv)
    p_copies = ring(p_at, p_ref, *p_to, p_send, p_recv)
    for k in range(5):
        q_copies[k].start()
        p_copies[k].start()

    sib_copies = [
        remote(q_ref if k == ME else q_at(k), q_at(k), sib_send, sib_recv.at[k], sibling)
        for k in range(8)
    ]
    sib_copies[ME].start()

    sub = lax.broadcasted_iota(jnp.int32, (128, 128), 0)
    lane = lax.broadcasted_iota(jnp.int32, (128, 128), 1)
    earlier = jnp.where(sub < lane, 1.0, 0.0).astype(BF)
    prefix = jnp.concatenate([earlier, jnp.ones((128, 128), BF)], axis=1)
    row_code = (lane + 1 + 128 * h).astype(F32)
    second_core = h.astype(F32)
    slot_of = (sub % 64).astype(F32)
    rows_here = jnp.where(sub < 64, 1.0 - second_core, second_core)
    table[...] = jnp.zeros_like(table)

    def slot_step(k, count):
        dest = dest_ref[pl.ds(k, 1), :]
        code = code_ref[pl.ds(k, 1), :]
        live = jnp.where(sub == dest, 1.0, 0.0)
        both = dot_nn(live.astype(BF), prefix)
        rank = jnp.sum(live * (both[:, :128] + count), axis=0, keepdims=True)
        value = rows_here * row_code + (1.0 - rows_here) * code
        chosen = jnp.where(slot_of == rank, value, 0.0).astype(BF)
        table[...] += dot_nt(live.astype(BF), chosen)
        return count + both[:, 128:]

    lax.fori_loop(0, 32, slot_step, jnp.zeros((128, 128), F32), unroll=4)

    def tab_copy(idx, to):
        q, hh = to // 2, to % 2
        zz = (pair * 2 + q % 2 + 3) % 4
        group = (q // 2) * 4 + (zz // 2) * 2 + hh
        return remote(
            table.at[pl.ds(pl.multiple_of(group * 8, 8), 8), :],
            tabs.at[idx],
            tab_send,
            tab_recv,
            row_peer(to),
        )

    def tab_start(j, carry):
        tab_copy(me_row, (me_row + j) % 16).start()
        return carry

    lax.fori_loop(1, 16, tab_start, 0)
    tabs[me_row] = table[pl.ds(pl.multiple_of((x * 4 + half * 2 + h) * 8, 8), 8), :]

    def arrive(*ks):
        for k in ks:
            q_copies[k].wait_recv()
            p_copies[k].wait_recv()

    def forward(*ks):
        for k in ks:
            q_copies[k].start()
            p_copies[k].start()

    arrive(0)
    forward(5, 7)
    arrive(1)
    forward(6, 8)
    arrive(3, 4)
    sib_copies[LEFT].start()
    sib_copies[RIGHT].start()
    arrive(2)
    forward(9, 10)
    sib_copies[PAIR].start()

    cmax[...] = jnp.full(cmax.shape, NEG, F32)
    cnext[...] = jnp.full(cnext.shape, NEG, F32)
    csum[...] = jnp.zeros_like(csum)
    rnext[...] = jnp.full(rnext.shape, NEG, F32)

    def scores(k, slots, c):
        cols = slice(c * 256, (c + 1) * 256)
        left = qbuf[k : k + slots].reshape(slots * QB, D)
        part = dot_nt(left, pbuf[2 * c : 2 * c + 2].reshape(256, D)) * LOG2E
        cnext[:, cols] = jnp.maximum(cnext[:, cols], eighths(part).max(0))
        for n in range(slots):
            own = part[n * QB : (n + 1) * QB]
            sbuf[k + n, :, cols] = own
            top = jnp.maximum(own[:, :128], own[:, 128:])
            rnext[c // 2, k + n] = jnp.maximum(rnext[c // 2, k + n], top)

    sib_copies[ME].wait_recv()
    sib_copies[RIGHT].wait_recv()
    scores(RIGHT, 2, 3)
    scores(RIGHT, 2, 2)

    arrive(7)
    forward(11)
    arrive(8)
    forward(12)
    arrive(5, 6)
    sib_copies[FAR].start()
    sib_copies[LEFT].wait_recv()
    sib_copies[PAIR].wait_recv()
    scores(PAIR, 2, 3)
    scores(PAIR, 2, 2)

    def group(ref, send, recv):
        return remote(ref, ref, send, recv, sibling)

    group(tabs.at[0:15], tab_send, tab_recv).wait_recv()

    tall = (lax.broadcasted_iota(jnp.int32, (QB, 128), 0) + 1).astype(F32)
    near = lane[:8] < 64
    for k in range(8):
        first, last = tabs[2 * q_index(k)], tabs[2 * q_index(k) + 1]
        codes[k, 0:8, :] = jnp.where(near, first, last)
        codes[k, 8:16, :] = pltpu.roll(jnp.where(near, last, first), 64, 1)

    def count_step(k, carry):
        for p in range(NP):
            rows = codes[k, pl.ds(p_index(p), 1), :]
            cols = codes[k, pl.ds(p_index(p) + 8, 1), :]
            rows = jnp.where(tall == rows, 1.0, 0.0).astype(BF)
            cols = jnp.where(tall[:128] == cols, 1.0, 0.0).astype(BF)
            mbuf[k, :, p * 128 : (p + 1) * 128] = dot_nt(rows, cols).astype(BF)
        return carry

    lax.fori_loop(FAR, NQ, count_step, 0, unroll=True)
    sib_copies[FAR].wait_recv()

    def levels(half, k):
        cols = slice(half * 512, half * 512 + 512)
        csum[:, cols] = csum[:, cols] * jnp.exp2(cmax[:, cols] - cnext[:, cols])
        cmax[:, cols] = cnext[:, cols]
        top = jnp.max(rnext[half, k], axis=1, keepdims=True)
        wide_ref[half, k] = jnp.broadcast_to(top, (QB, 128))

    def sums(half, k, r):
        rows = slice(r * CH, (r + 1) * CH)
        wide = wide_ref[half, k, rows, :]
        total = jnp.zeros((CH, 128), F32)
        for g in range(half * 4, half * 4 + 4):
            cols = slice(g * 128, (g + 1) * 128)
            s = sbuf[k, rows, cols]
            e = jnp.exp2(s - wide)
            total += e + e * mbuf[k, rows, cols].astype(F32)
            csum[:, cols] += jnp.exp2(eighths(s) - cmax[:, cols][None]).sum(0)
        rsum[half, k, rows, :] = total

    def row_level(k):
        top = jnp.maximum(wide_ref[0, k], wide_ref[1, k])
        total = rsum[0, k] * jnp.exp2(wide_ref[0, k] - top)
        total += rsum[1, k] * jnp.exp2(wide_ref[1, k] - top)
        total = jnp.sum(total.T, axis=0, keepdims=True)
        rstat[me_row, pl.ds(q_index(k), 1), :] = top.T[0:1, :] + jnp.log2(total)

    def sweep(half, k, *todo):
        levels(half, k)
        for r in range(4):
            sums(half, k, r)
            for work in todo[r // 2 :: 2] if r % 2 else ():
                scores(*work)

    sweep(1, ME, (FAR, 1, 3))
    sweep(1, RIGHT, (FAR, 1, 2))
    sweep(1, LEFT)
    sweep(1, PAIR)
    sweep(1, FAR)
    lax.fori_loop(PO, FAR, count_step, 0, unroll=True)

    arrive(9, 10)
    sib_copies[PL].start()
    sib_copies[PR].start()
    arrive(11, 12)
    sib_copies[PO].start()
    scores(RIGHT, 2, 1)
    scores(RIGHT, 2, 0)
    sweep(0, ME, (PAIR, 2, 1))
    sweep(0, RIGHT, (PAIR, 2, 0))
    row_level(ME)
    row_level(RIGHT)
    sib_copies[PR].wait_recv()
    sweep(0, LEFT, (PR, 2, 1))
    sweep(0, PAIR, (PR, 2, 0))
    row_level(LEFT)
    row_level(PAIR)
    sib_copies[PL].wait_recv()
    sib_copies[PO].wait_recv()
    sweep(0, FAR, (PR, 1, 3), (PR, 1, 2))
    row_level(FAR)
    sweep(0, PR, (PO, 2, 3))
    sweep(1, PR, (PO, 2, 2))
    row_level(PR)
    sweep(1, PL, (PO, 2, 1))
    sweep(1, PO, (PO, 2, 0))
    sweep(0, PL)
    sweep(0, PO)
    row_level(PL)
    row_level(PO)

    top = jnp.max(cmax[...], axis=0, keepdims=True)
    total = jnp.sum(csum[...] * jnp.exp2(cmax[...] - top), axis=0, keepdims=True)
    total = top + jnp.log2(total)
    for p in range(NP):
        cstat[me_p, pl.ds(p_index(p), 1), :] = total[:, p * 128 : (p + 1) * 128]
    diag = eighths(q_ref[...].astype(F32) * p_ref[...].astype(F32)).sum(0)
    diag = functools.reduce(jnp.add, [diag[:, g * 128 : (g + 1) * 128] for g in range(6)])
    cstat[me_p, 8:16, :] = diag

    def all_row(buf, send, recv):
        def start(j, carry):
            here = buf.at[me_row]
            remote(here, here, send, recv, row_peer((me_row + j) % 16)).start()
            return carry

        return start

    def all_col(buf, send, recv):
        def start(j, carry):
            here = buf.at[me_p]
            remote(here, here, send, recv, col_peer((me_p + j) % 8)).start()
            return carry

        return start

    rs_start = all_row(rstat, rs_send, rs_recv)
    cs_start = all_col(cstat, cs_send, cs_recv)
    lax.fori_loop(1, 16, rs_start, 0)
    lax.fori_loop(1, 8, cs_start, 0)
    group(cstat.at[0:7], cs_send, cs_recv).wait_recv()

    peak = functools.reduce(jnp.maximum, [cstat[k, 0:8, :] for k in range(8)])
    total = functools.reduce(jnp.add, [jnp.exp2(cstat[k, 0:8, :] - peak) for k in range(8)])
    column_lse = peak + jnp.log2(total)
    clse[...] = column_lse
    for p in range(NP):
        level = clse[pl.ds(p_index(p), 1), :]
        lcol[:, p * 128 : (p + 1) * 128] = jnp.broadcast_to(level, (8, 128))
    diag = functools.reduce(jnp.add, [cstat[k, 8:16, :] for k in range(8)])
    loss_c[me_row] = LN2 * column_lse - 2.0 * diag

    group(rstat.at[0:15], rs_send, rs_recv).wait_recv()
    peak = rstat[0]
    for k in range(1, 16):
        peak = jnp.maximum(peak, rstat[k])
    total = jnp.zeros((8, QB), F32)
    for k in range(16):
        total += jnp.exp2(rstat[k] - peak)
    row_lse = peak + jnp.log2(total)
    rlse[...] = row_lse
    for k in range(NQ):
        level = rlse[pl.ds(q_index(k), 1), :]
        lrow[k] = jnp.broadcast_to(level, (128, QB)).T
    loss_r[me_p] = LN2 * (row_lse[:, :128] + row_lse[:, 128:])

    def weights(k, c):
        for r in range(QB // CH):
            rows = slice(r * CH, (r + 1) * CH)
            level = lrow[k, rows, :]
            for g in (2 * c, 2 * c + 1):
                cols = slice(g * 128, (g + 1) * 128)
                s = sbuf[k, rows, cols]
                er = jnp.exp2(s - level)
                ec = jnp.exp2(eighths(s) - lcol[:, cols][None]).reshape(CH, 128)
                pair_weight = (er + ec).astype(BF)
                hard_weight = er.astype(BF)
                wbuf[k, rows, cols] = pair_weight + mbuf[k, rows, cols] * hard_weight

    def query_sums(k, slots):
        def part(n):
            cols = slice(n * 256, (n + 1) * 256)
            left = wbuf[k : k + slots].reshape(slots * QB, COLS)
            found = dot_nn(left, pbuf[...].reshape(COLS, D)[:, cols])
            dq[k : k + slots, :, cols] = found.reshape(slots, QB, 256)

        return part

    def passage_sums(first, slots):
        def part(n):
            cols = slice(n * 256, (n + 1) * 256)
            wide = slots * OWN
            left = wbuf[:, :, first * OWN : first * OWN + wide].reshape(ROWS, wide)
            found = dot_tn(left, qbuf[...].reshape(ROWS, D)[:, cols])
            dp[first : first + slots, :, cols] = found.reshape(slots, OWN, 256)

        return part

    def dsib_copy(k):
        return remote(
            dq.at[k, others, :], sib.at[k], dsib_send, dsib_recv.at[k], sibling
        )

    def query_part(k):
        def rows(first, size):
            start = pl.multiple_of(h * OWN + first, 16)
            return dq[k, pl.ds(start, size), :] + sib[k, first : first + size, :]

        return rows

    def passage_part(p):
        return lambda first, size: dp[p, first : first + size, :]

    class Sums:
        def __init__(self, part, to, exact, bufs, sems):
            self.exact = exact
            to_left, to_right, to_pair = to
            self.part = part
            self.out, self.inn, self.out_scale, self.in_scale = bufs
            self.sems = sems
            self.slots = (
                (PO, 0, OWN, to_pair),
                (PL, 0, OWN, to_left),
                (PR, 0, OWN, to_right),
                (FAR, 0, 64, to_left),
                (FAR, 64, OWN, to_right),
                (PAIR, 0, OWN, to_pair),
                (LEFT, 64, OWN, to_left),
                (RIGHT, 0, 64, to_right),
                (LEFT, 0, 64, to_left),
                (RIGHT, 64, OWN, to_right),
            )

        def copies(self, k):
            send, recv, scale_send, scale_recv = self.sems
            _, low, high, to = self.slots[k]
            src, dst = self.out.at[k], self.inn.at[k]
            if high - low < OWN:
                src, dst = src.at[pl.ds(low, high - low), :], dst.at[pl.ds(low, high - low), :]
            scale, scale_dst = self.out_scale.at[k], self.in_scale.at[k]
            return [
                remote(src, dst, send, recv.at[k], to),
                remote(scale, scale_dst, scale_send, scale_recv.at[k], to),
            ]

        def start(self, *slots):
            for k in slots:
                for copy in self.copies(k):
                    copy.start()

        def arrive(self, *slots):
            for k in slots:
                for copy in self.copies(k):
                    copy.wait_recv()

        def decoded(self, k, first, size):
            value = self.inn[k, first : first + size, :].astype(jnp.int32).astype(F32)
            return value * self.in_scale[k]

        def encode(self, k, added=()):
            block, low, high, _ = self.slots[k]
            part = self.part(block)
            exact = self.exact
            top = jnp.full((8, D), 1e-30, F32)
            for first in range(low, high, 16):
                value = part(first, 16)
                for a in added:
                    value = value + self.decoded(a, first, 16)
                exact[first : first + 16, :] = value
                top = jnp.maximum(top, eighths(jnp.abs(value)).max(0))
            top = jnp.max(top, axis=0, keepdims=True)
            scale = 32766.0 / top
            for first in range(low, high, 16):
                rows = slice(first, first + 16)
                whole = jnp.round(exact[rows, :] * scale).astype(jnp.int32)
                self.out[k, rows, :] = whole.astype(jnp.int16)
            self.out_scale[k] = top * (1.0 / 32766.0)

        def finish(self, grad, positive):
            part = self.part(ME)
            for first in range(0, OWN, 16):
                value = part(first, 16)
                for a in range(5, 10):
                    if self.slots[a][1] <= first < self.slots[a][2]:
                        value = value + self.decoded(a, first, 16)
                rows = slice(first, first + 16)
                grad[rows, :] = 0.5 * (value - 2.0 * positive[rows, :].astype(F32))

    qs = Sums(
        query_part,
        q_to,
        exact.at[0],
        (outq, inq, outq_scale, inq_scale),
        (gq_send, gq_recv, gq_scale_send, gq_scale_recv),
    )
    ps = Sums(
        passage_part,
        p_to,
        exact.at[1],
        (outp, inp, outp_scale, inp_scale),
        (gp_send, gp_recv, gp_scale_send, gp_scale_recv),
    )
    lr_start = all_col(loss_r, lr_send, lr_recv)
    lc_start = all_row(loss_c, lc_send, lc_recv)

    def beside(part, todo=()):
        for n in range(3):
            part(n)
            for work in todo[n::3]:
                weights(*work)

    def every(slots, columns):
        return [(k, c) for k in slots for c in columns]

    rest = (FAR, PAIR, LEFT, RIGHT, ME)
    for work in every((PO, PL, PR), range(4)):
        weights(*work)
    beside(query_sums(PO, 3), every(rest, (0,)))
    dsib_copy(PO).start()
    dsib_copy(PL).start()
    dsib_copy(PR).start()
    beside(passage_sums(PO, 2))
    dsib_copy(PO).wait_recv()
    qs.encode(0)
    ps.encode(0)
    qs.start(0)
    ps.encode(1)
    ps.start(0)
    for work in every(rest, (1,)):
        weights(*work)
    ps.start(1)
    dsib_copy(PL).wait_recv()
    qs.encode(1)
    beside(passage_sums(PR, 2))
    qs.start(1)
    dsib_copy(PR).wait_recv()
    qs.encode(2)
    ps.encode(2)
    qs.start(2)
    for work in every(rest[:2], (2, 3)):
        weights(*work)
    ps.start(2)
    beside(query_sums(FAR, 2))
    for work in every(rest[2:], (2, 3)):
        weights(*work)
    dsib_copy(FAR).start()
    dsib_copy(PAIR).start()
    beside(query_sums(LEFT, 2))
    dsib_copy(LEFT).start()
    dsib_copy(RIGHT).start()
    beside(passage_sums(PAIR, 3))
    dsib_copy(FAR).wait_recv()
    qs.arrive(0)
    qs.encode(3, [0])
    qs.encode(4, [0])
    qs.start(3, 4)
    ps.arrive(0)
    ps.encode(3, [0])
    ps.encode(4, [0])
    ps.start(3, 4)
    ps.encode(6)
    ps.encode(7)
    dsib_copy(LEFT).wait_recv()
    qs.encode(6)
    dsib_copy(RIGHT).wait_recv()
    qs.encode(7)
    ps.start(6, 7)
    dsib_copy(PAIR).wait_recv()
    qs.arrive(1, 2)
    qs.encode(5, [1, 2])
    qs.start(6, 7)
    ps.arrive(1, 2)
    ps.encode(5, [1, 2])
    qs.start(5)
    ps.start(5)
    beside(query_sums(ME, 1))
    lax.fori_loop(1, 8, lr_start, 0)
    lax.fori_loop(1, 16, lc_start, 0)
    dsib_copy(ME).start()
    beside(passage_sums(ME, 1))
    qs.arrive(3)
    qs.encode(8, [3])
    qs.arrive(4)
    qs.encode(9, [4])
    qs.start(8, 9)
    ps.arrive(3)
    ps.encode(8, [3])
    ps.arrive(4)
    ps.encode(9, [4])
    ps.start(8, 9)
    dsib_copy(ME).wait_recv()
    qs.arrive(5, 6, 7, 8, 9)
    qs.finish(gq_ref, p_ref)
    ps.arrive(5, 6, 7, 8, 9)
    ps.finish(gp_ref, q_ref)

    group(loss_r.at[0:7], lr_send, lr_recv).wait_recv()
    group(loss_c.at[0:15], lc_send, lc_recv).wait_recv()
    halves = []
    for s in range(2):
        halves.append(functools.reduce(jnp.add, [loss_r[s * 4 + k] for k in range(4)]))
    both = halves[0] + halves[1]
    halves = []
    for s in range(2):
        terms = [loss_c[xx * 4 + s * 2 + hh] for xx in range(4) for hh in range(2)]
        halves.append(functools.reduce(jnp.add, terms))
    both = both + (halves[0] + halves[1])
    both = jnp.sum(jnp.sum(both, axis=0, keepdims=True), axis=1, keepdims=True)
    loss_ref[...] = both / (2.0 * 16384)

    group(pbuf.at[0:7], q_send, q_recv.at[0]).wait_send()
    group(pbuf.at[0:7], p_send, p_recv.at[0]).wait_send()
    group(pbuf, sib_send, sib_recv.at[0]).wait_send()
    group(tabs.at[0:15], tab_send, tab_recv).wait_send()
    group(rstat.at[0:15], rs_send, rs_recv).wait_send()
    group(cstat.at[0:7], cs_send, cs_recv).wait_send()
    group(loss_r.at[0:7], lr_send, lr_recv).wait_send()
    group(loss_c.at[0:15], lc_send, lc_recv).wait_send()
    group(sib, dsib_send, dsib_recv.at[0]).wait_send()
    group(outq.at[0:7], gq_send, gq_recv.at[0]).wait_send()
    group(outp.at[0:7], gp_send, gp_recv.at[0]).wait_send()
    group(outq_scale, gq_scale_send, gq_scale_recv.at[0]).wait_send()
    group(outp_scale, gp_scale_send, gp_scale_recv.at[0]).wait_send()


def per_device(queries, passages, hard_ids, list_lengths):
    given = (queries, passages, hard_ids.T, list_lengths.reshape(1, OWN))
    given = [pltpu.with_memory_space_constraint(value, pltpu.HBM) for value in given]
    vm = pl.BlockSpec(memory_space=pltpu.VMEM)
    dma = pltpu.SemaphoreType.DMA
    loss, grad_queries, grad_passages = pl.pallas_call(
        kernel,
        out_shape=(
            jax.ShapeDtypeStruct((1, 1), F32),
            jax.ShapeDtypeStruct((OWN, D), F32),
            jax.ShapeDtypeStruct((OWN, D), F32),
        ),
        in_specs=[pl.BlockSpec(memory_space=pltpu.HBM)] * 4,
        out_specs=(vm, vm, vm),
        scratch_shapes=[
            pltpu.VMEM((OWN, D), F32),
            pltpu.VMEM((OWN, D), F32),
            pltpu.VMEM((32, OWN), jnp.int32),
            pltpu.VMEM((1, OWN), jnp.int32),
            pltpu.VMEM((OWN, D), BF),
            pltpu.VMEM((OWN, D), BF),
            pltpu.VMEM((32, OWN), jnp.int32),
            pltpu.VMEM((32, OWN), F32),
            pltpu.VMEM((NQ, QB, D), BF),
            pltpu.VMEM((NP, OWN, D), BF),
            pltpu.VMEM((NQ, QB, COLS), F32),
            pltpu.VMEM((NQ, QB, COLS), BF),
            pltpu.VMEM((NQ, QB, COLS), BF),
            pltpu.VMEM((128, 128), F32),
            pltpu.VMEM((16, 8, 128), F32),
            pltpu.VMEM((NQ, 16, 128), F32),
            pltpu.VMEM((8, COLS), F32),
            pltpu.VMEM((8, COLS), F32),
            pltpu.VMEM((8, COLS), F32),
            pltpu.VMEM((2, NQ, QB, 128), F32),
            pltpu.VMEM((2, NQ, QB, 128), F32),
            pltpu.VMEM((2, NQ, QB, 128), F32),
            pltpu.VMEM((16, 8, QB), F32),
            pltpu.VMEM((8, 16, 128), F32),
            pltpu.VMEM((8, QB), F32),
            pltpu.VMEM((8, 128), F32),
            pltpu.VMEM((NQ, QB, 128), F32),
            pltpu.VMEM((8, COLS), F32),
            pltpu.VMEM((8, 8, 128), F32),
            pltpu.VMEM((16, 8, 128), F32),
            pltpu.VMEM((NQ, QB, D), F32),
            pltpu.VMEM((NQ, OWN, D), F32),
            pltpu.VMEM((NP, OWN, D), F32),
            pltpu.VMEM((2, OWN, D), F32),
            pltpu.VMEM((10, OWN, D), jnp.int16),
            pltpu.VMEM((10, OWN, D), jnp.int16),
            pltpu.VMEM((10, 1, D), F32),
            pltpu.VMEM((10, 1, D), F32),
            pltpu.VMEM((10, OWN, D), jnp.int16),
            pltpu.VMEM((10, OWN, D), jnp.int16),
            pltpu.VMEM((10, 1, D), F32),
            pltpu.VMEM((10, 1, D), F32),
            dma((4,)),
            dma,
            dma((13,)),
            dma,
            dma((13,)),
            dma,
            dma((8,)),
            dma,
            dma,
            dma,
            dma,
            dma,
            dma,
            dma,
            dma,
            dma,
            dma,
            dma,
            dma((8,)),
            dma,
            dma((10,)),
            dma,
            dma((10,)),
            dma,
            dma((10,)),
            dma,
            dma((10,)),
        ],
        compiler_params=pltpu.CompilerParams(
            collective_id=0, has_side_effects=True, vmem_limit_bytes=51 * 1024 * 1024
        ),
        name="infonce",
    )(*given)
    return loss[0, 0], grad_queries, grad_passages


def solution(mesh):
    placed = (P(("pb", "pa"), None), P(("pb", "pa"), None), P(("pb", "pa"), None), P(("pb", "pa")))
    return jax.shard_map(
        per_device,
        mesh=mesh,
        in_specs=placed,
        out_specs=(P(), P(("pb", "pa"), None), P(("pb", "pa"), None)),
        check_vma=False,
    )
```

```python
import functools

import jax
import jax.numpy as jnp
from jax import lax
from jax.experimental import pallas as pl
from jax.experimental.pallas import tpu as pltpu
from jax.sharding import PartitionSpec as P

BF = jnp.bfloat16
F32 = jnp.float32
MESH = pl.DeviceIdType.MESH
D = 768
OWN = 128
NQ = 8
NP = 8
QB = 256
COLS = 1024
ROWS = 2048
CH = 64
PO, PL, PR, FAR, PAIR, LEFT, RIGHT, ME = range(8)
RING = (2, 3, 1, 2, 0, 3, 1, 0)
FLIP = (1, 1, 1, 0, 1, 0, 0, 0)
NEG = float("-inf")
LOG2E = 1.4426950408889634
LN2 = 0.6931471805599453


def dot_nt(a, b):
    return lax.dot_general(a, b, (((1,), (1,)), ((), ())), preferred_element_type=F32)


def dot_nn(a, b):
    return lax.dot_general(a, b, (((1,), (0,)), ((), ())), preferred_element_type=F32)


def dot_tn(a, b):
    return lax.dot_general(a, b, (((0,), (0,)), ((), ())), preferred_element_type=F32)


def eighths(value):
    return value.reshape(value.shape[0] // 8, 8, value.shape[1])


def kernel(
    queries_hbm,
    passages_hbm,
    ids_hbm,
    lengths_hbm,
    loss_ref,
    gq_ref,
    gp_ref,
    queries_ref,
    passages_ref,
    ids_ref,
    lengths_ref,
    q_ref,
    p_ref,
    dest_ref,
    code_ref,
    qbuf,
    pbuf,
    sbuf,
    mbuf,
    wbuf,
    table,
    tabs,
    codes,
    cmax,
    cnext,
    csum,
    rnext,
    wide_ref,
    rsum,
    rstat,
    cstat,
    rlse,
    clse,
    lrow,
    lcol,
    loss_r,
    loss_c,
    dq,
    sib,
    dp,
    exact,
    outq,
    inq,
    outq_scale,
    inq_scale,
    outp,
    inp,
    outp_scale,
    inp_scale,
    in_sem,
    q_send,
    q_recv,
    p_send,
    p_recv,
    sib_send,
    sib_recv,
    tab_send,
    tab_recv,
    rs_send,
    rs_recv,
    cs_send,
    cs_recv,
    lr_send,
    lr_recv,
    lc_send,
    lc_recv,
    dsib_send,
    dsib_recv,
    gq_send,
    gq_recv,
    gq_scale_send,
    gq_scale_recv,
    gp_send,
    gp_recv,
    gp_scale_send,
    gp_scale_recv,
):
    pb = lax.axis_index("pb")
    pa = lax.axis_index("pa")
    z, h = pb // 2, pb % 2
    x, y = pa // 4, pa % 4
    pair = z // 2
    zs = z % 2
    zc = (z + 3) % 4
    half, sel = zc // 2, zc % 2
    me_q = x * 2 + zs
    me_p = sel * 4 + y
    me_row = me_q * 2 + h

    def device(xx, yy, zz, hh):
        return (zz * 2 + hh, xx * 4 + yy)

    def row_peer(idx):
        q, hh = idx // 2, idx % 2
        return device(q // 2, y, pair * 2 + q % 2, hh)

    def col_peer(p):
        return device(x, p % 4, (half * 2 + p // 4 + 1) % 4, h)

    def q_index(k):
        return (x + RING[k]) % 4 * 2 + (1 - zs if FLIP[k] else zs)

    def p_index(k):
        return (1 - sel if FLIP[k] else sel) * 4 + (y + RING[k]) % 4

    sibling = device(x, y, z, 1 - h)
    mine = pl.ds(pl.multiple_of(h * OWN, OWN), OWN)
    others = pl.ds(pl.multiple_of((1 - h) * OWN, OWN), OWN)
    loads = [
        pltpu.make_async_copy(src, dst, in_sem.at[k])
        for k, (src, dst) in enumerate(
            [
                (queries_hbm, queries_ref),
                (passages_hbm, passages_ref),
                (ids_hbm, ids_ref),
                (lengths_hbm, lengths_ref),
            ]
        )
    ]
    for load in loads:
        load.start()

    def remote(src, dst, send, recv, to):
        return pltpu.make_async_remote_copy(
            src_ref=src,
            dst_ref=dst,
            send_sem=send,
            recv_sem=recv,
            device_id=to,
            device_id_type=MESH,
        )

    barrier = pltpu.get_barrier_semaphore()

    def greet_row(j, carry):
        pl.semaphore_signal(
            barrier, inc=1, device_id=row_peer((me_row + j) % 16), device_id_type=MESH
        )
        return carry

    def greet_col(j, carry):
        pl.semaphore_signal(
            barrier, inc=1, device_id=col_peer((me_p + j) % 8), device_id_type=MESH
        )
        return carry

    lax.fori_loop(1, 16, greet_row, 0)
    lax.fori_loop(1, 8, greet_col, 0)

    for load in loads:
        load.wait()
    q_ref[...] = queries_ref[...].astype(BF)
    p_ref[...] = passages_ref[...].astype(BF)
    ids = ids_ref[...]
    owner = ids // OWN
    third_z = (owner // 32 + 3) % 4
    dest = (owner // 4) % 4 * 32 + (third_z // 2) * 16 + (owner // 16) % 2 * 8
    dest = dest + (third_z % 2) * 4 + owner % 4
    place = lax.broadcasted_iota(jnp.int32, ids.shape, 0)
    dest_ref[...] = jnp.where(place < lengths_ref[...], dest, -1)
    code_ref[...] = (ids % OWN + 1).astype(F32)
    qbuf[ME, mine, :] = q_ref[...]
    pbuf[ME] = p_ref[...]
    pl.semaphore_wait(barrier, 22)

    def q_at(k, first=0, size=OWN):
        return qbuf.at[k, pl.ds(pl.multiple_of(h * OWN + first, 64), size), :]

    def p_at(k, first=0, size=OWN):
        return pbuf.at[k, pl.ds(first, size), :]

    def ring(at, own, to_left, to_right, to_pair, send, recv):
        low, high = own.at[pl.ds(0, 64), :], own.at[pl.ds(64, 64), :]
        plan = [
            (low, at(LEFT, 0, 64), to_right),
            (high, at(RIGHT, 64, 64), to_left),
            (own, at(PAIR), to_pair),
            (high, at(LEFT, 64, 64), to_right),
            (low, at(RIGHT, 0, 64), to_left),
            (at(LEFT, 0, 64), at(FAR, 0, 64), to_right),
            (at(RIGHT, 64, 64), at(FAR, 64, 64), to_left),
            (at(LEFT, 0, 64), at(PL, 0, 64), to_pair),
            (at(RIGHT, 64, 64), at(PR, 64, 64), to_pair),
            (at(PAIR, 64, 64), at(PL, 64, 64), to_right),
            (at(PAIR, 0, 64), at(PR, 0, 64), to_left),
            (at(PL, 0, 64), at(PO, 0, 64), to_right),
            (at(PR, 64, 64), at(PO, 64, 64), to_left),
        ]
        return [
            remote(src, dst, send, recv.at[k], to) for k, (src, dst, to) in enumerate(plan)
        ]

    q_to = (
        device((x + 3) % 4, y, z, h),
        device((x + 1) % 4, y, z, h),
        device(x, y, pair * 2 + 1 - zs, h),
    )
    p_to = (
        device(x, (y + 3) % 4, z, h),
        device(x, (y + 1) % 4, z, h),
        device(x, y, (half * 2 + (1 - sel) + 1) % 4, h),
    )
    q_copies = ring(q_at, q_ref, *q_to, q_send, q_recv)
    p_copies = ring(p_at, p_ref, *p_to, p_send, p_recv)
    for k in range(5):
        q_copies[k].start()
        p_copies[k].start()

    sib_copies = [
        remote(q_ref if k == ME else q_at(k), q_at(k), sib_send, sib_recv.at[k], sibling)
        for k in range(8)
    ]
    sib_copies[ME].start()

    sub = lax.broadcasted_iota(jnp.int32, (128, 128), 0)
    lane = lax.broadcasted_iota(jnp.int32, (128, 128), 1)
    earlier = jnp.where(sub < lane, 1.0, 0.0).astype(BF)
    prefix = jnp.concatenate([earlier, jnp.ones((128, 128), BF)], axis=1)
    row_code = (lane + 1 + 128 * h).astype(F32)
    second_core = h.astype(F32)
    slot_of = (sub % 64).astype(F32)
    rows_here = jnp.where(sub < 64, 1.0 - second_core, second_core)
    table[...] = jnp.zeros_like(table)

    def slot_step(k, count):
        dest = dest_ref[pl.ds(k, 1), :]
        code = code_ref[pl.ds(k, 1), :]
        live = jnp.where(sub == dest, 1.0, 0.0)
        both = dot_nn(live.astype(BF), prefix)
        rank = jnp.sum(live * (both[:, :128] + count), axis=0, keepdims=True)
        value = rows_here * row_code + (1.0 - rows_here) * code
        chosen = jnp.where(slot_of == rank, value, 0.0).astype(BF)
        table[...] += dot_nt(live.astype(BF), chosen)
        return count + both[:, 128:]

    lax.fori_loop(0, 32, slot_step, jnp.zeros((128, 128), F32), unroll=4)

    def tab_copy(idx, to):
        q, hh = to // 2, to % 2
        zz = (pair * 2 + q % 2 + 3) % 4
        group = (q // 2) * 4 + (zz // 2) * 2 + hh
        return remote(
            table.at[pl.ds(pl.multiple_of(group * 8, 8), 8), :],
            tabs.at[idx],
            tab_send,
            tab_recv,
            row_peer(to),
        )

    def tab_start(j, carry):
        tab_copy(me_row, (me_row + j) % 16).start()
        return carry

    lax.fori_loop(1, 16, tab_start, 0)
    tabs[me_row] = table[pl.ds(pl.multiple_of((x * 4 + half * 2 + h) * 8, 8), 8), :]

    def arrive(*ks):
        for k in ks:
            q_copies[k].wait_recv()
            p_copies[k].wait_recv()

    def forward(*ks):
        for k in ks:
            q_copies[k].start()
            p_copies[k].start()

    arrive(0)
    forward(5, 7)
    arrive(1)
    forward(6, 8)
    arrive(3, 4)
    sib_copies[LEFT].start()
    sib_copies[RIGHT].start()
    arrive(2)
    forward(9, 10)
    sib_copies[PAIR].start()

    cmax[...] = jnp.full(cmax.shape, NEG, F32)
    cnext[...] = jnp.full(cnext.shape, NEG, F32)
    csum[...] = jnp.zeros_like(csum)
    rnext[...] = jnp.full(rnext.shape, NEG, F32)

    def scores(k, slots, c):
        cols = slice(c * 256, (c + 1) * 256)
        left = qbuf[k : k + slots].reshape(slots * QB, D)
        part = dot_nt(left, pbuf[2 * c : 2 * c + 2].reshape(256, D)) * LOG2E
        cnext[:, cols] = jnp.maximum(cnext[:, cols], eighths(part).max(0))
        for n in range(slots):
            own = part[n * QB : (n + 1) * QB]
            sbuf[k + n, :, cols] = own
            top = jnp.maximum(own[:, :128], own[:, 128:])
            rnext[c // 2, k + n] = jnp.maximum(rnext[c // 2, k + n], top)

    sib_copies[ME].wait_recv()
    sib_copies[RIGHT].wait_recv()
    scores(RIGHT, 2, 3)
    scores(RIGHT, 2, 2)

    arrive(7)
    forward(11)
    arrive(8)
    forward(12)
    arrive(5, 6)
    sib_copies[FAR].start()
    sib_copies[LEFT].wait_recv()
    sib_copies[PAIR].wait_recv()
    scores(PAIR, 2, 3)
    scores(PAIR, 2, 2)

    def group(ref, send, recv):
        return remote(ref, ref, send, recv, sibling)

    group(tabs.at[0:15], tab_send, tab_recv).wait_recv()

    tall = (lax.broadcasted_iota(jnp.int32, (QB, 128), 0) + 1).astype(F32)
    near = lane[:8] < 64
    for k in range(8):
        first, last = tabs[2 * q_index(k)], tabs[2 * q_index(k) + 1]
        codes[k, 0:8, :] = jnp.where(near, first, last)
        codes[k, 8:16, :] = pltpu.roll(jnp.where(near, last, first), 64, 1)

    def count_step(k, carry):
        for p in range(NP):
            rows = codes[k, pl.ds(p_index(p), 1), :]
            cols = codes[k, pl.ds(p_index(p) + 8, 1), :]
            rows = jnp.where(tall == rows, 1.0, 0.0).astype(BF)
            cols = jnp.where(tall[:128] == cols, 1.0, 0.0).astype(BF)
            mbuf[k, :, p * 128 : (p + 1) * 128] = dot_nt(rows, cols).astype(BF)
        return carry

    lax.fori_loop(FAR, NQ, count_step, 0, unroll=True)
    sib_copies[FAR].wait_recv()

    def levels(half, k):
        cols = slice(half * 512, half * 512 + 512)
        csum[:, cols] = csum[:, cols] * jnp.exp2(cmax[:, cols] - cnext[:, cols])
        cmax[:, cols] = cnext[:, cols]
        top = jnp.max(rnext[half, k], axis=1, keepdims=True)
        wide_ref[half, k] = jnp.broadcast_to(top, (QB, 128))

    def sums(half, k, r):
        rows = slice(r * CH, (r + 1) * CH)
        wide = wide_ref[half, k, rows, :]
        total = jnp.zeros((CH, 128), F32)
        for g in range(half * 4, half * 4 + 4):
            cols = slice(g * 128, (g + 1) * 128)
            s = sbuf[k, rows, cols]
            e = jnp.exp2(s - wide)
            total += e + e * mbuf[k, rows, cols].astype(F32)
            csum[:, cols] += jnp.exp2(eighths(s) - cmax[:, cols][None]).sum(0)
        rsum[half, k, rows, :] = total

    def row_level(k):
        top = jnp.maximum(wide_ref[0, k], wide_ref[1, k])
        total = rsum[0, k] * jnp.exp2(wide_ref[0, k] - top)
        total += rsum[1, k] * jnp.exp2(wide_ref[1, k] - top)
        total = jnp.sum(total.T, axis=0, keepdims=True)
        rstat[me_row, pl.ds(q_index(k), 1), :] = top.T[0:1, :] + jnp.log2(total)

    def sweep(half, k, *todo):
        levels(half, k)
        for r in range(4):
            sums(half, k, r)
            for work in todo[r // 2 :: 2] if r % 2 else ():
                scores(*work)

    sweep(1, ME, (FAR, 1, 3))
    sweep(1, RIGHT, (FAR, 1, 2))
    sweep(1, LEFT)
    sweep(1, PAIR)
    sweep(1, FAR)
    lax.fori_loop(PO, FAR, count_step, 0, unroll=True)

    arrive(9, 10)
    sib_copies[PL].start()
    sib_copies[PR].start()
    arrive(11, 12)
    sib_copies[PO].start()
    scores(RIGHT, 2, 1)
    scores(RIGHT, 2, 0)
    sweep(0, ME, (PAIR, 2, 1))
    sweep(0, RIGHT, (PAIR, 2, 0))
    row_level(ME)
    row_level(RIGHT)
    sib_copies[PR].wait_recv()
    sweep(0, LEFT, (PR, 2, 1))
    sweep(0, PAIR, (PR, 2, 0))
    row_level(LEFT)
    row_level(PAIR)
    sib_copies[PL].wait_recv()
    sib_copies[PO].wait_recv()
    sweep(0, FAR, (PR, 1, 3), (PR, 1, 2))
    row_level(FAR)
    sweep(0, PR, (PO, 2, 3))
    sweep(1, PR, (PO, 2, 2))
    row_level(PR)
    sweep(1, PL, (PO, 2, 1))
    sweep(1, PO, (PO, 2, 0))
    sweep(0, PL)
    sweep(0, PO)
    row_level(PL)
    row_level(PO)

    top = jnp.max(cmax[...], axis=0, keepdims=True)
    total = jnp.sum(csum[...] * jnp.exp2(cmax[...] - top), axis=0, keepdims=True)
    total = top + jnp.log2(total)
    for p in range(NP):
        cstat[me_p, pl.ds(p_index(p), 1), :] = total[:, p * 128 : (p + 1) * 128]
    diag = eighths(q_ref[...].astype(F32) * p_ref[...].astype(F32)).sum(0)
    diag = functools.reduce(jnp.add, [diag[:, g * 128 : (g + 1) * 128] for g in range(6)])
    cstat[me_p, 8:16, :] = diag

    def all_row(buf, send, recv):
        def start(j, carry):
            here = buf.at[me_row]
            remote(here, here, send, recv, row_peer((me_row + j) % 16)).start()
            return carry

        return start

    def all_col(buf, send, recv):
        def start(j, carry):
            here = buf.at[me_p]
            remote(here, here, send, recv, col_peer((me_p + j) % 8)).start()
            return carry

        return start

    rs_start = all_row(rstat, rs_send, rs_recv)
    cs_start = all_col(cstat, cs_send, cs_recv)
    lax.fori_loop(1, 16, rs_start, 0)
    lax.fori_loop(1, 8, cs_start, 0)
    group(cstat.at[0:7], cs_send, cs_recv).wait_recv()

    peak = functools.reduce(jnp.maximum, [cstat[k, 0:8, :] for k in range(8)])
    total = functools.reduce(jnp.add, [jnp.exp2(cstat[k, 0:8, :] - peak) for k in range(8)])
    column_lse = peak + jnp.log2(total)
    clse[...] = column_lse
    for p in range(NP):
        level = clse[pl.ds(p_index(p), 1), :]
        lcol[:, p * 128 : (p + 1) * 128] = jnp.broadcast_to(level, (8, 128))
    diag = functools.reduce(jnp.add, [cstat[k, 8:16, :] for k in range(8)])
    loss_c[me_row] = LN2 * column_lse - 2.0 * diag

    group(rstat.at[0:15], rs_send, rs_recv).wait_recv()
    peak = rstat[0]
    for k in range(1, 16):
        peak = jnp.maximum(peak, rstat[k])
    total = jnp.zeros((8, QB), F32)
    for k in range(16):
        total += jnp.exp2(rstat[k] - peak)
    row_lse = peak + jnp.log2(total)
    rlse[...] = row_lse
    for k in range(NQ):
        level = rlse[pl.ds(q_index(k), 1), :]
        lrow[k] = jnp.broadcast_to(level, (128, QB)).T
    loss_r[me_p] = LN2 * (row_lse[:, :128] + row_lse[:, 128:])

    def weights(k, c):
        for r in range(QB // CH):
            rows = slice(r * CH, (r + 1) * CH)
            level = lrow[k, rows, :]
            for g in (2 * c, 2 * c + 1):
                cols = slice(g * 128, (g + 1) * 128)
                s = sbuf[k, rows, cols]
                er = jnp.exp2(s - level)
                ec = jnp.exp2(eighths(s) - lcol[:, cols][None]).reshape(CH, 128)
                pair_weight = (er + ec).astype(BF)
                hard_weight = er.astype(BF)
                wbuf[k, rows, cols] = pair_weight + mbuf[k, rows, cols] * hard_weight

    def query_sums(k, slots):
        def part(n):
            cols = slice(n * 256, (n + 1) * 256)
            left = wbuf[k : k + slots].reshape(slots * QB, COLS)
            found = dot_nn(left, pbuf[...].reshape(COLS, D)[:, cols])
            dq[k : k + slots, :, cols] = found.reshape(slots, QB, 256)

        return part

    def passage_sums(first, slots):
        def part(n):
            cols = slice(n * 256, (n + 1) * 256)
            wide = slots * OWN
            left = wbuf[:, :, first * OWN : first * OWN + wide].reshape(ROWS, wide)
            found = dot_tn(left, qbuf[...].reshape(ROWS, D)[:, cols])
            dp[first : first + slots, :, cols] = found.reshape(slots, OWN, 256)

        return part

    def dsib_copy(k):
        return remote(
            dq.at[k, others, :], sib.at[k], dsib_send, dsib_recv.at[k], sibling
        )

    def query_part(k):
        def rows(first, size):
            start = pl.multiple_of(h * OWN + first, 16)
            return dq[k, pl.ds(start, size), :] + sib[k, first : first + size, :]

        return rows

    def passage_part(p):
        return lambda first, size: dp[p, first : first + size, :]

    class Sums:
        def __init__(self, part, to, exact, bufs, sems):
            self.exact = exact
            to_left, to_right, to_pair = to
            self.part = part
            self.out, self.inn, self.out_scale, self.in_scale = bufs
            self.sems = sems
            self.slots = (
                (PO, 0, OWN, to_pair),
                (PL, 0, OWN, to_left),
                (PR, 0, OWN, to_right),
                (FAR, 0, 64, to_left),
                (FAR, 64, OWN, to_right),
                (PAIR, 0, OWN, to_pair),
                (LEFT, 64, OWN, to_left),
                (RIGHT, 0, 64, to_right),
                (LEFT, 0, 64, to_left),
                (RIGHT, 64, OWN, to_right),
            )

        def copies(self, k):
            send, recv, scale_send, scale_recv = self.sems
            _, low, high, to = self.slots[k]
            src, dst = self.out.at[k], self.inn.at[k]
            if high - low < OWN:
                src, dst = src.at[pl.ds(low, high - low), :], dst.at[pl.ds(low, high - low), :]
            scale, scale_dst = self.out_scale.at[k], self.in_scale.at[k]
            return [
                remote(src, dst, send, recv.at[k], to),
                remote(scale, scale_dst, scale_send, scale_recv.at[k], to),
            ]

        def start(self, *slots):
            for k in slots:
                for copy in self.copies(k):
                    copy.start()

        def arrive(self, *slots):
            for k in slots:
                for copy in self.copies(k):
                    copy.wait_recv()

        def decoded(self, k, first, size):
            value = self.inn[k, first : first + size, :].astype(jnp.int32).astype(F32)
            return value * self.in_scale[k]

        def encode(self, k, added=()):
            block, low, high, _ = self.slots[k]
            part = self.part(block)
            exact = self.exact
            top = jnp.full((8, D), 1e-30, F32)
            for first in range(low, high, 16):
                value = part(first, 16)
                for a in added:
                    value = value + self.decoded(a, first, 16)
                exact[first : first + 16, :] = value
                top = jnp.maximum(top, eighths(jnp.abs(value)).max(0))
            top = jnp.max(top, axis=0, keepdims=True)
            scale = 32766.0 / top
            for first in range(low, high, 16):
                rows = slice(first, first + 16)
                whole = jnp.round(exact[rows, :] * scale).astype(jnp.int32)
                self.out[k, rows, :] = whole.astype(jnp.int16)
            self.out_scale[k] = top * (1.0 / 32766.0)

        def finish(self, grad, positive):
            part = self.part(ME)
            for first in range(0, OWN, 16):
                value = part(first, 16)
                for a in range(5, 10):
                    if self.slots[a][1] <= first < self.slots[a][2]:
                        value = value + self.decoded(a, first, 16)
                rows = slice(first, first + 16)
                grad[rows, :] = 0.5 * (value - 2.0 * positive[rows, :].astype(F32))

    qs = Sums(
        query_part,
        q_to,
        exact.at[0],
        (outq, inq, outq_scale, inq_scale),
        (gq_send, gq_recv, gq_scale_send, gq_scale_recv),
    )
    ps = Sums(
        passage_part,
        p_to,
        exact.at[1],
        (outp, inp, outp_scale, inp_scale),
        (gp_send, gp_recv, gp_scale_send, gp_scale_recv),
    )
    lr_start = all_col(loss_r, lr_send, lr_recv)
    lc_start = all_row(loss_c, lc_send, lc_recv)

    def beside(part, todo=()):
        for n in range(3):
            part(n)
            for work in todo[n::3]:
                weights(*work)

    def every(slots, columns):
        return [(k, c) for k in slots for c in columns]

    rest = (FAR, PAIR, LEFT, RIGHT, ME)
    for work in every((PO, PL, PR), range(4)):
        weights(*work)
    beside(query_sums(PO, 3), every(rest, (0,)))
    dsib_copy(PO).start()
    dsib_copy(PL).start()
    dsib_copy(PR).start()
    beside(passage_sums(PO, 2))
    dsib_copy(PO).wait_recv()
    qs.encode(0)
    ps.encode(0)
    qs.start(0)
    ps.encode(1)
    ps.start(0)
    for work in every(rest, (1,)):
        weights(*work)
    ps.start(1)
    dsib_copy(PL).wait_recv()
    qs.encode(1)
    beside(passage_sums(PR, 2))
    qs.start(1)
    dsib_copy(PR).wait_recv()
    qs.encode(2)
    ps.encode(2)
    qs.start(2)
    for work in every(rest[:2], (2, 3)):
        weights(*work)
    ps.start(2)
    beside(query_sums(FAR, 2))
    for work in every(rest[2:], (2, 3)):
        weights(*work)
    dsib_copy(FAR).start()
    dsib_copy(PAIR).start()
    beside(query_sums(LEFT, 2))
    dsib_copy(LEFT).start()
    dsib_copy(RIGHT).start()
    lax.fori_loop(1, 8, lr_start, 0)
    lax.fori_loop(1, 16, lc_start, 0)
    dsib_copy(FAR).wait_recv()
    qs.arrive(0)
    qs.encode(3, [0])
    qs.encode(4, [0])
    qs.start(3, 4)
    ps.arrive(0)
    ps.encode(3, [0])
    ps.encode(4, [0])
    ps.start(3, 4)
    beside(passage_sums(PAIR, 3))
    dsib_copy(PAIR).wait_recv()
    qs.arrive(1, 2)
    qs.encode(5, [1, 2])
    ps.arrive(1, 2)
    ps.encode(5, [1, 2])
    qs.start(5)
    ps.encode(6)
    ps.encode(7)
    ps.start(5)
    dsib_copy(LEFT).wait_recv()
    qs.encode(6)
    dsib_copy(RIGHT).wait_recv()
    qs.encode(7)
    ps.start(6, 7)
    qs.start(6, 7)
    beside(query_sums(ME, 1))
    dsib_copy(ME).start()
    beside(passage_sums(ME, 1))
    qs.arrive(3)
    qs.encode(8, [3])
    qs.arrive(4)
    qs.encode(9, [4])
    qs.start(8, 9)
    ps.arrive(3)
    ps.encode(8, [3])
    ps.arrive(4)
    ps.encode(9, [4])
    ps.start(8, 9)
    dsib_copy(ME).wait_recv()
    qs.arrive(5, 6, 7, 8, 9)
    qs.finish(gq_ref, p_ref)
    ps.arrive(5, 6, 7, 8, 9)
    ps.finish(gp_ref, q_ref)

    group(loss_r.at[0:7], lr_send, lr_recv).wait_recv()
    group(loss_c.at[0:15], lc_send, lc_recv).wait_recv()
    halves = []
    for s in range(2):
        halves.append(functools.reduce(jnp.add, [loss_r[s * 4 + k] for k in range(4)]))
    both = halves[0] + halves[1]
    halves = []
    for s in range(2):
        terms = [loss_c[xx * 4 + s * 2 + hh] for xx in range(4) for hh in range(2)]
        halves.append(functools.reduce(jnp.add, terms))
    both = both + (halves[0] + halves[1])
    both = jnp.sum(jnp.sum(both, axis=0, keepdims=True), axis=1, keepdims=True)
    loss_ref[...] = both / (2.0 * 16384)

    group(pbuf.at[0:7], q_send, q_recv.at[0]).wait_send()
    group(pbuf.at[0:7], p_send, p_recv.at[0]).wait_send()
    group(pbuf, sib_send, sib_recv.at[0]).wait_send()
    group(tabs.at[0:15], tab_send, tab_recv).wait_send()
    group(rstat.at[0:15], rs_send, rs_recv).wait_send()
    group(cstat.at[0:7], cs_send, cs_recv).wait_send()
    group(loss_r.at[0:7], lr_send, lr_recv).wait_send()
    group(loss_c.at[0:15], lc_send, lc_recv).wait_send()
    group(sib, dsib_send, dsib_recv.at[0]).wait_send()
    group(outq.at[0:7], gq_send, gq_recv.at[0]).wait_send()
    group(outp.at[0:7], gp_send, gp_recv.at[0]).wait_send()
    group(outq_scale, gq_scale_send, gq_scale_recv.at[0]).wait_send()
    group(outp_scale, gp_scale_send, gp_scale_recv.at[0]).wait_send()


def per_device(queries, passages, hard_ids, list_lengths):
    given = (queries, passages, hard_ids.T, list_lengths.reshape(1, OWN))
    given = [pltpu.with_memory_space_constraint(value, pltpu.HBM) for value in given]
    vm = pl.BlockSpec(memory_space=pltpu.VMEM)
    dma = pltpu.SemaphoreType.DMA
    loss, grad_queries, grad_passages = pl.pallas_call(
        kernel,
        out_shape=(
            jax.ShapeDtypeStruct((1, 1), F32),
            jax.ShapeDtypeStruct((OWN, D), F32),
            jax.ShapeDtypeStruct((OWN, D), F32),
        ),
        in_specs=[pl.BlockSpec(memory_space=pltpu.HBM)] * 4,
        out_specs=(vm, vm, vm),
        scratch_shapes=[
            pltpu.VMEM((OWN, D), F32),
            pltpu.VMEM((OWN, D), F32),
            pltpu.VMEM((32, OWN), jnp.int32),
            pltpu.VMEM((1, OWN), jnp.int32),
            pltpu.VMEM((OWN, D), BF),
            pltpu.VMEM((OWN, D), BF),
            pltpu.VMEM((32, OWN), jnp.int32),
            pltpu.VMEM((32, OWN), F32),
            pltpu.VMEM((NQ, QB, D), BF),
            pltpu.VMEM((NP, OWN, D), BF),
            pltpu.VMEM((NQ, QB, COLS), F32),
            pltpu.VMEM((NQ, QB, COLS), BF),
            pltpu.VMEM((NQ, QB, COLS), BF),
            pltpu.VMEM((128, 128), F32),
            pltpu.VMEM((16, 8, 128), F32),
            pltpu.VMEM((NQ, 16, 128), F32),
            pltpu.VMEM((8, COLS), F32),
            pltpu.VMEM((8, COLS), F32),
            pltpu.VMEM((8, COLS), F32),
            pltpu.VMEM((2, NQ, QB, 128), F32),
            pltpu.VMEM((2, NQ, QB, 128), F32),
            pltpu.VMEM((2, NQ, QB, 128), F32),
            pltpu.VMEM((16, 8, QB), F32),
            pltpu.VMEM((8, 16, 128), F32),
            pltpu.VMEM((8, QB), F32),
            pltpu.VMEM((8, 128), F32),
            pltpu.VMEM((NQ, QB, 128), F32),
            pltpu.VMEM((8, COLS), F32),
            pltpu.VMEM((8, 8, 128), F32),
            pltpu.VMEM((16, 8, 128), F32),
            pltpu.VMEM((NQ, QB, D), F32),
            pltpu.VMEM((NQ, OWN, D), F32),
            pltpu.VMEM((NP, OWN, D), F32),
            pltpu.VMEM((2, OWN, D), F32),
            pltpu.VMEM((10, OWN, D), jnp.int16),
            pltpu.VMEM((10, OWN, D), jnp.int16),
            pltpu.VMEM((10, 1, D), F32),
            pltpu.VMEM((10, 1, D), F32),
            pltpu.VMEM((10, OWN, D), jnp.int16),
            pltpu.VMEM((10, OWN, D), jnp.int16),
            pltpu.VMEM((10, 1, D), F32),
            pltpu.VMEM((10, 1, D), F32),
            dma((4,)),
            dma,
            dma((13,)),
            dma,
            dma((13,)),
            dma,
            dma((8,)),
            dma,
            dma,
            dma,
            dma,
            dma,
            dma,
            dma,
            dma,
            dma,
            dma,
            dma,
            dma((8,)),
            dma,
            dma((10,)),
            dma,
            dma((10,)),
            dma,
            dma((10,)),
            dma,
            dma((10,)),
        ],
        compiler_params=pltpu.CompilerParams(
            collective_id=0, has_side_effects=True, vmem_limit_bytes=51 * 1024 * 1024
        ),
        name="infonce",
    )(*given)
    return loss[0, 0], grad_queries, grad_passages


def solution(mesh):
    placed = (P(("pb", "pa"), None), P(("pb", "pa"), None), P(("pb", "pa"), None), P(("pb", "pa")))
    return jax.shard_map(
        per_device,
        mesh=mesh,
        in_specs=placed,
        out_specs=(P(), P(("pb", "pa"), None), P(("pb", "pa"), None)),
        check_vma=False,
    )
```

```python
import functools

import jax
import jax.numpy as jnp
from jax import lax
from jax.experimental import pallas as pl
from jax.experimental.pallas import tpu as pltpu
from jax.sharding import PartitionSpec as P

BF = jnp.bfloat16
F32 = jnp.float32
MESH = pl.DeviceIdType.MESH
D = 768
OWN = 128
NQ = 8
NP = 8
QB = 256
COLS = 1024
ROWS = 2048
CH = 64
PO, PL, PR, FAR, PAIR, LEFT, RIGHT, ME = range(8)
RING = (2, 3, 1, 2, 0, 3, 1, 0)
FLIP = (1, 1, 1, 0, 1, 0, 0, 0)
NEG = float("-inf")
LOG2E = 1.4426950408889634
LN2 = 0.6931471805599453


def dot_nt(a, b):
    return lax.dot_general(a, b, (((1,), (1,)), ((), ())), preferred_element_type=F32)


def dot_nn(a, b):
    return lax.dot_general(a, b, (((1,), (0,)), ((), ())), preferred_element_type=F32)


def dot_tn(a, b):
    return lax.dot_general(a, b, (((0,), (0,)), ((), ())), preferred_element_type=F32)


def eighths(value):
    return value.reshape(value.shape[0] // 8, 8, value.shape[1])


def kernel(
    queries_hbm,
    passages_hbm,
    ids_hbm,
    lengths_hbm,
    loss_ref,
    gq_ref,
    gp_ref,
    queries_ref,
    passages_ref,
    ids_ref,
    lengths_ref,
    q_ref,
    p_ref,
    dest_ref,
    code_ref,
    qbuf,
    pbuf,
    sbuf,
    mbuf,
    wbuf,
    table,
    tabs,
    codes,
    cmax,
    cnext,
    csum,
    rnext,
    wide_ref,
    rsum,
    rstat,
    cstat,
    rlse,
    clse,
    lrow,
    lcol,
    loss_r,
    loss_c,
    dq,
    sib,
    dp,
    exact,
    outq,
    inq,
    outq_scale,
    inq_scale,
    outp,
    inp,
    outp_scale,
    inp_scale,
    in_sem,
    q_send,
    q_recv,
    p_send,
    p_recv,
    sib_send,
    sib_recv,
    tab_send,
    tab_recv,
    rs_send,
    rs_recv,
    cs_send,
    cs_recv,
    lr_send,
    lr_recv,
    lc_send,
    lc_recv,
    dsib_send,
    dsib_recv,
    gq_send,
    gq_recv,
    gq_scale_send,
    gq_scale_recv,
    gp_send,
    gp_recv,
    gp_scale_send,
    gp_scale_recv,
):
    pb = lax.axis_index("pb")
    pa = lax.axis_index("pa")
    z, h = pb // 2, pb % 2
    x, y = pa // 4, pa % 4
    pair = z // 2
    zs = z % 2
    zc = (z + 3) % 4
    half, sel = zc // 2, zc % 2
    me_q = x * 2 + zs
    me_p = sel * 4 + y
    me_row = me_q * 2 + h

    def device(xx, yy, zz, hh):
        return (zz * 2 + hh, xx * 4 + yy)

    def row_peer(idx):
        q, hh = idx // 2, idx % 2
        return device(q // 2, y, pair * 2 + q % 2, hh)

    def col_peer(p):
        return device(x, p % 4, (half * 2 + p // 4 + 1) % 4, h)

    def q_index(k):
        return (x + RING[k]) % 4 * 2 + (1 - zs if FLIP[k] else zs)

    def p_index(k):
        return (1 - sel if FLIP[k] else sel) * 4 + (y + RING[k]) % 4

    sibling = device(x, y, z, 1 - h)
    mine = pl.ds(pl.multiple_of(h * OWN, OWN), OWN)
    others = pl.ds(pl.multiple_of((1 - h) * OWN, OWN), OWN)
    loads = [
        pltpu.make_async_copy(src, dst, in_sem.at[k])
        for k, (src, dst) in enumerate(
            [
                (queries_hbm, queries_ref),
                (passages_hbm, passages_ref),
                (ids_hbm, ids_ref),
                (lengths_hbm, lengths_ref),
            ]
        )
    ]
    for load in loads:
        load.start()

    def remote(src, dst, send, recv, to):
        return pltpu.make_async_remote_copy(
            src_ref=src,
            dst_ref=dst,
            send_sem=send,
            recv_sem=recv,
            device_id=to,
            device_id_type=MESH,
        )

    barrier = pltpu.get_barrier_semaphore()

    def greet_row(j, carry):
        pl.semaphore_signal(
            barrier, inc=1, device_id=row_peer((me_row + j) % 16), device_id_type=MESH
        )
        return carry

    def greet_col(j, carry):
        pl.semaphore_signal(
            barrier, inc=1, device_id=col_peer((me_p + j) % 8), device_id_type=MESH
        )
        return carry

    lax.fori_loop(1, 16, greet_row, 0)
    lax.fori_loop(1, 8, greet_col, 0)

    for load in loads:
        load.wait()
    q_ref[...] = queries_ref[...].astype(BF)
    p_ref[...] = passages_ref[...].astype(BF)
    ids = ids_ref[...]
    owner = ids // OWN
    third_z = (owner // 32 + 3) % 4
    dest = (owner // 4) % 4 * 32 + (third_z // 2) * 16 + (owner // 16) % 2 * 8
    dest = dest + (third_z % 2) * 4 + owner % 4
    place = lax.broadcasted_iota(jnp.int32, ids.shape, 0)
    dest_ref[...] = jnp.where(place < lengths_ref[...], dest, -1)
    code_ref[...] = (ids % OWN + 1).astype(F32)
    qbuf[ME, mine, :] = q_ref[...]
    pbuf[ME] = p_ref[...]
    pl.semaphore_wait(barrier, 22)

    def q_at(k, first=0, size=OWN):
        return qbuf.at[k, pl.ds(pl.multiple_of(h * OWN + first, 64), size), :]

    def p_at(k, first=0, size=OWN):
        return pbuf.at[k, pl.ds(first, size), :]

    def ring(at, own, to_left, to_right, to_pair, send, recv):
        low, high = own.at[pl.ds(0, 64), :], own.at[pl.ds(64, 64), :]
        plan = [
            (low, at(LEFT, 0, 64), to_right),
            (high, at(RIGHT, 64, 64), to_left),
            (own, at(PAIR), to_pair),
            (high, at(LEFT, 64, 64), to_right),
            (low, at(RIGHT, 0, 64), to_left),
            (at(LEFT, 0, 64), at(FAR, 0, 64), to_right),
            (at(RIGHT, 64, 64), at(FAR, 64, 64), to_left),
            (at(LEFT, 0, 64), at(PL, 0, 64), to_pair),
            (at(RIGHT, 64, 64), at(PR, 64, 64), to_pair),
            (at(PAIR, 64, 64), at(PL, 64, 64), to_right),
            (at(PAIR, 0, 64), at(PR, 0, 64), to_left),
            (at(PL, 0, 64), at(PO, 0, 64), to_right),
            (at(PR, 64, 64), at(PO, 64, 64), to_left),
        ]
        return [
            remote(src, dst, send, recv.at[k], to) for k, (src, dst, to) in enumerate(plan)
        ]

    q_to = (
        device((x + 3) % 4, y, z, h),
        device((x + 1) % 4, y, z, h),
        device(x, y, pair * 2 + 1 - zs, h),
    )
    p_to = (
        device(x, (y + 3) % 4, z, h),
        device(x, (y + 1) % 4, z, h),
        device(x, y, (half * 2 + (1 - sel) + 1) % 4, h),
    )
    q_copies = ring(q_at, q_ref, *q_to, q_send, q_recv)
    p_copies = ring(p_at, p_ref, *p_to, p_send, p_recv)
    for k in range(5):
        q_copies[k].start()
        p_copies[k].start()

    sib_copies = [
        remote(q_ref if k == ME else q_at(k), q_at(k), sib_send, sib_recv.at[k], sibling)
        for k in range(8)
    ]
    sib_copies[ME].start()

    sub = lax.broadcasted_iota(jnp.int32, (128, 128), 0)
    lane = lax.broadcasted_iota(jnp.int32, (128, 128), 1)
    earlier = jnp.where(sub < lane, 1.0, 0.0).astype(BF)
    prefix = jnp.concatenate([earlier, jnp.ones((128, 128), BF)], axis=1)
    row_code = (lane + 1 + 128 * h).astype(F32)
    second_core = h.astype(F32)
    slot_of = (sub % 64).astype(F32)
    rows_here = jnp.where(sub < 64, 1.0 - second_core, second_core)
    table[...] = jnp.zeros_like(table)

    def slot_step(k, count):
        dest = dest_ref[pl.ds(k, 1), :]
        code = code_ref[pl.ds(k, 1), :]
        live = jnp.where(sub == dest, 1.0, 0.0)
        both = dot_nn(live.astype(BF), prefix)
        rank = jnp.sum(live * (both[:, :128] + count), axis=0, keepdims=True)
        value = rows_here * row_code + (1.0 - rows_here) * code
        chosen = jnp.where(slot_of == rank, value, 0.0).astype(BF)
        table[...] += dot_nt(live.astype(BF), chosen)
        return count + both[:, 128:]

    lax.fori_loop(0, 32, slot_step, jnp.zeros((128, 128), F32), unroll=4)

    def tab_copy(idx, to):
        q, hh = to // 2, to % 2
        zz = (pair * 2 + q % 2 + 3) % 4
        group = (q // 2) * 4 + (zz // 2) * 2 + hh
        return remote(
            table.at[pl.ds(pl.multiple_of(group * 8, 8), 8), :],
            tabs.at[idx],
            tab_send,
            tab_recv,
            row_peer(to),
        )

    def tab_start(j, carry):
        tab_copy(me_row, (me_row + j) % 16).start()
        return carry

    lax.fori_loop(1, 16, tab_start, 0)
    tabs[me_row] = table[pl.ds(pl.multiple_of((x * 4 + half * 2 + h) * 8, 8), 8), :]

    def arrive(*ks):
        for k in ks:
            q_copies[k].wait_recv()
            p_copies[k].wait_recv()

    def forward(*ks):
        for k in ks:
            q_copies[k].start()
            p_copies[k].start()

    arrive(0)
    forward(5, 7)
    arrive(1)
    forward(6, 8)
    arrive(3, 4)
    sib_copies[LEFT].start()
    sib_copies[RIGHT].start()
    arrive(2)
    forward(9, 10)
    sib_copies[PAIR].start()

    cmax[...] = jnp.full(cmax.shape, NEG, F32)
    cnext[...] = jnp.full(cnext.shape, NEG, F32)
    csum[...] = jnp.zeros_like(csum)
    rnext[...] = jnp.full(rnext.shape, NEG, F32)

    def scores(k, slots, c):
        cols = slice(c * 256, (c + 1) * 256)
        left = qbuf[k : k + slots].reshape(slots * QB, D)
        part = dot_nt(left, pbuf[2 * c : 2 * c + 2].reshape(256, D)) * LOG2E
        cnext[:, cols] = jnp.maximum(cnext[:, cols], eighths(part).max(0))
        for n in range(slots):
            own = part[n * QB : (n + 1) * QB]
            sbuf[k + n, :, cols] = own
            top = jnp.maximum(own[:, :128], own[:, 128:])
            rnext[c // 2, k + n] = jnp.maximum(rnext[c // 2, k + n], top)

    sib_copies[ME].wait_recv()
    sib_copies[RIGHT].wait_recv()
    scores(RIGHT, 2, 3)
    scores(RIGHT, 2, 2)

    arrive(7)
    forward(11)
    arrive(8)
    forward(12)
    arrive(5, 6)
    sib_copies[FAR].start()
    sib_copies[LEFT].wait_recv()
    sib_copies[PAIR].wait_recv()
    scores(PAIR, 2, 3)
    scores(PAIR, 2, 2)

    def group(ref, send, recv):
        return remote(ref, ref, send, recv, sibling)

    group(tabs.at[0:15], tab_send, tab_recv).wait_recv()

    tall = (lax.broadcasted_iota(jnp.int32, (QB, 128), 0) + 1).astype(F32)
    near = lane[:8] < 64
    for k in range(8):
        first, last = tabs[2 * q_index(k)], tabs[2 * q_index(k) + 1]
        codes[k, 0:8, :] = jnp.where(near, first, last)
        codes[k, 8:16, :] = pltpu.roll(jnp.where(near, last, first), 64, 1)

    def count_step(k, carry):
        for p in range(NP):
            rows = codes[k, pl.ds(p_index(p), 1), :]
            cols = codes[k, pl.ds(p_index(p) + 8, 1), :]
            rows = jnp.where(tall == rows, 1.0, 0.0).astype(BF)
            cols = jnp.where(tall[:128] == cols, 1.0, 0.0).astype(BF)
            mbuf[k, :, p * 128 : (p + 1) * 128] = dot_nt(rows, cols).astype(BF)
        return carry

    lax.fori_loop(FAR, NQ, count_step, 0, unroll=True)
    sib_copies[FAR].wait_recv()

    def levels(half, k):
        cols = slice(half * 512, half * 512 + 512)
        csum[:, cols] = csum[:, cols] * jnp.exp2(cmax[:, cols] - cnext[:, cols])
        cmax[:, cols] = cnext[:, cols]
        top = jnp.max(rnext[half, k], axis=1, keepdims=True)
        wide_ref[half, k] = jnp.broadcast_to(top, (QB, 128))

    def sums(half, k, r):
        rows = slice(r * CH, (r + 1) * CH)
        wide = wide_ref[half, k, rows, :]
        total = jnp.zeros((CH, 128), F32)
        for g in range(half * 4, half * 4 + 4):
            cols = slice(g * 128, (g + 1) * 128)
            s = sbuf[k, rows, cols]
            e = jnp.exp2(s - wide)
            total += e + e * mbuf[k, rows, cols].astype(F32)
            csum[:, cols] += jnp.exp2(eighths(s) - cmax[:, cols][None]).sum(0)
        rsum[half, k, rows, :] = total

    def row_level(k):
        top = jnp.maximum(wide_ref[0, k], wide_ref[1, k])
        total = rsum[0, k] * jnp.exp2(wide_ref[0, k] - top)
        total += rsum[1, k] * jnp.exp2(wide_ref[1, k] - top)
        total = jnp.sum(total.T, axis=0, keepdims=True)
        rstat[me_row, pl.ds(q_index(k), 1), :] = top.T[0:1, :] + jnp.log2(total)

    def sweep(half, k, *todo):
        levels(half, k)
        for r in range(4):
            sums(half, k, r)
            for work in todo[r // 2 :: 2] if r % 2 else ():
                scores(*work)

    sweep(1, ME, (FAR, 1, 3))
    sweep(1, RIGHT, (FAR, 1, 2))
    sweep(1, LEFT)
    sweep(1, PAIR)
    sweep(1, FAR)
    lax.fori_loop(PO, FAR, count_step, 0, unroll=True)

    arrive(9, 10)
    sib_copies[PL].start()
    sib_copies[PR].start()
    arrive(11, 12)
    sib_copies[PO].start()
    scores(RIGHT, 2, 1)
    scores(RIGHT, 2, 0)
    sweep(0, ME, (PAIR, 2, 1))
    sweep(0, RIGHT, (PAIR, 2, 0))
    row_level(ME)
    row_level(RIGHT)
    sib_copies[PR].wait_recv()
    sweep(0, LEFT, (PR, 2, 1))
    sweep(0, PAIR, (PR, 2, 0))
    row_level(LEFT)
    row_level(PAIR)
    sib_copies[PL].wait_recv()
    sib_copies[PO].wait_recv()
    sweep(0, FAR, (PR, 1, 3), (PR, 1, 2))
    row_level(FAR)
    sweep(0, PR, (PO, 2, 3))
    sweep(1, PR, (PO, 2, 2))
    row_level(PR)
    sweep(1, PL, (PO, 2, 1))
    sweep(1, PO, (PO, 2, 0))
    sweep(0, PL)
    sweep(0, PO)
    row_level(PL)
    row_level(PO)

    top = jnp.max(cmax[...], axis=0, keepdims=True)
    total = jnp.sum(csum[...] * jnp.exp2(cmax[...] - top), axis=0, keepdims=True)
    total = top + jnp.log2(total)
    for p in range(NP):
        cstat[me_p, pl.ds(p_index(p), 1), :] = total[:, p * 128 : (p + 1) * 128]
    diag = eighths(q_ref[...].astype(F32) * p_ref[...].astype(F32)).sum(0)
    diag = functools.reduce(jnp.add, [diag[:, g * 128 : (g + 1) * 128] for g in range(6)])
    cstat[me_p, 8:16, :] = diag

    def all_row(buf, send, recv):
        def start(j, carry):
            here = buf.at[me_row]
            remote(here, here, send, recv, row_peer((me_row + j) % 16)).start()
            return carry

        return start

    def all_col(buf, send, recv):
        def start(j, carry):
            here = buf.at[me_p]
            remote(here, here, send, recv, col_peer((me_p + j) % 8)).start()
            return carry

        return start

    rs_start = all_row(rstat, rs_send, rs_recv)
    cs_start = all_col(cstat, cs_send, cs_recv)
    lax.fori_loop(1, 16, rs_start, 0)
    lax.fori_loop(1, 8, cs_start, 0)
    group(cstat.at[0:7], cs_send, cs_recv).wait_recv()

    peak = functools.reduce(jnp.maximum, [cstat[k, 0:8, :] for k in range(8)])
    total = functools.reduce(jnp.add, [jnp.exp2(cstat[k, 0:8, :] - peak) for k in range(8)])
    column_lse = peak + jnp.log2(total)
    clse[...] = column_lse
    for p in range(NP):
        level = clse[pl.ds(p_index(p), 1), :]
        lcol[:, p * 128 : (p + 1) * 128] = jnp.broadcast_to(level, (8, 128))
    diag = functools.reduce(jnp.add, [cstat[k, 8:16, :] for k in range(8)])
    loss_c[me_row] = LN2 * column_lse - 2.0 * diag

    group(rstat.at[0:15], rs_send, rs_recv).wait_recv()
    peak = rstat[0]
    for k in range(1, 16):
        peak = jnp.maximum(peak, rstat[k])
    total = jnp.zeros((8, QB), F32)
    for k in range(16):
        total += jnp.exp2(rstat[k] - peak)
    row_lse = peak + jnp.log2(total)
    rlse[...] = row_lse
    for k in range(NQ):
        level = rlse[pl.ds(q_index(k), 1), :]
        lrow[k] = jnp.broadcast_to(level, (128, QB)).T
    loss_r[me_p] = LN2 * (row_lse[:, :128] + row_lse[:, 128:])

    def weights(k, c):
        for r in range(QB // CH):
            rows = slice(r * CH, (r + 1) * CH)
            level = lrow[k, rows, :]
            for g in (2 * c, 2 * c + 1):
                cols = slice(g * 128, (g + 1) * 128)
                s = sbuf[k, rows, cols]
                er = jnp.exp2(s - level)
                ec = jnp.exp2(eighths(s) - lcol[:, cols][None]).reshape(CH, 128)
                pair_weight = (er + ec).astype(BF)
                hard_weight = er.astype(BF)
                wbuf[k, rows, cols] = pair_weight + mbuf[k, rows, cols] * hard_weight

    def query_sums(k, slots):
        def part(n):
            cols = slice(n * 256, (n + 1) * 256)
            left = wbuf[k : k + slots].reshape(slots * QB, COLS)
            found = dot_nn(left, pbuf[...].reshape(COLS, D)[:, cols])
            dq[k : k + slots, :, cols] = found.reshape(slots, QB, 256)

        return part

    def passage_sums(first, slots):
        def part(n):
            cols = slice(n * 256, (n + 1) * 256)
            wide = slots * OWN
            left = wbuf[:, :, first * OWN : first * OWN + wide].reshape(ROWS, wide)
            found = dot_tn(left, qbuf[...].reshape(ROWS, D)[:, cols])
            dp[first : first + slots, :, cols] = found.reshape(slots, OWN, 256)

        return part

    def dsib_copy(k):
        return remote(
            dq.at[k, others, :], sib.at[k], dsib_send, dsib_recv.at[k], sibling
        )

    def query_part(k):
        def rows(first, size):
            start = pl.multiple_of(h * OWN + first, 16)
            return dq[k, pl.ds(start, size), :] + sib[k, first : first + size, :]

        return rows

    def passage_part(p):
        return lambda first, size: dp[p, first : first + size, :]

    class Sums:
        def __init__(self, part, to, exact, bufs, sems):
            self.exact = exact
            to_left, to_right, to_pair = to
            self.part = part
            self.out, self.inn, self.out_scale, self.in_scale = bufs
            self.sems = sems
            self.slots = (
                (PO, 0, OWN, to_pair),
                (PL, 0, OWN, to_left),
                (PR, 0, OWN, to_right),
                (FAR, 0, 64, to_left),
                (FAR, 64, OWN, to_right),
                (PAIR, 0, OWN, to_pair),
                (LEFT, 64, OWN, to_left),
                (RIGHT, 0, 64, to_right),
                (LEFT, 0, 64, to_left),
                (RIGHT, 64, OWN, to_right),
            )

        def copies(self, k):
            send, recv, scale_send, scale_recv = self.sems
            _, low, high, to = self.slots[k]
            src, dst = self.out.at[k], self.inn.at[k]
            if high - low < OWN:
                src, dst = src.at[pl.ds(low, high - low), :], dst.at[pl.ds(low, high - low), :]
            scale, scale_dst = self.out_scale.at[k], self.in_scale.at[k]
            return [
                remote(src, dst, send, recv.at[k], to),
                remote(scale, scale_dst, scale_send, scale_recv.at[k], to),
            ]

        def start(self, *slots):
            for k in slots:
                for copy in self.copies(k):
                    copy.start()

        def arrive(self, *slots):
            for k in slots:
                for copy in self.copies(k):
                    copy.wait_recv()

        def decoded(self, k, first, size):
            value = self.inn[k, first : first + size, :].astype(jnp.int32).astype(F32)
            return value * self.in_scale[k]

        def encode(self, k, added=()):
            block, low, high, _ = self.slots[k]
            part = self.part(block)
            exact = self.exact
            top = jnp.full((8, D), 1e-30, F32)
            for first in range(low, high, 16):
                value = part(first, 16)
                for a in added:
                    value = value + self.decoded(a, first, 16)
                exact[first : first + 16, :] = value
                top = jnp.maximum(top, eighths(jnp.abs(value)).max(0))
            top = jnp.max(top, axis=0, keepdims=True)
            scale = 32766.0 / top
            for first in range(low, high, 16):
                rows = slice(first, first + 16)
                whole = jnp.round(exact[rows, :] * scale).astype(jnp.int32)
                self.out[k, rows, :] = whole.astype(jnp.int16)
            self.out_scale[k] = top * (1.0 / 32766.0)

        def finish(self, grad, positive):
            part = self.part(ME)
            for first in range(0, OWN, 16):
                value = part(first, 16)
                for a in range(5, 10):
                    if self.slots[a][1] <= first < self.slots[a][2]:
                        value = value + self.decoded(a, first, 16)
                rows = slice(first, first + 16)
                grad[rows, :] = 0.5 * (value - 2.0 * positive[rows, :].astype(F32))

    qs = Sums(
        query_part,
        q_to,
        exact.at[0],
        (outq, inq, outq_scale, inq_scale),
        (gq_send, gq_recv, gq_scale_send, gq_scale_recv),
    )
    ps = Sums(
        passage_part,
        p_to,
        exact.at[1],
        (outp, inp, outp_scale, inp_scale),
        (gp_send, gp_recv, gp_scale_send, gp_scale_recv),
    )
    lr_start = all_col(loss_r, lr_send, lr_recv)
    lc_start = all_row(loss_c, lc_send, lc_recv)

    def beside(part, todo=()):
        for n in range(3):
            part(n)
            for work in todo[n::3]:
                weights(*work)

    def every(slots, columns):
        return [(k, c) for k in slots for c in columns]

    rest = (FAR, PAIR, LEFT, RIGHT, ME)
    for work in every((PO, PL, PR), range(4)):
        weights(*work)
    beside(query_sums(PO, 3), every(rest, (0,)))
    dsib_copy(PO).start()
    dsib_copy(PL).start()
    dsib_copy(PR).start()
    beside(passage_sums(PO, 2))
    dsib_copy(PO).wait_recv()
    qs.encode(0)
    ps.encode(0)
    qs.start(0)
    ps.encode(1)
    ps.start(0)
    for work in every(rest, (1,)):
        weights(*work)
    ps.start(1)
    dsib_copy(PL).wait_recv()
    qs.encode(1)
    beside(passage_sums(PR, 2))
    qs.start(1)
    dsib_copy(PR).wait_recv()
    qs.encode(2)
    ps.encode(2)
    qs.start(2)
    for work in every(rest[:2], (2, 3)):
        weights(*work)
    ps.start(2)
    beside(query_sums(FAR, 2))
    for work in every(rest[2:], (2, 3)):
        weights(*work)
    dsib_copy(FAR).start()
    dsib_copy(PAIR).start()
    beside(query_sums(LEFT, 2))
    dsib_copy(LEFT).start()
    dsib_copy(RIGHT).start()
    dsib_copy(FAR).wait_recv()
    qs.arrive(0)
    qs.encode(3, [0])
    qs.encode(4, [0])
    qs.start(3, 4)
    ps.arrive(0)
    ps.encode(3, [0])
    ps.encode(4, [0])
    ps.start(3, 4)
    beside(passage_sums(PAIR, 3))
    dsib_copy(PAIR).wait_recv()
    qs.arrive(1, 2)
    qs.encode(5, [1, 2])
    ps.arrive(1, 2)
    ps.encode(5, [1, 2])
    qs.start(5)
    ps.encode(6)
    ps.encode(7)
    ps.start(5)
    dsib_copy(LEFT).wait_recv()
    qs.encode(6)
    dsib_copy(RIGHT).wait_recv()
    qs.encode(7)
    ps.start(6, 7)
    qs.start(6, 7)
    lax.fori_loop(1, 8, lr_start, 0)
    lax.fori_loop(1, 16, lc_start, 0)
    beside(query_sums(ME, 1))
    dsib_copy(ME).start()
    beside(passage_sums(ME, 1))
    qs.arrive(3)
    qs.encode(8, [3])
    qs.arrive(4)
    qs.encode(9, [4])
    qs.start(8, 9)
    ps.arrive(3)
    ps.encode(8, [3])
    ps.arrive(4)
    ps.encode(9, [4])
    ps.start(8, 9)
    dsib_copy(ME).wait_recv()
    qs.arrive(5, 6, 7, 8, 9)
    qs.finish(gq_ref, p_ref)
    ps.arrive(5, 6, 7, 8, 9)
    ps.finish(gp_ref, q_ref)

    group(loss_r.at[0:7], lr_send, lr_recv).wait_recv()
    group(loss_c.at[0:15], lc_send, lc_recv).wait_recv()
    halves = []
    for s in range(2):
        halves.append(functools.reduce(jnp.add, [loss_r[s * 4 + k] for k in range(4)]))
    both = halves[0] + halves[1]
    halves = []
    for s in range(2):
        terms = [loss_c[xx * 4 + s * 2 + hh] for xx in range(4) for hh in range(2)]
        halves.append(functools.reduce(jnp.add, terms))
    both = both + (halves[0] + halves[1])
    both = jnp.sum(jnp.sum(both, axis=0, keepdims=True), axis=1, keepdims=True)
    loss_ref[...] = both / (2.0 * 16384)

    group(pbuf.at[0:7], q_send, q_recv.at[0]).wait_send()
    group(pbuf.at[0:7], p_send, p_recv.at[0]).wait_send()
    group(pbuf, sib_send, sib_recv.at[0]).wait_send()
    group(tabs.at[0:15], tab_send, tab_recv).wait_send()
    group(rstat.at[0:15], rs_send, rs_recv).wait_send()
    group(cstat.at[0:7], cs_send, cs_recv).wait_send()
    group(loss_r.at[0:7], lr_send, lr_recv).wait_send()
    group(loss_c.at[0:15], lc_send, lc_recv).wait_send()
    group(sib, dsib_send, dsib_recv.at[0]).wait_send()
    group(outq.at[0:7], gq_send, gq_recv.at[0]).wait_send()
    group(outp.at[0:7], gp_send, gp_recv.at[0]).wait_send()
    group(outq_scale, gq_scale_send, gq_scale_recv.at[0]).wait_send()
    group(outp_scale, gp_scale_send, gp_scale_recv.at[0]).wait_send()


def per_device(queries, passages, hard_ids, list_lengths):
    given = (queries, passages, hard_ids.T, list_lengths.reshape(1, OWN))
    given = [pltpu.with_memory_space_constraint(value, pltpu.HBM) for value in given]
    vm = pl.BlockSpec(memory_space=pltpu.VMEM)
    dma = pltpu.SemaphoreType.DMA
    loss, grad_queries, grad_passages = pl.pallas_call(
        kernel,
        out_shape=(
            jax.ShapeDtypeStruct((1, 1), F32),
            jax.ShapeDtypeStruct((OWN, D), F32),
            jax.ShapeDtypeStruct((OWN, D), F32),
        ),
        in_specs=[pl.BlockSpec(memory_space=pltpu.HBM)] * 4,
        out_specs=(vm, vm, vm),
        scratch_shapes=[
            pltpu.VMEM((OWN, D), F32),
            pltpu.VMEM((OWN, D), F32),
            pltpu.VMEM((32, OWN), jnp.int32),
            pltpu.VMEM((1, OWN), jnp.int32),
            pltpu.VMEM((OWN, D), BF),
            pltpu.VMEM((OWN, D), BF),
            pltpu.VMEM((32, OWN), jnp.int32),
            pltpu.VMEM((32, OWN), F32),
            pltpu.VMEM((NQ, QB, D), BF),
            pltpu.VMEM((NP, OWN, D), BF),
            pltpu.VMEM((NQ, QB, COLS), F32),
            pltpu.VMEM((NQ, QB, COLS), BF),
            pltpu.VMEM((NQ, QB, COLS), BF),
            pltpu.VMEM((128, 128), F32),
            pltpu.VMEM((16, 8, 128), F32),
            pltpu.VMEM((NQ, 16, 128), F32),
            pltpu.VMEM((8, COLS), F32),
            pltpu.VMEM((8, COLS), F32),
            pltpu.VMEM((8, COLS), F32),
            pltpu.VMEM((2, NQ, QB, 128), F32),
            pltpu.VMEM((2, NQ, QB, 128), F32),
            pltpu.VMEM((2, NQ, QB, 128), F32),
            pltpu.VMEM((16, 8, QB), F32),
            pltpu.VMEM((8, 16, 128), F32),
            pltpu.VMEM((8, QB), F32),
            pltpu.VMEM((8, 128), F32),
            pltpu.VMEM((NQ, QB, 128), F32),
            pltpu.VMEM((8, COLS), F32),
            pltpu.VMEM((8, 8, 128), F32),
            pltpu.VMEM((16, 8, 128), F32),
            pltpu.VMEM((NQ, QB, D), F32),
            pltpu.VMEM((NQ, OWN, D), F32),
            pltpu.VMEM((NP, OWN, D), F32),
            pltpu.VMEM((2, OWN, D), F32),
            pltpu.VMEM((10, OWN, D), jnp.int16),
            pltpu.VMEM((10, OWN, D), jnp.int16),
            pltpu.VMEM((10, 1, D), F32),
            pltpu.VMEM((10, 1, D), F32),
            pltpu.VMEM((10, OWN, D), jnp.int16),
            pltpu.VMEM((10, OWN, D), jnp.int16),
            pltpu.VMEM((10, 1, D), F32),
            pltpu.VMEM((10, 1, D), F32),
            dma((4,)),
            dma,
            dma((13,)),
            dma,
            dma((13,)),
            dma,
            dma((8,)),
            dma,
            dma,
            dma,
            dma,
            dma,
            dma,
            dma,
            dma,
            dma,
            dma,
            dma,
            dma((8,)),
            dma,
            dma((10,)),
            dma,
            dma((10,)),
            dma,
            dma((10,)),
            dma,
            dma((10,)),
        ],
        compiler_params=pltpu.CompilerParams(
            collective_id=0, has_side_effects=True, vmem_limit_bytes=51 * 1024 * 1024
        ),
        name="infonce",
    )(*given)
    return loss[0, 0], grad_queries, grad_passages


def solution(mesh):
    placed = (P(("pb", "pa"), None), P(("pb", "pa"), None), P(("pb", "pa"), None), P(("pb", "pa")))
    return jax.shard_map(
        per_device,
        mesh=mesh,
        in_specs=placed,
        out_specs=(P(), P(("pb", "pa"), None), P(("pb", "pa"), None)),
        check_vma=False,
    )
```
